32 devices in a mesh: seq: 4 (over x, core), chan: 8 (over z, y).
Axes of the slice: x: 2, y: 2, z: 4, core: 2. Of those that a mesh axis runs over, the one named last changes fastest.
Arguments:
- tokens: bfloat16 [8, 1024, 2048], P(None, ('seq', 'chan')), may hold values from -6 to 6
- norm_gain: bfloat16 [2048], P(('chan', 'seq')), may hold values from 0.5 to 1.5
- mlp_gain: bfloat16 [2048], P(('chan', 'seq')), may hold values from 0.5 to 1.5
- recur_proj: bfloat16 [2048, 2560], P('seq', 'chan'), may hold values from -0.125 to 0.125
- branch_proj: bfloat16 [2048, 2560], P('seq', 'chan'), may hold values from -0.125 to 0.125
- out_proj: bfloat16 [2560, 2048], P('chan', 'seq'), may hold values from -0.25 to 0.25
- gate_proj: bfloat16 [2048, 6144], P('seq', 'chan'), may hold values from -0.125 to 0.125
- up_proj: bfloat16 [2048, 6144], P('seq', 'chan'), may hold values from -0.125 to 0.125
- down_proj: bfloat16 [6144, 2048], P('chan', 'seq'), may hold values from -0.15625 to 0.15625
- recur_gate: bfloat16 [16, 160, 160], P('chan', 'seq'), may hold values from -0.5 to 0.5
- input_gate: bfloat16 [16, 160, 160], P('chan', 'seq'), may hold values from -0.5 to 0.5
- recur_bias: bfloat16 [2560], P(('chan', 'seq')), may hold values from -3 to 3
- input_bias: bfloat16 [2560], P(('chan', 'seq')), may hold values from -3 to 3
- decay_param: bfloat16 [2560], P(('chan', 'seq')), may hold values from 4.5 to 13
- conv_bias: bfloat16 [2560], P(('chan', 'seq')), may hold values from -3 to 3
- conv_weight: bfloat16 [4, 2560], P(None, ('chan', 'seq')), may hold values from -3 to 3
- init_state: bfloat16 [8, 2560], P(None, ('chan', 'seq')), may hold values from -6 to 6
- init_tail: bfloat16 [8, 3, 2560], P(None, None, ('chan', 'seq')), may hold values from -6 to 6
- reset_flags: int32 [8], replicated, may hold values from 0 to 1
- cotangent: bfloat16 [8, 1024, 2048], P(None, ('seq', 'chan')), may hold values from -6 to 6
Outputs:
- mixed: bfloat16 [8, 1024, 2048], P(None, ('seq', 'chan'))
- tokens_grad: float32 [8, 1024, 2048], P(None, ('seq', 'chan'))
- norm_gain_grad: float32 [2048], P(('chan', 'seq'))
- mlp_gain_grad: float32 [2048], P(('chan', 'seq'))
- recur_proj_grad: float32 [2048, 2560], P('seq', 'chan')
- branch_proj_grad: float32 [2048, 2560], P('seq', 'chan')
- out_proj_grad: float32 [2560, 2048], P('chan', 'seq')
- gate_proj_grad: float32 [2048, 6144], P('seq', 'chan')
- up_proj_grad: float32 [2048, 6144], P('seq', 'chan')
- down_proj_grad: float32 [6144, 2048], P('chan', 'seq')
- recur_gate_grad: float32 [16, 160, 160], P('chan', 'seq')
- input_gate_grad: float32 [16, 160, 160], P('chan', 'seq')
- recur_bias_grad: float32 [2560], P(('chan', 'seq'))
- input_bias_grad: float32 [2560], P(('chan', 'seq'))
- decay_grad: float32 [2560], P(('chan', 'seq'))
- conv_bias_grad: float32 [2560], P(('chan', 'seq'))
- conv_weight_grad: float32 [4, 2560], P(None, ('chan', 'seq'))
- state_grad: float32 [8, 2560], P(None, ('chan', 'seq'))
- tail_grad: float32 [8, 3, 2560], P(None, None, ('chan', 'seq'))
- group_states: float32 [4, 8, 2560], P('seq', None, 'chan')
- group_tails: bfloat16 [4, 8, 3, 2560], P('seq', None, None, 'chan')
The draws below stay inside these ranges and needn't reach their ends.
All inputs are finite; a program needn't handle non-finite values.
Results may differ from the reference program's by a relative error of at most 0.02.
Values may be sent and summed in bfloat16 or wider, within the bound.
No kernel may reach another device: no remote copies, remote signals or barrier semaphores. Data moves between devices by JAX's collectives and lax.ppermute only.
A program may use at most 384 MiB of HBM per device.

```python
import jax
import jax.numpy as jnp
from jax import lax

D = 2048
FF = 6144
HEADS = 16
BLOCK = 160
KW = 4
ROWS = 8
GROUP = 256
RNN = 2560
SEQLEN = 1024


def plant(values, own_key, least, top_value):
    index_at = [jax.random.randint(jax.random.fold_in(own_key, axis), (), 0, length) for axis, length in enumerate(values.shape)]
    main_axis = values.shape.index(max(values.shape))
    next_to = index_at[:main_axis] + [(index_at[main_axis] + 1) % values.shape[main_axis]] + index_at[main_axis + 1:]
    return values.at[tuple(index_at)].set(least).at[tuple(next_to)].set(top_value)


def block_scale(own_key, shape, pieces, smallest, largest):
    level = 1.0
    for axis_at, blocks in pieces:
        draws = jax.random.uniform(jax.random.fold_in(jax.random.fold_in(own_key, 6), axis_at), (blocks,), jnp.float32, smallest / len(pieces), largest / len(pieces))
        level = level * jnp.repeat(jnp.exp(draws), shape[axis_at] // blocks).reshape((-1,) + (1,) * (len(shape) - 1 - axis_at))
    return level


def scatter_about(stream_key, dims, scale, reach, pieces=(), dtype=jnp.bfloat16):
    array = scale * jax.random.normal(stream_key, dims, jnp.float32)
    if pieces:
        array = array * block_scale(stream_key, dims, pieces, -0.22, 0.18)
    return jnp.clip(array, -reach, reach).astype(dtype)


def setup_inputs(seed: int = 0) -> dict:
    key_of = jax.random.split(jax.random.key(seed), 21)
    tokens = scatter_about(key_of[0], (ROWS, SEQLEN, D), 1.0, 6.0, ((1, 32),))
    norm_gain = jnp.clip(1.0 + 0.1 * jax.random.normal(key_of[1], (D,), jnp.float32), 0.5, 1.5).astype(jnp.bfloat16)
    mlp_gain = jnp.clip(1.0 + 0.1 * jax.random.normal(key_of[2], (D,), jnp.float32), 0.5, 1.5).astype(jnp.bfloat16)
    recur_proj = scatter_about(key_of[3], (D, RNN), D ** -0.5, 0.125, ((0, 4), (1, 8)))
    branch_proj = scatter_about(key_of[4], (D, RNN), D ** -0.5, 0.125, ((0, 4), (1, 8)))
    out_proj = scatter_about(key_of[5], (RNN, D), (RNN // 4) ** -0.5, 0.25, ((0, 8), (1, 4)))
    gate_proj = scatter_about(key_of[6], (D, FF), D ** -0.5, 0.125, ((0, 4), (1, 8)))
    up_proj = scatter_about(key_of[7], (D, FF), D ** -0.5, 0.125, ((0, 4), (1, 8)))
    down_proj = scatter_about(key_of[8], (FF, D), (FF // 4) ** -0.5, 0.15625, ((0, 8), (1, 4)))
    recur_gate = scatter_about(key_of[9], (HEADS, BLOCK, BLOCK), BLOCK ** -0.5, 0.5, ((0, 8), (1, 4)))
    input_gate = scatter_about(key_of[10], (HEADS, BLOCK, BLOCK), BLOCK ** -0.5, 0.5, ((0, 8), (1, 4)))
    recur_bias = scatter_about(key_of[11], (RNN,), 1.0, 3.0, ((0, 32),))
    input_bias = scatter_about(key_of[12], (RNN,), 1.0, 3.0, ((0, 32),))
    decay_param = jnp.clip(4.5 + 8.5 * jax.random.uniform(key_of[13], (RNN,), jnp.float32) ** block_scale(key_of[13], (RNN,), ((0, 32),), -0.2, 0.2), 4.5, 13.0).astype(jnp.bfloat16)
    conv_bias = scatter_about(key_of[14], (RNN,), 0.5, 3.0, ((0, 32),))
    conv_weight = scatter_about(key_of[15], (KW, RNN), 0.5, 3.0, ((1, 32),))
    init_state = scatter_about(key_of[16], (ROWS, RNN), 1.0, 6.0, ((1, 32),))
    init_tail = scatter_about(key_of[17], (ROWS, KW - 1, RNN), 1.0, 6.0, ((2, 32),))
    reset_flags = plant(jax.random.randint(key_of[18], (ROWS,), 0, 2), jax.random.fold_in(key_of[18], 1), 0, 1).astype(jnp.int32)
    cotangent = scatter_about(key_of[19], (ROWS, SEQLEN, D), 1.0, 6.0, ((1, 32),))
    return {"tokens": tokens, "norm_gain": norm_gain, "mlp_gain": mlp_gain, "recur_proj": recur_proj, "branch_proj": branch_proj, "out_proj": out_proj, "gate_proj": gate_proj, "up_proj": up_proj, "down_proj": down_proj, "recur_gate": recur_gate, "input_gate": input_gate, "recur_bias": recur_bias, "input_bias": input_bias, "decay_param": decay_param, "conv_bias": conv_bias, "conv_weight": conv_weight, "init_state": init_state, "init_tail": init_tail, "reset_flags": reset_flags, "cotangent": cotangent}


@jax.custom_vjp
def low(v):
    return lax.optimization_barrier(v.astype(jnp.bfloat16)).astype(jnp.float32)

@jax.custom_vjp
def low_back(v):
    return v

def low_keep(v):
    return (low(v), None)

def low_pass(kept, grad):
    return (grad,)

def back_keep(v):
    return (v, None)

def back_low(kept, grad):
    return (low(grad),)
low.defvjp(low_keep, low_pass)
low_back.defvjp(back_keep, back_low)

def matmul(left, right):
    return jnp.dot(left, right, precision=lax.Precision.HIGHEST)

def rms_scale(value, gain):
    return value * lax.rsqrt(lax.optimization_barrier(jnp.mean(value * value, axis=-1, keepdims=True)) + 1e-06) * gain

def recur_block(state, pair):

    def advance(carry, item):
        fresh = item[0] * carry + item[1]
        return (fresh, fresh)
    return lax.scan(advance, state, pair)

def forward_row(x_row, h_row, tail_row, keep, gain_one, gain_two, recur_proj, branch_proj, out_proj, gate_proj, up_proj, down_proj, recur_gate, input_gate, recur_bias, input_bias, decay_param, conv_bias, conv_weight):
    seqlen = x_row.shape[0]
    taps = conv_weight.shape[0]
    lag = taps - 1
    heads = recur_gate.shape[0]
    normal_in = low(rms_scale(x_row, gain_one))
    conv_in = low(low_back(matmul(normal_in, recur_proj)))
    branch_pre = low_back(matmul(normal_in, branch_proj))
    branch_act = jax.nn.gelu(branch_pre)
    padded = jnp.concatenate([tail_row * keep, conv_in], axis=0)
    conv_out = conv_bias + sum((conv_weight[offset] * padded[lag - offset:lag - offset + seqlen] for offset in range(taps)))
    conv_low = low(conv_out)
    split_v = conv_low.reshape(seqlen, heads, -1)
    recur_pre = low_back(jnp.einsum('thb,hbe->the', split_v, recur_gate, precision=lax.Precision.HIGHEST).reshape(seqlen, -1) + recur_bias)
    input_pre = low_back(jnp.einsum('thb,hbe->the', split_v, input_gate, precision=lax.Precision.HIGHEST).reshape(seqlen, -1) + input_bias)
    recur_rate = jax.nn.sigmoid(recur_pre)
    input_rate = jax.nn.sigmoid(input_pre)
    log_decay = -8.0 * recur_rate * jax.nn.softplus(-decay_param)
    decay = jnp.exp(log_decay)
    drive = conv_low * input_rate * jnp.sqrt(-jnp.expm1(2.0 * log_decay))
    blocks = seqlen // GROUP
    last, states = lax.scan(jax.checkpoint(recur_block), h_row * keep, (decay.reshape(blocks, GROUP, -1), drive.reshape(blocks, GROUP, -1)))
    hidden_state = states.reshape(seqlen, -1)
    mixed_rec = low(hidden_state * branch_act)
    branch_out = low_back(matmul(mixed_rec, out_proj))
    resid = x_row + branch_out
    normal_mid = low(rms_scale(resid, gain_two))
    gate_pre = low_back(matmul(normal_mid, gate_proj))
    up_pre = low_back(matmul(normal_mid, up_proj))
    hidden = low(jax.nn.gelu(gate_pre) * up_pre)
    output = resid + matmul(hidden, down_proj)
    group_end = hidden_state.reshape(blocks, GROUP, -1)[:, GROUP - 1]
    group_tail = conv_in.reshape(blocks, GROUP, -1)[:, GROUP - lag:]
    return (output, (group_end, group_tail))

def reference(tokens, norm_gain, mlp_gain, recur_proj, branch_proj, out_proj, gate_proj, up_proj, down_proj, recur_gate, input_gate, recur_bias, input_bias, decay_param, conv_bias, conv_weight, init_state, init_tail, reset_flags, cotangent):
    params = tuple((item.astype(jnp.float32) for item in (norm_gain, mlp_gain, recur_proj, branch_proj, out_proj, gate_proj, up_proj, down_proj, recur_gate, input_gate, recur_bias, input_bias, decay_param, conv_bias, conv_weight)))
    keep_all = 1.0 - reset_flags.astype(jnp.float32)
    totals_init = tuple((jnp.zeros(item.shape, jnp.float32) for item in params))

    def one_row(totals, item):
        x_row, cot_row, h_row, tail_row, keep = item

        def forward(x_in, h_in, tail_in, *weights):
            return forward_row(x_in, h_in, tail_in, keep, *weights)
        output, pullback, extra = jax.vjp(forward, x_row, h_row, tail_row, *params, has_aux=True)
        grads = pullback(cot_row)
        summed = tuple((total + grad for total, grad in zip(totals, grads[3:])))
        return (summed, (output, grads[0], grads[1], grads[2], extra[0], extra[1]))
    totals, results = lax.scan(one_row, totals_init, (tokens.astype(jnp.float32), cotangent.astype(jnp.float32), init_state.astype(jnp.float32), init_tail.astype(jnp.float32), keep_all))
    output, tokens_grad, state_grad, tail_grad, ends, tails = results
    return (output.astype(jnp.bfloat16), tokens_grad, totals[0], totals[1], totals[2], totals[3], totals[4], totals[5], totals[6], totals[7], totals[8], totals[9], totals[10], totals[11], totals[12], totals[13], totals[14], state_grad, tail_grad, jnp.transpose(ends, (1, 0, 2)), jnp.transpose(tails, (1, 0, 2, 3)).astype(jnp.bfloat16))
```

```python
import functools

import jax
import jax.numpy as jnp
from jax import lax
from jax.experimental import pallas as pl
from jax.experimental.pallas import tpu as pltpu
from jax.sharding import Mesh
from jax.sharding import PartitionSpec as P

BF = jnp.bfloat16
F32 = jnp.float32
BLOCKS = ("sx", "sc", "co")
PEERS = ("ca", "cb")
EVERY = ("co", "ca", "cb", "sx", "sc")
PEER = 4
GELU_C = 0.7978845608028654
GELU_K = 0.044715


def shift(value, axis, step):
    count = lax.axis_size(axis)
    return lax.ppermute(value, axis, [(i, (i + step) % count) for i in range(count)])


def peer(value, step):
    return lax.ppermute(value, PEERS, [(i, i ^ step) for i in range(PEER)])


def block_shift(value, step):
    count = lax.axis_size(BLOCKS)
    route = [(i, i + step) for i in range(count) if 0 <= i + step < count]
    return lax.ppermute(value, BLOCKS, route)


def chunk_roll(value, step):
    count = lax.axis_size("co")
    step = step % count
    if step == 0:
        return value
    width = value.shape[-1] // count
    cut = width * (count - step)
    return jnp.concatenate([value[..., cut:], value[..., :cut]], axis=-1)


def feature_order(value):
    nsx, nsc = lax.axis_size("sx"), lax.axis_size("sc")
    sx, sc = lax.axis_index("sx"), lax.axis_index("sc")
    width = value.shape[-1] // (nsx * nsc)
    parts = []
    for rc in range(nsc):
        for rx in range(nsx):
            owner = lax.rem(sx - rx + nsx, nsx) * nsc + lax.rem(sc - rc + nsc, nsc)
            parts.append(lax.dynamic_slice_in_dim(value, owner * width, width, value.ndim - 1))
    return jnp.concatenate(parts, axis=-1)


def feature_restore(value):
    nsx, nsc = lax.axis_size("sx"), lax.axis_size("sc")
    sx, sc = lax.axis_index("sx"), lax.axis_index("sc")
    width = value.shape[-1] // (nsx * nsc)
    parts = []
    for owner in range(nsx * nsc):
        rx = lax.rem(sx - owner // nsc + nsx, nsx)
        rc = lax.rem(sc - owner % nsc + nsc, nsc)
        parts.append(
            lax.dynamic_slice_in_dim(value, (rc * nsx + rx) * width, width, value.ndim - 1)
        )
    return jnp.concatenate(parts, axis=-1)


def chunk_order(value, axis):
    count, mine = lax.axis_size("co"), lax.axis_index("co")
    return jnp.concatenate(
        [
            lax.dynamic_slice_in_dim(value, lax.rem(mine - r + count, count), 1, axis)
            for r in range(count)
        ],
        axis=axis,
    )


def gather_weight(shard, join):
    held = join([shard] + [shift(shard, "co", r) for r in range(1, lax.axis_size("co"))])
    rows = [held] + [shift(held, "sx", r) for r in range(1, lax.axis_size("sx"))]
    return rows + [shift(item, "sc", 1) for item in rows]


def scatter_weight(grad, cut, axis):
    nsx = lax.axis_size("sx")
    half = grad.shape[axis] // 2
    mine = lax.slice_in_dim(grad, 0, half, axis=axis).astype(F32)
    mine = mine + shift(lax.slice_in_dim(grad, half, 2 * half, axis=axis), "sc", -1).astype(F32)
    width = half // nsx
    total = lax.slice_in_dim(mine, 0, width, axis=axis)
    for r in range(1, nsx):
        part = lax.slice_in_dim(mine, r * width, (r + 1) * width, axis=axis).astype(BF)
        total = total + shift(part, "sx", -r).astype(F32)
    parts = cut(total)
    total = parts[0]
    for r in range(1, len(parts)):
        total = total + shift(parts[r].astype(BF), "co", -r).astype(F32)
    return total


def matmul(left, right):
    return jnp.dot(left, right, preferred_element_type=F32)


def over_tokens(left, right):
    return lax.dot_general(left, right, (((0,), (0,)), ((), ())), preferred_element_type=F32)


def times_transpose(left, right):
    return lax.dot_general(left, right, (((1,), (1,)), ((), ())), preferred_element_type=F32)


def collect(value):
    return [value] + [peer(value, k) for k in range(1, PEER)]


def hand_back(pieces):
    total = pieces[0]
    for k in range(1, PEER):
        total = total + peer(pieces[k].astype(BF), k).astype(F32)
    return total


def gelu_parts(value):
    square = value * value
    wave = jnp.tanh(GELU_C * (value + GELU_K * value * square))
    half = 0.5 * (1.0 + wave)
    slope = half + 0.5 * value * (1.0 - wave * wave) * (GELU_C * (1.0 + 3.0 * GELU_K * square))
    return value * half, slope


def minus_expm1(value):
    series = 1.0 + value * (1.0 / 7.0)
    for order in (6.0, 5.0, 4.0, 3.0, 2.0):
        series = 1.0 + value * (1.0 / order) * series
    return -jnp.where(value > -0.3, value * series, jnp.exp(value) - 1.0)


def decay_terms(rate, soft):
    log_decay = -8.0 * rate * soft
    return jnp.exp(log_decay), jnp.sqrt(minus_expm1(2.0 * log_decay))


def gates_kernel(
    ci, u_ref, edge_ref, gate_ref, vec_ref, v_ref, ra_ref, ri_ref, a_ref, e_ref, before_ref, end_ref,
    pad, held,
):
    step = pl.program_id(0)
    rows = held.shape[0] // 2
    size = u_ref.shape[0]
    lag = edge_ref.shape[0]
    width = u_ref.shape[1]

    @pl.when(step == 0)
    def _():
        pad[0:lag, :] = edge_ref[...].astype(F32)
        held[0:rows, :] = jnp.ones((rows, width), F32)
        held[rows:, :] = jnp.zeros((rows, width), F32)

    @pl.when(step > 0)
    def _():
        pad[0:lag, :] = pad[size : size + lag, :]

    pad[lag:, :] = u_ref[...].astype(BF).astype(F32)
    before_ref[...] = pad[0:lag, :]
    taps = lag // rows + 1
    conv = vec_ref[taps : taps + 1, :] + vec_ref[0:1, :] * pad[lag : lag + size, :]
    for k in range(1, taps):
        conv = conv + vec_ref[k : k + 1, :] * pad[lag - rows * k : lag - rows * k + size, :]
    low = conv.astype(BF)
    v_ref[...] = low
    pre = jnp.dot(low, gate_ref[...], preferred_element_type=F32)
    ra = jax.nn.sigmoid(pre[:, :width] + vec_ref[taps + 1 : taps + 2, :])
    ri = jax.nn.sigmoid(pre[:, width:] + vec_ref[taps + 2 : taps + 3, :])
    decay, root = decay_terms(ra, vec_ref[taps + 3 : taps + 4, :])
    ra_ref[...] = ra
    ri_ref[...] = ri
    a_ref[...] = decay
    e_ref[...] = low.astype(F32) * ri * root
    prod = held[0:rows, :]
    state = held[rows:, :]
    for t in range(size // rows):
        now = a_ref[t * rows : (t + 1) * rows, :]
        state = now * state + e_ref[t * rows : (t + 1) * rows, :]
        prod = prod * now
    held[0:rows, :] = prod
    held[rows:, :] = state
    end_ref[0:rows, :] = prod
    end_ref[rows:, :] = state


def states_kernel(ci, a_ref, e_ref, yp_ref, enter_ref, h_ref, z_ref, before_ref, end_ref, held):
    step = pl.program_id(0)
    rows = held.shape[0]

    @pl.when(step == 0)
    def _():
        held[...] = enter_ref[...]

    state = held[...]
    before_ref[...] = state
    for t in range(a_ref.shape[0] // rows):
        at = slice(t * rows, (t + 1) * rows)
        state = a_ref[at, :] * state + e_ref[at, :]
        h_ref[at, :] = state
    held[...] = state
    end_ref[...] = state
    act, _ = gelu_parts(yp_ref[...])
    z_ref[...] = (h_ref[...] * act).astype(BF)


def back_kernel(ci, dz_ref, yp_ref, h_ref, a_ref, dh_ref, dyp_ref, end_ref, held):
    step = pl.program_id(0)
    rows = held.shape[0]

    @pl.when(step == 0)
    def _():
        held[...] = jnp.zeros(held.shape, F32)

    act, slope = gelu_parts(yp_ref[...])
    dz = dz_ref[...]
    dh_ref[...] = dz * act
    dyp_ref[...] = (dz * h_ref[...] * slope).astype(BF)
    carry = held[...]
    for t in reversed(range(a_ref.shape[0] // rows)):
        at = slice(t * rows, (t + 1) * rows)
        carry = a_ref[at, :] * (dh_ref[at, :] + carry)
    held[...] = carry
    end_ref[...] = carry


def grads_kernel(
    ci, dh_ref, a_ref, ra_ref, ri_ref, v_ref, h_ref, hb_ref, u_ref, ub_ref, gate_ref, vec_ref,
    late_ref, gates_ref, du_ref, edge_ref, last_ref, sums_ref, end_ref, held, pad, spad, hpad, upad,
):
    step = pl.program_id(0)
    rows = held.shape[0]
    size = dh_ref.shape[0]
    width = dh_ref.shape[1]
    lag = ub_ref.shape[0]
    taps = lag // rows + 1

    @pl.when(step == 0)
    def _():
        held[...] = late_ref[...]
        pad[size:, :] = jnp.zeros((lag, width), F32)
        sums_ref[...] = jnp.zeros(sums_ref.shape, F32)

    @pl.when(step > 0)
    def _():
        pad[size:, :] = pad[0:lag, :]

    carry = held[...]
    for t in reversed(range(size // rows)):
        at = slice(t * rows, (t + 1) * rows)
        now = dh_ref[at, :] + carry
        spad[at, :] = now
        carry = a_ref[at, :] * now
    held[...] = carry
    end_ref[...] = carry
    hpad[0:rows, :] = hb_ref[...]
    hpad[rows:, :] = h_ref[...]
    upad[0:lag, :] = ub_ref[...]
    upad[lag:, :] = u_ref[...].astype(BF).astype(F32)
    s = spad[...]
    ra = ra_ref[...]
    ri = ri_ref[...]
    soft = vec_ref[taps + 3 : taps + 4, :]
    decay, root = decay_terms(ra, soft)
    v = v_ref[...].astype(F32)
    sv = s * v
    grad_log = decay * (s * hpad[0:size, :] - sv * ri * decay / root)
    rated = grad_log * ra
    dap = (-8.0 * soft * rated * (1.0 - ra)).astype(BF)
    dip = (sv * root * ri * (1.0 - ri)).astype(BF)
    gates_ref[:, :width] = dap
    gates_ref[:, width:] = dip
    dv = s * ri * root + lax.dot_general(
        gates_ref[...], gate_ref[...], (((1,), (1,)), ((), ())), preferred_element_type=F32
    )
    pad[0:size, :] = dv

    def fold(value):
        return jnp.sum(value.reshape(size // rows, rows, width), axis=0)

    terms = [dap.astype(F32), dip.astype(F32), rated, dv]
    terms = terms + [dv * upad[lag - rows * k : lag - rows * k + size, :] for k in range(taps)]
    for i, term in enumerate(terms):
        sums_ref[i * rows : (i + 1) * rows, :] += fold(term)
    du = vec_ref[0:1, :] * dv
    for k in range(1, taps):
        du = du + vec_ref[k : k + 1, :] * pad[rows * k : rows * k + size, :]
    du_ref[...] = du.astype(BF)

    @pl.when(step == 0)
    def _():
        last_ref[...] = du[size - lag :, :]

    for t in range(taps - 1):
        row = jnp.zeros((rows, width), F32)
        for k in range(taps - 1 - t, taps):
            at = (t + k - (taps - 1)) * rows
            row = row + vec_ref[k : k + 1, :] * pad[at : at + rows, :]
        edge_ref[t * rows : (t + 1) * rows, :] = row


def gates_call(ci, uy, edge, gate, vec, rows):
    steps, size, wide = uy.shape
    width = wide // 2
    lag = edge.shape[0]
    here = pl.BlockSpec((None, size, width), lambda j, c: (j, 0, 0))
    whole = lambda shape: pl.BlockSpec(shape, lambda j, c: (0,) * len(shape))
    full = jax.ShapeDtypeStruct((steps, size, width), F32)
    return pl.pallas_call(
        gates_kernel,
        out_shape=(
            jax.ShapeDtypeStruct((steps, size, width), BF),
            full,
            full,
            full,
            full,
            jax.ShapeDtypeStruct((steps, lag, width), F32),
            jax.ShapeDtypeStruct((2 * rows, width), F32),
        ),
        grid_spec=pltpu.PrefetchScalarGridSpec(
            num_scalar_prefetch=1,
            grid=(steps,),
            in_specs=[
                pl.BlockSpec((None, size, width), lambda j, c: (j ^ c[0], 0, 0)),
                whole(edge.shape),
                whole(gate.shape),
                whole(vec.shape),
            ],
            out_specs=[
                here,
                here,
                here,
                here,
                here,
                pl.BlockSpec((None, lag, width), lambda j, c: (j, 0, 0)),
                whole((2 * rows, width)),
            ],
            scratch_shapes=[
                pltpu.VMEM((size + lag, width), F32),
                pltpu.VMEM((2 * rows, width), F32),
            ],
        ),
        name="gates",
    )(ci, uy, edge, gate, vec)


def states_call(ci, a, e, uy, enter):
    steps, size, width = a.shape
    rows = enter.shape[0]
    here = pl.BlockSpec((None, size, width), lambda j, c: (j, 0, 0))
    whole = pl.BlockSpec((rows, width), lambda j, c: (0, 0))
    return pl.pallas_call(
        states_kernel,
        out_shape=(
            jax.ShapeDtypeStruct((steps, size, width), F32),
            jax.ShapeDtypeStruct((steps, size, width), BF),
            jax.ShapeDtypeStruct((steps, rows, width), F32),
            jax.ShapeDtypeStruct((rows, width), F32),
        ),
        grid_spec=pltpu.PrefetchScalarGridSpec(
            num_scalar_prefetch=1,
            grid=(steps,),
            in_specs=[
                here,
                here,
                pl.BlockSpec((None, size, width), lambda j, c: (j ^ c[0], 0, 1)),
                whole,
            ],
            out_specs=[
                here,
                pl.BlockSpec((None, size, width), lambda j, c: (j ^ c[0], 0, 0)),
                pl.BlockSpec((None, rows, width), lambda j, c: (j, 0, 0)),
                whole,
            ],
            scratch_shapes=[pltpu.VMEM((rows, width), F32)],
        ),
        name="states",
    )(ci, a, e, uy, enter)


def back_call(ci, dz, uy, h, a, rows):
    steps, size, width = a.shape
    last = steps - 1
    here = pl.BlockSpec((None, size, width), lambda j, c: (last - j, 0, 0))
    there = pl.BlockSpec((None, size, width), lambda j, c: ((last - j) ^ c[0], 0, 0))
    return pl.pallas_call(
        back_kernel,
        out_shape=(
            jax.ShapeDtypeStruct((steps, size, width), F32),
            jax.ShapeDtypeStruct((steps, size, width), BF),
            jax.ShapeDtypeStruct((rows, width), F32),
        ),
        grid_spec=pltpu.PrefetchScalarGridSpec(
            num_scalar_prefetch=1,
            grid=(steps,),
            in_specs=[
                there,
                pl.BlockSpec((None, size, width), lambda j, c: ((last - j) ^ c[0], 0, 1)),
                here,
                here,
            ],
            out_specs=[here, there, pl.BlockSpec((rows, width), lambda j, c: (0, 0))],
            scratch_shapes=[pltpu.VMEM((rows, width), F32)],
        ),
        name="back",
    )(ci, dz, uy, h, a)


def grads_call(ci, dh, a, ra, ri, v, h, h_before, uy, u_before, gate, vec, late):
    steps, size, width = a.shape
    rows = late.shape[0]
    lag = u_before.shape[1]
    last = steps - 1
    count = lag // rows + 5
    here = pl.BlockSpec((None, size, width), lambda j, c: (last - j, 0, 0))
    there = pl.BlockSpec((None, size, width), lambda j, c: ((last - j) ^ c[0], 0, 0))
    small = lambda size: pl.BlockSpec((None, size, width), lambda j, c: (last - j, 0, 0))
    whole = lambda shape: pl.BlockSpec(shape, lambda j, c: (0,) * len(shape))
    return pl.pallas_call(
        grads_kernel,
        out_shape=(
            jax.ShapeDtypeStruct((steps, size, 2 * width), BF),
            jax.ShapeDtypeStruct((steps, size, width), BF),
            jax.ShapeDtypeStruct((lag, width), F32),
            jax.ShapeDtypeStruct((lag, width), F32),
            jax.ShapeDtypeStruct((count * rows, width), F32),
            jax.ShapeDtypeStruct((rows, width), F32),
        ),
        grid_spec=pltpu.PrefetchScalarGridSpec(
            num_scalar_prefetch=1,
            grid=(steps,),
            in_specs=[
                here,
                here,
                here,
                here,
                here,
                here,
                small(rows),
                there,
                small(lag),
                whole(gate.shape),
                whole(vec.shape),
                whole(late.shape),
            ],
            out_specs=[
                pl.BlockSpec((None, size, 2 * width), lambda j, c: (last - j, 0, 0)),
                there,
                whole((lag, width)),
                whole((lag, width)),
                whole((count * rows, width)),
                whole((rows, width)),
            ],
            scratch_shapes=[
                pltpu.VMEM((rows, width), F32),
                pltpu.VMEM((size + lag, width), F32),
                pltpu.VMEM((size, width), F32),
                pltpu.VMEM((size + rows, width), F32),
                pltpu.VMEM((size + lag, width), F32),
            ],
        ),
        name="grads",
    )(ci, dh, a, ra, ri, v, h, h_before, uy, u_before, gate, vec, late)


def norm_back(grad_norm, normed, inv_root, gain):
    scaled = grad_norm * gain
    mean_term = jnp.mean(scaled * normed, axis=-1, keepdims=True)
    return inv_root * (scaled - normed * mean_term)


def inverse_rms(value):
    return lax.rsqrt(jnp.mean(value * value, axis=-1, keepdims=True) + 1e-06)


def shards(
    tokens,
    norm_gain,
    mlp_gain,
    recur_proj,
    branch_proj,
    out_proj,
    gate_proj,
    up_proj,
    down_proj,
    recur_gate,
    input_gate,
    recur_bias,
    input_bias,
    decay_param,
    conv_bias,
    conv_weight,
    init_state,
    init_tail,
    reset_flags,
    cotangent,
):
    nsx, nsc, nco = (lax.axis_size(name) for name in BLOCKS)
    nseq = nsx * nsc
    blocks = nseq * nco
    co = lax.axis_index("co")
    block = lax.axis_index(BLOCKS)
    first = block == 0
    ci = lax.axis_index(PEERS)
    order = ci.astype(jnp.int32).reshape(1)
    rows, share, model = tokens.shape
    own = rows * share
    taps = conv_weight.shape[0]
    lag = taps - 1
    part = conv_bias.shape[0]
    chunk = part * nseq
    width = chunk * nco
    keep = (1 - reset_flags).astype(F32)[:, None]

    def owned(value):
        return feature_order(jnp.swapaxes(value, 0, 1).reshape(own, model))

    gains = lax.all_gather(jnp.stack([norm_gain, mlp_gain]), EVERY, axis=0)
    gains = feature_order(jnp.swapaxes(gains, 0, 1).reshape(2, model).astype(F32))
    gain_one, gain_two = (gains[0:1], gains[1:2])
    vectors = jnp.concatenate(
        [
            conv_weight,
            conv_bias[None],
            recur_bias[None],
            input_bias[None],
            decay_param[None],
            init_state,
            jnp.swapaxes(init_tail, 0, 1).reshape(lag * rows, part),
        ],
        axis=0,
    )
    vectors = lax.all_gather(vectors, BLOCKS, axis=0)
    vectors = jnp.transpose(vectors.reshape(nseq, nco, -1, part), (2, 1, 0, 3))
    vectors = chunk_order(vectors, 1).reshape(-1, width).astype(F32)
    decay32 = vectors[taps + 3 : taps + 4]
    vec = jnp.concatenate([vectors[: taps + 3], jax.nn.softplus(-decay32)], axis=0)
    vec = jnp.pad(vec, ((0, -vec.shape[0] % 8), (0, 0)))
    state_start = vectors[taps + 4 : taps + 4 + rows] * keep
    tail_start = vectors[taps + 4 + rows :] * jnp.tile(keep, (lag, 1))
    both = jnp.stack([recur_gate, input_gate])
    heads, span = both.shape[1], both.shape[3]
    both = lax.all_gather(both, BLOCKS, axis=0).reshape(nseq, nco, 2, heads, -1, span)
    both = chunk_order(jnp.transpose(both, (2, 1, 3, 0, 4, 5)), 1)
    both = both.reshape(2, nco * heads, span, span)
    gate = jnp.concatenate(
        [
            jnp.concatenate(
                [
                    jnp.pad(both[g, h], ((0, 0), (span * h, width - span * (h + 1))))
                    for h in range(nco * heads)
                ],
                axis=0,
            )
            for g in range(2)
        ],
        axis=1,
    )

    def sides(items):
        half = items[0].shape[1] // 2
        return jnp.concatenate(
            [item[:, :half] for item in items] + [item[:, half:] for item in items], axis=1
        )

    def stacked(items):
        return jnp.concatenate(items, axis=0)

    mine = owned(tokens)
    group = collect(mine)
    full_in = jnp.concatenate(
        gather_weight(jnp.concatenate([recur_proj, branch_proj], axis=1), sides), axis=0
    )
    full_out = jnp.concatenate(gather_weight(out_proj, stacked), axis=1)
    mlp_parts = gather_weight(jnp.concatenate([gate_proj, up_proj], axis=1), sides)
    inner = mlp_parts[0].shape[1] // 2
    full_gate = jnp.concatenate([item[:, :inner] for item in mlp_parts], axis=0)
    full_up = jnp.concatenate([item[:, inner:] for item in mlp_parts], axis=0)
    full_down = jnp.concatenate(gather_weight(down_proj, stacked), axis=1)
    grad_mine = owned(cotangent)
    grad_full = jnp.concatenate(collect(grad_mine), axis=0)

    def normal(piece):
        value = piece.astype(F32)
        return (value * inverse_rms(value) * gain_one).astype(BF)

    normal_in = jnp.concatenate([normal(piece) for piece in group], axis=0)
    uy = matmul(normal_in, full_in).reshape(PEER, own, 2 * width)

    edge_at = (lax.bitwise_xor(jnp.int32(PEER - 1), ci.astype(jnp.int32)), own - lag * rows, 0)
    ends = lax.dynamic_slice(uy, edge_at, (1, lag * rows, width))[0].astype(BF)
    edge = jnp.where(first, tail_start.astype(BF), chunk_roll(block_shift(ends, 1), 1))
    v, ra, ri, decay, drive, u_before, summary = gates_call(order, uy, edge, gate, vec, rows)
    enter = state_start
    for k in reversed(range(1, blocks)):
        other = chunk_roll(block_shift(summary, k), k)
        enter = jnp.where(block >= k, other[:rows] * enter + other[rows:], enter)
    h, z, h_before, h_end = states_call(order, decay, drive, uy, enter)
    branch = matmul(z.reshape(PEER * own, width), full_out).reshape(PEER, own, model)
    resid = mine.astype(F32) + hand_back([branch[k] for k in range(PEER)])

    inv_two = inverse_rms(resid)
    normed_two = resid * inv_two
    normal_mine = (normed_two * gain_two).astype(BF)
    normal_mid = jnp.concatenate(collect(normal_mine), axis=0)
    gate_pre = matmul(normal_mid, full_gate)
    up_pre = matmul(normal_mid, full_up)
    gate_act, gate_slope = gelu_parts(gate_pre)
    hidden = (gate_act * up_pre).astype(BF)
    mlp = matmul(hidden, full_down).astype(BF).reshape(PEER, own, model)
    mlp_sum = hand_back([mlp[k].astype(F32) for k in range(PEER)])
    mixed = (resid + mlp_sum).astype(BF)

    grad_hidden = times_transpose(grad_full, full_down)
    grad_gate = (grad_hidden * up_pre * gate_slope).astype(BF)
    grad_up = (grad_hidden * gate_act).astype(BF)
    mid = times_transpose(grad_gate, full_gate) + times_transpose(grad_up, full_up)
    mid = mid.reshape(PEER, own, model)
    mid_sum = hand_back([mid[k] for k in range(PEER)])
    gain_two_part = jnp.sum(mid_sum * normed_two, axis=0)
    resid_grad = grad_mine.astype(F32) + norm_back(mid_sum, normed_two, inv_two, gain_two)
    resid_low = jnp.concatenate(collect(resid_grad.astype(BF)), axis=0)
    down_grad = over_tokens(hidden, grad_full).astype(BF)
    gate_grad = over_tokens(normal_mid, grad_gate).astype(BF)
    up_grad = over_tokens(normal_mid, grad_up).astype(BF)

    out_grad = over_tokens(z.reshape(PEER * own, width), resid_low).astype(BF)
    dz = times_transpose(resid_low, full_out).reshape(PEER, own, width)
    dh, grad_branch, local_end = back_call(order, dz, uy, h, decay, rows)
    message = jnp.concatenate([summary[:rows], local_end], axis=0)
    late = jnp.zeros((rows, width), F32)
    for k in reversed(range(1, blocks)):
        other = chunk_roll(block_shift(message, -k), -k)
        late = jnp.where(block + k < blocks, other[:rows] * late + other[rows:], late)
    gates_low, grad_u, edge_out, last, sums, start_grad = grads_call(
        order, dh, decay, ra, ri, v, h, h_before, uy, u_before, gate, vec, late
    )
    edge_in = chunk_roll(block_shift(edge_out, -1), -1)
    grad_u = lax.dynamic_update_slice(grad_u, (last + edge_in).astype(BF)[None], edge_at)
    grad_u = grad_u.reshape(PEER * own, width)
    grad_branch = grad_branch.reshape(PEER * own, width)
    recur_grad = over_tokens(normal_in, grad_u).astype(BF)
    branch_grad = over_tokens(normal_in, grad_branch).astype(BF)
    both_grad = over_tokens(v.reshape(PEER * own, width), gates_low.reshape(PEER * own, 2 * width))
    back_terms = times_transpose(grad_u, full_in[:, :width]) + times_transpose(
        grad_branch, full_in[:, width:]
    )
    back_terms = back_terms.reshape(PEER, own, model)
    back_sum = hand_back([back_terms[k] for k in range(PEER)])
    value = mine.astype(F32)
    inv_one = inverse_rms(value)
    normed_one = value * inv_one
    gain_one_part = jnp.sum(back_sum * normed_one, axis=0)
    tokens_grad = resid_grad + norm_back(back_sum, normed_one, inv_one, gain_one)

    def right(total):
        half = total.shape[1] // nco
        return [total[:, r * half : (r + 1) * half] for r in range(nco)]

    def low(total):
        half = total.shape[0] // nco
        return [total[r * half : (r + 1) * half] for r in range(nco)]

    recur_out = scatter_weight(recur_grad, right, 0)
    branch_out = scatter_weight(branch_grad, right, 0)
    out_out = scatter_weight(out_grad, low, 1)
    gate_out = scatter_weight(gate_grad, right, 0)
    up_out = scatter_weight(up_grad, right, 0)
    down_out = scatter_weight(down_grad, low, 1)

    pieces = jnp.stack(
        [
            both_grad[span * h : span * (h + 1), g * width + span * h : g * width + span * (h + 1)]
            for g in range(2)
            for h in range(nco * heads)
        ]
    )
    pieces = chunk_order(pieces.reshape(2, nco, heads, nseq, -1, span), 1)
    pieces = jnp.transpose(pieces, (3, 1, 0, 2, 4, 5)).reshape(blocks, 2, heads, -1, span)
    both_out = lax.psum_scatter(
        pieces.astype(BF), BLOCKS, scatter_dimension=0, tiled=True
    )[0].astype(F32)

    sums = jnp.sum(sums.reshape(-1, rows, width), axis=1)
    small = jnp.concatenate(
        [
            sums[0:2],
            sums[2:3] * 8.0 * jax.nn.sigmoid(-decay32),
            sums[3:],
            jnp.where(first, keep * start_grad, 0.0),
            jnp.where(first, jnp.tile(keep, (lag, 1)) * edge_out, 0.0),
        ],
        axis=0,
    )
    small = chunk_order(small.reshape(-1, nco, nseq, part), 1)
    small = jnp.transpose(small, (2, 1, 0, 3)).reshape(blocks, -1, part)
    small = lax.psum_scatter(small, BLOCKS, scatter_dimension=0, tiled=True)[0]

    gain_parts = feature_restore(jnp.stack([gain_one_part, gain_two_part]))
    gain_parts = jnp.swapaxes(gain_parts.reshape(2, -1, norm_gain.shape[0]), 0, 1)
    gain_out = lax.psum_scatter(gain_parts, EVERY, scatter_dimension=0, tiled=True)[0]

    finish = jnp.concatenate([h_end, ends.astype(F32)], axis=0)
    reach = jnp.where(co == nco - 1, finish[:, :chunk], 0.0)
    for k in range(1, nco):
        piece = finish[:, (nco - k) * chunk : (nco - k + 1) * chunk]
        reach = reach + lax.ppermute(piece, "co", [(nco - 1, k - 1)])
    group_states = reach[:rows][None]
    group_tails = jnp.swapaxes(reach[rows:].reshape(lag, rows, chunk), 0, 1).astype(BF)[None]

    def returned(value):
        return jnp.swapaxes(feature_restore(value).reshape(share, rows, model), 0, 1)

    return (
        returned(mixed),
        returned(tokens_grad),
        gain_out[0],
        gain_out[1],
        recur_out,
        branch_out,
        out_out,
        gate_out,
        up_out,
        down_out,
        both_out[0],
        both_out[1],
        small[0],
        small[1],
        small[2],
        small[3],
        small[4 : 4 + taps],
        small[4 + taps : 4 + taps + rows],
        jnp.swapaxes(small[4 + taps + rows :].reshape(lag, rows, part), 0, 1),
        group_states,
        group_tails,
    )


def solution(mesh):
    nseq, nchan = mesh.devices.shape
    fine = Mesh(
        mesh.devices.reshape(nseq // 2, 2, nchan // PEER, 2, 2), ("sx", "sc", "co", "ca", "cb")
    )
    seq = ("sx", "sc")
    chan = ("co", "ca", "cb")
    place = P(None, seq + chan, None)
    vector = P(chan + seq)
    in_specs = (
        place,
        vector,
        vector,
        P(seq, chan),
        P(seq, chan),
        P(chan, seq),
        P(seq, chan),
        P(seq, chan),
        P(chan, seq),
        P(chan, seq, None),
        P(chan, seq, None),
        vector,
        vector,
        vector,
        vector,
        P(None, chan + seq),
        P(None, chan + seq),
        P(None, None, chan + seq),
        P(),
        place,
    )
    out_specs = (
        place,
        place,
        vector,
        vector,
        P(seq, chan),
        P(seq, chan),
        P(chan, seq),
        P(seq, chan),
        P(seq, chan),
        P(chan, seq),
        P(chan, seq, None),
        P(chan, seq, None),
        vector,
        vector,
        vector,
        vector,
        P(None, chan + seq),
        P(None, chan + seq),
        P(None, None, chan + seq),
        P(seq, None, chan),
        P(seq, None, None, chan),
    )
    return jax.shard_map(shards, mesh=fine, in_specs=in_specs, out_specs=out_specs, check_vma=False)
```

```python
import functools

import jax
import jax.numpy as jnp
from jax import lax
from jax.experimental import pallas as pl
from jax.experimental.pallas import tpu as pltpu
from jax.sharding import Mesh
from jax.sharding import PartitionSpec as P

BF = jnp.bfloat16
F32 = jnp.float32
BLOCKS = ("sx", "sc", "co")
PEERS = ("ca", "cb")
PEER = 4
GELU_C = 0.7978845608028654
GELU_K = 0.044715


def shift(value, axis, step):
    count = lax.axis_size(axis)
    return lax.ppermute(value, axis, [(i, (i + step) % count) for i in range(count)])


def peer(value, step):
    return lax.ppermute(value, PEERS, [(i, i ^ step) for i in range(PEER)])


def block_shift(value, step):
    count = lax.axis_size(BLOCKS)
    route = [(i, i + step) for i in range(count) if 0 <= i + step < count]
    return lax.ppermute(value, BLOCKS, route)


def chunk_roll(value, step):
    count = lax.axis_size("co")
    step = step % count
    if step == 0:
        return value
    width = value.shape[-1] // count
    cut = width * (count - step)
    return jnp.concatenate([value[..., cut:], value[..., :cut]], axis=-1)


def feature_order(value):
    nsx, nsc = lax.axis_size("sx"), lax.axis_size("sc")
    sx, sc = lax.axis_index("sx"), lax.axis_index("sc")
    width = value.shape[-1] // (nsx * nsc)
    parts = []
    for rc in range(nsc):
        for rx in range(nsx):
            owner = lax.rem(sx - rx + nsx, nsx) * nsc + lax.rem(sc - rc + nsc, nsc)
            parts.append(lax.dynamic_slice_in_dim(value, owner * width, width, value.ndim - 1))
    return jnp.concatenate(parts, axis=-1)


def feature_restore(value):
    nsx, nsc = lax.axis_size("sx"), lax.axis_size("sc")
    sx, sc = lax.axis_index("sx"), lax.axis_index("sc")
    width = value.shape[-1] // (nsx * nsc)
    parts = []
    for owner in range(nsx * nsc):
        rx = lax.rem(sx - owner // nsc + nsx, nsx)
        rc = lax.rem(sc - owner % nsc + nsc, nsc)
        parts.append(
            lax.dynamic_slice_in_dim(value, (rc * nsx + rx) * width, width, value.ndim - 1)
        )
    return jnp.concatenate(parts, axis=-1)


def after(value, *done):
    return lax.optimization_barrier((value, *done))[0]


def around(value, axis):
    return [value] + [shift(value, axis, r) for r in range(1, lax.axis_size(axis))]


def sum_around(parts, axis):
    total = parts[0].astype(F32)
    for r in range(1, len(parts)):
        total = total + shift(parts[r].astype(BF), axis, -r).astype(F32)
    return total


def cut(value, count, axis):
    size = value.shape[axis] // count
    return [lax.slice_in_dim(value, r * size, (r + 1) * size, axis=axis) for r in range(count)]


def over_cores(grad, axis):
    return sum_around(cut(grad, lax.axis_size("sc"), axis), "sc")


def over_chips(grad, axis):
    return sum_around(cut(grad, lax.axis_size("sx"), axis), "sx")


def over_chunks(grad, axis):
    return sum_around(cut(grad, lax.axis_size("co"), axis), "co")


def join_kernel(groups, *refs):
    out = refs[-1]
    width = refs[0].shape[1] // groups
    at = 0
    for g in range(groups):
        for ref in refs[:-1]:
            out[:, at : at + width] = ref[:, g * width : (g + 1) * width]
            at += width


def join_columns(items, groups):
    rows, width = items[0].shape
    block = rows // 4
    return pl.pallas_call(
        functools.partial(join_kernel, groups),
        out_shape=jax.ShapeDtypeStruct((rows, width * len(items)), items[0].dtype),
        grid=(4,),
        in_specs=[pl.BlockSpec((block, width), lambda i: (i, 0))] * len(items),
        out_specs=pl.BlockSpec((block, width * len(items)), lambda i: (i, 0)),
        name="join",
    )(*items)


def compose(earlier, later, rows):
    decay, state = later[:rows], later[rows:]
    return jnp.concatenate([earlier[:rows] * decay, decay * earlier[rows:] + state], axis=0)


def other_blocks(summary, rows, backward):
    width = summary.shape[-1]
    empty = jnp.concatenate([jnp.ones((rows, width), F32), jnp.zeros((rows, width), F32)], axis=0)
    outer = empty
    for axis in ("co", "sc", "sx"):
        count, mine = lax.axis_size(axis), lax.axis_index(axis)
        items = around(summary, axis)
        if axis == "co":
            items = [chunk_roll(item, r) for r, item in enumerate(items)]
        if count == 2:
            mate = items[1]
            ahead = (mine == 0) if backward else (mine == 1)
            joined = compose(mate, summary, rows)
            outer = jnp.where(ahead, compose(mate, outer, rows), outer)
            summary = jnp.where(ahead, joined, compose(summary, mate, rows))
        else:
            table = jnp.stack(items)
            total, inner = empty, empty
            for place in reversed(range(count)) if backward else range(count):
                item = table[lax.rem(mine - place + count, count)]
                total = compose(total, item, rows)
                ahead = (place > mine) if backward else (place < mine)
                inner = jnp.where(ahead, compose(inner, item, rows), inner)
            outer = compose(inner, outer, rows)
            summary = total
    return outer


def matmul(left, right):
    return jnp.dot(left, right, preferred_element_type=F32)


def over_tokens(left, right):
    return lax.dot_general(left, right, (((0,), (0,)), ((), ())), preferred_element_type=F32)


def times_transpose(left, right):
    return lax.dot_general(left, right, (((1,), (1,)), ((), ())), preferred_element_type=F32)


def collect(value):
    return [value] + [peer(value, k) for k in range(1, PEER)]


def hand_back(pieces):
    total = pieces[0]
    for k in range(1, PEER):
        total = total + peer(pieces[k].astype(BF), k).astype(F32)
    return total


def gelu_parts(value):
    square = value * value
    wave = jnp.tanh(GELU_C * (value + GELU_K * value * square))
    half = 0.5 * (1.0 + wave)
    slope = half + 0.5 * value * (1.0 - wave * wave) * (GELU_C * (1.0 + 3.0 * GELU_K * square))
    return value * half, slope


def minus_expm1(value):
    series = 1.0 + value * (1.0 / 7.0)
    for order in (6.0, 5.0, 4.0, 3.0, 2.0):
        series = 1.0 + value * (1.0 / order) * series
    return -jnp.where(value > -0.3, value * series, jnp.exp(value) - 1.0)


def decay_terms(rate, soft):
    log_decay = -8.0 * rate * soft
    return jnp.exp(log_decay), jnp.sqrt(minus_expm1(2.0 * log_decay))


def gates_kernel(
    ci, u_ref, edge_ref, gate_ref, vec_ref, v_ref, ra_ref, ri_ref, a_ref, e_ref, before_ref, end_ref,
    pad, held,
):
    step = pl.program_id(0)
    rows = held.shape[0] // 2
    size = u_ref.shape[0]
    lag = edge_ref.shape[0]
    width = u_ref.shape[1]

    @pl.when(step == 0)
    def _():
        pad[0:lag, :] = edge_ref[...].astype(F32)
        held[0:rows, :] = jnp.ones((rows, width), F32)
        held[rows:, :] = jnp.zeros((rows, width), F32)

    @pl.when(step > 0)
    def _():
        pad[0:lag, :] = pad[size : size + lag, :]

    pad[lag:, :] = u_ref[...].astype(BF).astype(F32)
    before_ref[...] = pad[0:lag, :]
    taps = lag // rows + 1
    conv = vec_ref[taps : taps + 1, :] + vec_ref[0:1, :] * pad[lag : lag + size, :]
    for k in range(1, taps):
        conv = conv + vec_ref[k : k + 1, :] * pad[lag - rows * k : lag - rows * k + size, :]
    low = conv.astype(BF)
    v_ref[...] = low
    pre = jnp.dot(low, gate_ref[...], preferred_element_type=F32)
    ra = jax.nn.sigmoid(pre[:, :width] + vec_ref[taps + 1 : taps + 2, :])
    ri = jax.nn.sigmoid(pre[:, width:] + vec_ref[taps + 2 : taps + 3, :])
    decay, root = decay_terms(ra, vec_ref[taps + 3 : taps + 4, :])
    ra_ref[...] = ra
    ri_ref[...] = ri
    a_ref[...] = decay
    e_ref[...] = low.astype(F32) * ri * root
    prod = held[0:rows, :]
    state = held[rows:, :]
    for t in range(size // rows):
        now = a_ref[t * rows : (t + 1) * rows, :]
        state = now * state + e_ref[t * rows : (t + 1) * rows, :]
        prod = prod * now
    held[0:rows, :] = prod
    held[rows:, :] = state
    end_ref[0:rows, :] = prod
    end_ref[rows:, :] = state


def states_kernel(ci, a_ref, e_ref, yp_ref, enter_ref, h_ref, z_ref, before_ref, end_ref, held):
    step = pl.program_id(0)
    rows = held.shape[0]

    @pl.when(step == 0)
    def _():
        held[...] = enter_ref[...]

    state = held[...]
    before_ref[...] = state
    for t in range(a_ref.shape[0] // rows):
        at = slice(t * rows, (t + 1) * rows)
        state = a_ref[at, :] * state + e_ref[at, :]
        h_ref[at, :] = state
    held[...] = state
    end_ref[...] = state
    act, _ = gelu_parts(yp_ref[...])
    z_ref[...] = (h_ref[...] * act).astype(BF)


def back_kernel(ci, dz_ref, yp_ref, h_ref, a_ref, dh_ref, dyp_ref, end_ref, held):
    step = pl.program_id(0)
    rows = held.shape[0]

    @pl.when(step == 0)
    def _():
        held[...] = jnp.zeros(held.shape, F32)

    act, slope = gelu_parts(yp_ref[...])
    dz = dz_ref[...]
    dh_ref[...] = dz * act
    dyp_ref[...] = (dz * h_ref[...] * slope).astype(BF)
    carry = held[...]
    for t in reversed(range(a_ref.shape[0] // rows)):
        at = slice(t * rows, (t + 1) * rows)
        carry = a_ref[at, :] * (dh_ref[at, :] + carry)
    held[...] = carry
    end_ref[...] = carry


def grads_kernel(
    ci, dh_ref, a_ref, ra_ref, ri_ref, v_ref, h_ref, hb_ref, u_ref, ub_ref, gate_ref, vec_ref,
    late_ref, gates_ref, du_ref, edge_ref, last_ref, sums_ref, end_ref, held, pad, spad, hpad, upad,
):
    step = pl.program_id(0)
    rows = held.shape[0]
    size = dh_ref.shape[0]
    width = dh_ref.shape[1]
    lag = ub_ref.shape[0]
    taps = lag // rows + 1

    @pl.when(step == 0)
    def _():
        held[...] = late_ref[...]
        pad[size:, :] = jnp.zeros((lag, width), F32)
        sums_ref[...] = jnp.zeros(sums_ref.shape, F32)

    @pl.when(step > 0)
    def _():
        pad[size:, :] = pad[0:lag, :]

    carry = held[...]
    for t in reversed(range(size // rows)):
        at = slice(t * rows, (t + 1) * rows)
        now = dh_ref[at, :] + carry
        spad[at, :] = now
        carry = a_ref[at, :] * now
    held[...] = carry
    end_ref[...] = carry
    hpad[0:rows, :] = hb_ref[...]
    hpad[rows:, :] = h_ref[...]
    upad[0:lag, :] = ub_ref[...]
    upad[lag:, :] = u_ref[...].astype(BF).astype(F32)
    s = spad[...]
    ra = ra_ref[...]
    ri = ri_ref[...]
    soft = vec_ref[taps + 3 : taps + 4, :]
    decay, root = decay_terms(ra, soft)
    v = v_ref[...].astype(F32)
    sv = s * v
    grad_log = decay * (s * hpad[0:size, :] - sv * ri * decay / root)
    rated = grad_log * ra
    dap = (-8.0 * soft * rated * (1.0 - ra)).astype(BF)
    dip = (sv * root * ri * (1.0 - ri)).astype(BF)
    gates_ref[:, :width] = dap
    gates_ref[:, width:] = dip
    dv = s * ri * root + lax.dot_general(
        gates_ref[...], gate_ref[...], (((1,), (1,)), ((), ())), preferred_element_type=F32
    )
    pad[0:size, :] = dv

    def fold(value):
        return jnp.sum(value.reshape(size // rows, rows, width), axis=0)

    terms = [dap.astype(F32), dip.astype(F32), rated, dv]
    terms = terms + [dv * upad[lag - rows * k : lag - rows * k + size, :] for k in range(taps)]
    for i, term in enumerate(terms):
        sums_ref[i * rows : (i + 1) * rows, :] += fold(term)
    du = vec_ref[0:1, :] * dv
    for k in range(1, taps):
        du = du + vec_ref[k : k + 1, :] * pad[rows * k : rows * k + size, :]
    du_ref[...] = du.astype(BF)

    @pl.when(step == 0)
    def _():
        last_ref[...] = du[size - lag :, :]

    for t in range(taps - 1):
        row = jnp.zeros((rows, width), F32)
        for k in range(taps - 1 - t, taps):
            at = (t + k - (taps - 1)) * rows
            row = row + vec_ref[k : k + 1, :] * pad[at : at + rows, :]
        edge_ref[t * rows : (t + 1) * rows, :] = row


def gate_matrix_kernel(blocks_ref, out_ref):
    kinds, heads, span, _ = blocks_ref.shape
    out_ref[...] = jnp.zeros(out_ref.shape, BF)
    for g in range(kinds):
        for h in range(heads):
            at = (g * heads + h) * span
            out_ref[h * span : (h + 1) * span, at : at + span] = blocks_ref[g, h]


def gate_matrix(blocks):
    kinds, heads, span, _ = blocks.shape
    return pl.pallas_call(
        gate_matrix_kernel,
        out_shape=jax.ShapeDtypeStruct((heads * span, kinds * heads * span), BF),
        name="gate_matrix",
    )(blocks)


def gates_call(ci, uy, edge, gate, vec, rows):
    steps, size, wide = uy.shape
    width = wide // 2
    lag = edge.shape[0]
    here = pl.BlockSpec((None, size, width), lambda j, c: (j, 0, 0))
    whole = lambda shape: pl.BlockSpec(shape, lambda j, c: (0,) * len(shape))
    full = jax.ShapeDtypeStruct((steps, size, width), F32)
    return pl.pallas_call(
        gates_kernel,
        out_shape=(
            jax.ShapeDtypeStruct((steps, size, width), BF),
            full,
            full,
            full,
            full,
            jax.ShapeDtypeStruct((steps, lag, width), F32),
            jax.ShapeDtypeStruct((2 * rows, width), F32),
        ),
        grid_spec=pltpu.PrefetchScalarGridSpec(
            num_scalar_prefetch=1,
            grid=(steps,),
            in_specs=[
                pl.BlockSpec((None, size, width), lambda j, c: (j ^ c[0], 0, 0)),
                whole(edge.shape),
                whole(gate.shape),
                whole(vec.shape),
            ],
            out_specs=[
                here,
                here,
                here,
                here,
                here,
                pl.BlockSpec((None, lag, width), lambda j, c: (j, 0, 0)),
                whole((2 * rows, width)),
            ],
            scratch_shapes=[
                pltpu.VMEM((size + lag, width), F32),
                pltpu.VMEM((2 * rows, width), F32),
            ],
        ),
        name="gates",
    )(ci, uy, edge, gate, vec)


def states_call(ci, a, e, uy, enter):
    steps, size, width = a.shape
    rows = enter.shape[0]
    here = pl.BlockSpec((None, size, width), lambda j, c: (j, 0, 0))
    whole = pl.BlockSpec((rows, width), lambda j, c: (0, 0))
    return pl.pallas_call(
        states_kernel,
        out_shape=(
            jax.ShapeDtypeStruct((steps, size, width), F32),
            jax.ShapeDtypeStruct((steps, size, width), BF),
            jax.ShapeDtypeStruct((steps, rows, width), F32),
            jax.ShapeDtypeStruct((rows, width), F32),
        ),
        grid_spec=pltpu.PrefetchScalarGridSpec(
            num_scalar_prefetch=1,
            grid=(steps,),
            in_specs=[
                here,
                here,
                pl.BlockSpec((None, size, width), lambda j, c: (j ^ c[0], 0, 1)),
                whole,
            ],
            out_specs=[
                here,
                pl.BlockSpec((None, size, width), lambda j, c: (j ^ c[0], 0, 0)),
                pl.BlockSpec((None, rows, width), lambda j, c: (j, 0, 0)),
                whole,
            ],
            scratch_shapes=[pltpu.VMEM((rows, width), F32)],
        ),
        name="states",
    )(ci, a, e, uy, enter)


def back_call(ci, dz, uy, h, a, rows):
    steps, size, width = a.shape
    last = steps - 1
    here = pl.BlockSpec((None, size, width), lambda j, c: (last - j, 0, 0))
    there = pl.BlockSpec((None, size, width), lambda j, c: ((last - j) ^ c[0], 0, 0))
    return pl.pallas_call(
        back_kernel,
        out_shape=(
            jax.ShapeDtypeStruct((steps, size, width), F32),
            jax.ShapeDtypeStruct((steps, size, width), BF),
            jax.ShapeDtypeStruct((rows, width), F32),
        ),
        grid_spec=pltpu.PrefetchScalarGridSpec(
            num_scalar_prefetch=1,
            grid=(steps,),
            in_specs=[
                there,
                pl.BlockSpec((None, size, width), lambda j, c: ((last - j) ^ c[0], 0, 1)),
                here,
                here,
            ],
            out_specs=[here, there, pl.BlockSpec((rows, width), lambda j, c: (0, 0))],
            scratch_shapes=[pltpu.VMEM((rows, width), F32)],
        ),
        name="back",
    )(ci, dz, uy, h, a)


def grads_call(ci, dh, a, ra, ri, v, h, h_before, uy, u_before, gate, vec, late):
    steps, size, width = a.shape
    rows = late.shape[0]
    lag = u_before.shape[1]
    last = steps - 1
    count = lag // rows + 5
    here = pl.BlockSpec((None, size, width), lambda j, c: (last - j, 0, 0))
    there = pl.BlockSpec((None, size, width), lambda j, c: ((last - j) ^ c[0], 0, 0))
    small = lambda size: pl.BlockSpec((None, size, width), lambda j, c: (last - j, 0, 0))
    whole = lambda shape: pl.BlockSpec(shape, lambda j, c: (0,) * len(shape))
    return pl.pallas_call(
        grads_kernel,
        out_shape=(
            jax.ShapeDtypeStruct((steps, size, 2 * width), BF),
            jax.ShapeDtypeStruct((steps, size, width), BF),
            jax.ShapeDtypeStruct((lag, width), F32),
            jax.ShapeDtypeStruct((lag, width), F32),
            jax.ShapeDtypeStruct((count * rows, width), F32),
            jax.ShapeDtypeStruct((rows, width), F32),
        ),
        grid_spec=pltpu.PrefetchScalarGridSpec(
            num_scalar_prefetch=1,
            grid=(steps,),
            in_specs=[
                here,
                here,
                here,
                here,
                here,
                here,
                small(rows),
                there,
                small(lag),
                whole(gate.shape),
                whole(vec.shape),
                whole(late.shape),
            ],
            out_specs=[
                pl.BlockSpec((None, size, 2 * width), lambda j, c: (last - j, 0, 0)),
                there,
                whole((lag, width)),
                whole((lag, width)),
                whole((count * rows, width)),
                whole((rows, width)),
            ],
            scratch_shapes=[
                pltpu.VMEM((rows, width), F32),
                pltpu.VMEM((size + lag, width), F32),
                pltpu.VMEM((size, width), F32),
                pltpu.VMEM((size + rows, width), F32),
                pltpu.VMEM((size + lag, width), F32),
            ],
        ),
        name="grads",
    )(ci, dh, a, ra, ri, v, h, h_before, uy, u_before, gate, vec, late)


def norm_back(grad_norm, normed, inv_root, gain):
    scaled = grad_norm * gain
    mean_term = jnp.mean(scaled * normed, axis=-1, keepdims=True)
    return inv_root * (scaled - normed * mean_term)


def inverse_rms(value):
    return lax.rsqrt(jnp.mean(value * value, axis=-1, keepdims=True) + 1e-06)


def shards(
    tokens,
    norm_gain,
    mlp_gain,
    recur_proj,
    branch_proj,
    out_proj,
    gate_proj,
    up_proj,
    down_proj,
    recur_gate,
    input_gate,
    recur_bias,
    input_bias,
    decay_param,
    conv_bias,
    conv_weight,
    init_state,
    init_tail,
    reset_flags,
    cotangent,
):
    nsx, nsc, nco = (lax.axis_size(name) for name in BLOCKS)
    nseq = nsx * nsc
    co = lax.axis_index("co")
    first = lax.axis_index(BLOCKS) == 0
    ci = lax.axis_index(PEERS)
    order = ci.astype(jnp.int32).reshape(1)
    rows, share, model = tokens.shape
    own = rows * share
    taps = conv_weight.shape[0]
    lag = taps - 1
    part = conv_bias.shape[0]
    chunk = part * nseq
    width = chunk * nco
    keep = (1 - reset_flags).astype(F32)[:, None]

    def owned(value):
        return feature_order(jnp.swapaxes(value, 0, 1).reshape(own, model))

    vectors = jnp.concatenate(
        [
            conv_weight,
            conv_bias[None],
            recur_bias[None],
            input_bias[None],
            decay_param[None],
            init_state,
            jnp.swapaxes(init_tail, 0, 1).reshape(lag * rows, part),
        ],
        axis=0,
    )
    heads, span = recur_gate.shape[0], recur_gate.shape[2]
    both = jnp.stack([recur_gate, input_gate]).reshape(-1, span)
    gains = jnp.stack([norm_gain, mlp_gain])
    unit = norm_gain.shape[0]

    def gather_small(value):
        items = around(value, "co")
        mark = items[-1]
        items = [other for item in items for other in around(item, "sx")]
        return [other for item in items for other in around(item, "sc")], mark

    gains, mark_gains = gather_small(gains)
    vectors, mark_vectors = gather_small(vectors)
    both, mark_both = gather_small(both)

    def owned(value):
        return feature_order(jnp.swapaxes(value, 0, 1).reshape(own, model))

    mine = owned(tokens)
    group = collect(mine)
    in_shard = after(
        jnp.concatenate([recur_proj, branch_proj], axis=1), mark_gains, mark_vectors, mark_both
    )
    in_chunks = around(in_shard, "co")
    in_rows = around(join_columns(in_chunks, 2), "sx")
    full_in = jnp.concatenate(in_rows + [shift(item, "sc", 1) for item in in_rows], axis=0)
    out_chunks = around(after(out_proj, in_chunks[-1]), "co")
    out_columns = around(after(jnp.concatenate(out_chunks, axis=0), in_rows[-1]), "sx")
    full_out = jnp.concatenate(
        out_columns + [shift(item, "sc", 1) for item in out_columns], axis=1
    )
    grad_mine = owned(cotangent)
    grad_group = collect(after(grad_mine, *group[1:]))
    grad_full = jnp.concatenate(grad_group, axis=0)

    gains = jnp.stack(gains).reshape(-1, 2 * unit)
    gains = jnp.concatenate(collect(gains), axis=0)
    place = jnp.arange(model // unit)
    rel = place // (model // unit // nseq)
    sx, sc = lax.axis_index("sx"), lax.axis_index("sc")
    here_seq = ((sx - rel % nsx) % nsx) * nsc + (sc - rel // nsx) % nsc
    whole_unit = here_seq * (model // unit // nseq) + place % (model // unit // nseq)
    from_chan, from_seq = whole_unit // nseq, whole_unit % nseq
    source = (from_chan % PEER) ^ ci
    source = source * nco + (co - from_chan // PEER) % nco
    source = source * nsx + (sx - from_seq // nsc) % nsx
    source = source * nsc + (sc - from_seq % nsc) % nsc
    pick = (source[:, None] == jnp.arange(model // unit)[None, :]).astype(F32)
    gains = jnp.dot(pick, gains.astype(F32), precision=lax.Precision.HIGHEST)
    gain_one = gains[:, :unit].reshape(1, model)
    gain_two = gains[:, unit:].reshape(1, model)

    def blocks_in_order(items):
        table = jnp.stack(items).reshape(nco, nsx, nsc, *items[0].shape)
        table = jnp.moveaxis(table, 0, 2).reshape(nseq, nco, *items[0].shape)
        return jnp.concatenate(
            [
                lax.dynamic_slice_in_dim(
                    table, ((sx - s // nsc) % nsx) * nsc + (sc - s % nsc) % nsc, 1, 0
                )
                for s in range(nseq)
            ],
            axis=0,
        )

    vectors = jnp.transpose(blocks_in_order(vectors), (2, 1, 0, 3)).reshape(-1, width)
    vectors = vectors.astype(F32)
    decay32 = vectors[taps + 3 : taps + 4]
    vec = jnp.concatenate([vectors[: taps + 3], jax.nn.softplus(-decay32)], axis=0)
    vec = jnp.pad(vec, ((0, -vec.shape[0] % 8), (0, 0)))
    state_start = vectors[taps + 4 : taps + 4 + rows] * keep
    tail_start = vectors[taps + 4 + rows :] * jnp.tile(keep, (lag, 1))
    both = blocks_in_order(both).reshape(nseq, nco, 2, heads, -1, span)
    both = jnp.transpose(both, (2, 1, 3, 0, 4, 5)).reshape(2, nco * heads, span, span)
    gate = gate_matrix(both)

    def normed(piece):
        value = piece.astype(F32)
        return value * inverse_rms(value)

    def normal(piece):
        return (normed(piece) * gain_one).astype(BF)

    normal_in = jnp.concatenate([normal(piece) for piece in group], axis=0)
    final = lax.bitwise_xor(jnp.int32(PEER - 1), ci.astype(jnp.int32))
    tail_at = final * own + own - lag * rows
    ends = matmul(lax.dynamic_slice_in_dim(normal_in, tail_at, lag * rows, 0), full_in)
    ends = ends[:, :width].astype(BF)
    edge = jnp.where(first, tail_start.astype(BF), chunk_roll(block_shift(ends, 1), 1))
    uy = matmul(after(normal_in, ends), full_in).reshape(PEER, own, 2 * width)

    edge_at = (final, own - lag * rows, 0)
    v, ra, ri, decay, drive, u_before, summary = gates_call(order, uy, edge, gate, vec, rows)
    outer = other_blocks(summary, rows, False)
    enter = outer[:rows] * state_start + outer[rows:]

    gate_shard = after(gate_proj, enter)
    gate_chunks = around(gate_shard, "co")
    gate_rows = around(join_columns(gate_chunks, 1), "sx")
    full_gate = jnp.concatenate(gate_rows + [shift(item, "sc", 1) for item in gate_rows], axis=0)
    up_chunks = around(after(up_proj, gate_chunks[-1]), "co")
    up_rows = around(after(join_columns(up_chunks, 1), gate_rows[-1]), "sx")
    full_up = jnp.concatenate(up_rows + [shift(item, "sc", 1) for item in up_rows], axis=0)
    down_chunks = around(after(down_proj, up_chunks[-1]), "co")
    down_columns = around(after(jnp.concatenate(down_chunks, axis=0), up_rows[-1]), "sx")
    full_down = jnp.concatenate(
        down_columns + [shift(item, "sc", 1) for item in down_columns], axis=1
    )
    h, z, h_before, h_end = states_call(order, decay, drive, uy, enter)
    z_low = after(z, grad_full)
    branch = matmul(z_low.reshape(PEER * own, width), full_out).reshape(PEER, own, model)
    resid = mine.astype(F32) + hand_back([branch[k] for k in range(PEER)])

    inv_two = inverse_rms(resid)
    normed_two = resid * inv_two
    normal_mine = (normed_two * gain_two).astype(BF)
    normal_mid = jnp.concatenate(collect(normal_mine), axis=0)
    gate_pre = matmul(normal_mid, full_gate)
    up_pre = matmul(normal_mid, full_up)
    gate_act, gate_slope = gelu_parts(gate_pre)
    hidden = (gate_act * up_pre).astype(BF)
    mlp = matmul(hidden, full_down).astype(BF).reshape(PEER, own, model)

    grad_hidden = times_transpose(grad_full, full_down)
    grad_gate = (grad_hidden * up_pre * gate_slope).astype(BF)
    grad_up = (grad_hidden * gate_act).astype(BF)
    mid = times_transpose(grad_gate, full_gate) + times_transpose(grad_up, full_up)
    mid = mid.reshape(PEER, own, model)
    mid_sum = hand_back([mid[k] for k in range(PEER)])
    gain_two_part = jnp.sum(mid_sum * normed_two, axis=0, keepdims=True)
    resid_grad = grad_mine.astype(F32) + norm_back(mid_sum, normed_two, inv_two, gain_two)
    resid_group = collect(resid_grad.astype(BF))
    resid_low = jnp.concatenate(resid_group, axis=0)
    down_grad = over_cores(over_tokens(hidden, grad_full).astype(BF), 1)
    gate_grad = over_cores(over_tokens(normal_mid, grad_gate).astype(BF), 0)
    up_grad = over_cores(over_tokens(normal_mid, grad_up).astype(BF), 0)
    down_grad = over_chips(down_grad, 1)

    resid_low = after(resid_low, down_grad, gate_grad, up_grad)
    dz = times_transpose(resid_low, full_out).reshape(PEER, own, width)
    dh, grad_branch, local_end = back_call(order, dz, uy, h, decay, rows)
    mlp_low, local_end = lax.optimization_barrier((mlp, local_end))
    mlp_sum = hand_back([mlp_low[k].astype(F32) for k in range(PEER)])
    mixed = (resid + mlp_sum).astype(BF)
    late = other_blocks(jnp.concatenate([summary[:rows], local_end], axis=0), rows, True)[rows:]
    gate_grad = over_chips(after(gate_grad, late), 0)
    down_grad = over_chunks(after(down_grad, late), 0)
    gates_low, grad_u, edge_out, last, sums, start_grad = grads_call(
        order, dh, decay, ra, ri, v, h, h_before, uy, u_before, gate, vec, late
    )
    edge_in = chunk_roll(block_shift(edge_out, -1), -1)
    grad_u = lax.dynamic_update_slice(grad_u, (last + edge_in).astype(BF)[None], edge_at)
    grad_u = grad_u.reshape(PEER * own, width)
    grad_branch = grad_branch.reshape(PEER * own, width)
    out_grad = over_tokens(z.reshape(PEER * own, width), resid_low).astype(BF)
    out_grad = over_cores(out_grad, 1)
    branch_grad = over_cores(over_tokens(normal_in, grad_branch).astype(BF), 0)
    both_grad = over_tokens(v.reshape(PEER * own, width), gates_low.reshape(PEER * own, 2 * width))
    back_terms = times_transpose(grad_u, full_in[:, :width]) + times_transpose(
        grad_branch, full_in[:, width:]
    )
    back_terms = back_terms.reshape(PEER, own, model)
    back_low = back_terms[1:].astype(BF)
    gain_one_part = sum(
        jnp.sum(back_terms[k] * normed(group[k]), axis=0, keepdims=True) for k in range(PEER)
    )
    back_sum = back_terms[0]
    for k in range(1, PEER):
        back_sum = back_sum + peer(back_low[k - 1], k).astype(F32)
    recur_grad = over_cores(over_tokens(normal_in, grad_u).astype(BF), 0)
    value = mine.astype(F32)
    inv_one = inverse_rms(value)
    tokens_grad = resid_grad + norm_back(back_sum, value * inv_one, inv_one, gain_one)

    up_grad = over_chips(after(up_grad, gate_grad), 0)
    gate_out = over_chunks(after(gate_grad, down_grad), 1)
    out_grad = over_chips(after(out_grad, up_grad), 1)
    up_out = over_chunks(after(up_grad, gate_out), 1)
    branch_grad = over_chips(after(branch_grad, out_grad), 0)
    out_out = over_chunks(after(out_grad, up_out), 0)
    recur_grad = over_chips(after(recur_grad, branch_grad), 0)
    branch_out = over_chunks(after(branch_grad, out_out), 1)
    recur_out = over_chunks(after(recur_grad, branch_out), 1)
    down_out = down_grad

    def blocks_apart(value):
        return jnp.concatenate(
            [
                lax.dynamic_slice_in_dim(
                    value, ((sx - rx) % nsx) * nsc + (sc - rc) % nsc, 1, 0
                )
                for rc in range(nsc)
                for rx in range(nsx)
            ],
            axis=0,
        )

    def scatter_small(value):
        value = blocks_apart(value).astype(BF)
        return over_chunks(over_chips(over_cores(value, 0), 0)[0], 0)[0]

    pieces = jnp.stack(
        [
            both_grad[span * h : span * (h + 1), g * width + span * h : g * width + span * (h + 1)]
            for g in range(2)
            for h in range(nco * heads)
        ]
    )
    pieces = pieces.reshape(2, nco, heads, nseq, -1, span)
    pieces = jnp.transpose(pieces, (3, 1, 0, 2, 4, 5)).reshape(nseq, nco, -1, span)
    both_out = scatter_small(pieces).reshape(2, heads, -1, span)

    sums = jnp.sum(sums.reshape(-1, rows, width), axis=1)
    small = jnp.concatenate(
        [
            sums[0:2],
            sums[2:3] * 8.0 * jax.nn.sigmoid(-decay32),
            sums[3:],
            jnp.where(first, keep * start_grad, 0.0),
            jnp.where(first, jnp.tile(keep, (lag, 1)) * edge_out, 0.0),
        ],
        axis=0,
    )
    small = jnp.transpose(small.reshape(-1, nco, nseq, part), (2, 1, 0, 3))
    small = scatter_small(small)

    total = feature_restore(jnp.concatenate([gain_one_part, gain_two_part], axis=0))
    for axis in ("sc", "sx", "co"):
        total = sum(around(total, axis)[1:], total)
    total = sum(collect(total)[1:], total)
    place = (lax.axis_index(("co", "ca", "cb")) * nseq + sx * nsc + sc) * unit
    gain_out = lax.dynamic_slice_in_dim(total, place, unit, 1)

    finish = jnp.concatenate([h_end, ends.astype(F32)], axis=0)
    reach = jnp.where(co == nco - 1, finish[:, :chunk], 0.0)
    for k in range(1, nco):
        piece = finish[:, (nco - k) * chunk : (nco - k + 1) * chunk]
        reach = reach + lax.ppermute(piece, "co", [(nco - 1, k - 1)])
    group_states = reach[:rows][None]
    group_tails = jnp.swapaxes(reach[rows:].reshape(lag, rows, chunk), 0, 1).astype(BF)[None]

    def returned(value):
        return jnp.swapaxes(feature_restore(value).reshape(share, rows, model), 0, 1)

    return (
        returned(mixed),
        returned(tokens_grad),
        gain_out[0],
        gain_out[1],
        recur_out,
        branch_out,
        out_out,
        gate_out,
        up_out,
        down_out,
        both_out[0],
        both_out[1],
        small[0],
        small[1],
        small[2],
        small[3],
        small[4 : 4 + taps],
        small[4 + taps : 4 + taps + rows],
        jnp.swapaxes(small[4 + taps + rows :].reshape(lag, rows, part), 0, 1),
        group_states,
        group_tails,
    )


def solution(mesh):
    nseq, nchan = mesh.devices.shape
    fine = Mesh(
        mesh.devices.reshape(nseq // 2, 2, nchan // PEER, 2, 2), ("sx", "sc", "co", "ca", "cb")
    )
    seq = ("sx", "sc")
    chan = ("co", "ca", "cb")
    place = P(None, seq + chan, None)
    vector = P(chan + seq)
    in_specs = (
        place,
        vector,
        vector,
        P(seq, chan),
        P(seq, chan),
        P(chan, seq),
        P(seq, chan),
        P(seq, chan),
        P(chan, seq),
        P(chan, seq, None),
        P(chan, seq, None),
        vector,
        vector,
        vector,
        vector,
        P(None, chan + seq),
        P(None, chan + seq),
        P(None, None, chan + seq),
        P(),
        place,
    )
    out_specs = (
        place,
        place,
        vector,
        vector,
        P(seq, chan),
        P(seq, chan),
        P(chan, seq),
        P(seq, chan),
        P(seq, chan),
        P(chan, seq),
        P(chan, seq, None),
        P(chan, seq, None),
        vector,
        vector,
        vector,
        vector,
        P(None, chan + seq),
        P(None, chan + seq),
        P(None, None, chan + seq),
        P(seq, None, chan),
        P(seq, None, None, chan),
    )
    return jax.shard_map(shards, mesh=fine, in_specs=in_specs, out_specs=out_specs, check_vma=False)
```

```python
import functools

import jax
import jax.numpy as jnp
from jax import lax
from jax.experimental import pallas as pl
from jax.experimental.pallas import tpu as pltpu
from jax.sharding import Mesh
from jax.sharding import PartitionSpec as P

BF = jnp.bfloat16
F32 = jnp.float32
BLOCKS = ("sx", "sc", "co")
PEERS = ("ca", "cb")
PEER = 4
GELU_C = 0.7978845608028654
GELU_K = 0.044715


def shift(value, axis, step):
    count = lax.axis_size(axis)
    return lax.ppermute(value, axis, [(i, (i + step) % count) for i in range(count)])


def block_shift(value, step):
    count = lax.axis_size(BLOCKS)
    route = [(i, i + step) for i in range(count) if 0 <= i + step < count]
    return lax.ppermute(value, BLOCKS, route)


def peer(value, step):
    return lax.ppermute(value, PEERS, [(i, i ^ step) for i in range(PEER)])


def before_last(value):
    count = lax.axis_size(BLOCKS)
    return sum(
        lax.ppermute(
            value,
            BLOCKS + PEERS,
            [((b - 1) * PEER + PEER - 1, b * PEER + k) for b in range(1, count)],
        )
        for k in range(PEER)
    )


def peer_rows(value, hold=()):
    near = peer(value, 1)
    far = peer(after(value, *hold), 2)
    return [value, near, far, peer(after(far, near), 1)]


def peer_sum(terms, hold=()):
    mine, near, far, across = terms
    across = peer(across, 1)
    near = peer(after(near, across), 1)
    relay = (far.astype(F32) + across.astype(F32)).astype(BF)
    far = peer(after(relay, *hold), 2)
    return mine.astype(F32) + near.astype(F32) + far.astype(F32)


def after(value, *done):
    return lax.optimization_barrier((value, *done))[0]


def around(value, axis):
    return [value] + [shift(value, axis, r) for r in range(1, lax.axis_size(axis))]


def over_die(items):
    return items + [shift(item, "sc", r) for r in range(1, lax.axis_size("sc")) for item in items]


def cut(value, count, axis):
    size = value.shape[axis] // count
    return [lax.slice_in_dim(value, r * size, (r + 1) * size, axis=axis) for r in range(count)]


def around_back(parts, axis):
    return parts[:1] + [shift(part, axis, -1 - r) for r, part in enumerate(parts[1:])]


def sum_around(parts, axis, hold=()):
    total = parts[0].astype(F32)
    for r in range(1, len(parts)):
        term = shift(parts[r].astype(BF), axis, -r)
        total = total + after(term, *hold).astype(F32)
    return total


def chunk_roll(value, step):
    count = lax.axis_size("co")
    step = step % count
    if step == 0:
        return value
    width = value.shape[-1] // count
    cut = width * (count - step)
    return jnp.concatenate([value[..., cut:], value[..., :cut]], axis=-1)


def feature_order(value):
    nsx, nsc = lax.axis_size("sx"), lax.axis_size("sc")
    sx, sc = lax.axis_index("sx"), lax.axis_index("sc")
    width = value.shape[-1] // (nsx * nsc)
    parts = []
    for rc in range(nsc):
        for rx in range(nsx):
            owner = lax.rem(sx - rx + nsx, nsx) * nsc + lax.rem(sc - rc + nsc, nsc)
            parts.append(lax.dynamic_slice_in_dim(value, owner * width, width, value.ndim - 1))
    return jnp.concatenate(parts, axis=-1)


def feature_restore(value):
    nsx, nsc = lax.axis_size("sx"), lax.axis_size("sc")
    sx, sc = lax.axis_index("sx"), lax.axis_index("sc")
    width = value.shape[-1] // (nsx * nsc)
    parts = []
    for owner in range(nsx * nsc):
        rx = lax.rem(sx - owner // nsc + nsx, nsx)
        rc = lax.rem(sc - owner % nsc + nsc, nsc)
        parts.append(
            lax.dynamic_slice_in_dim(value, (rc * nsx + rx) * width, width, value.ndim - 1)
        )
    return jnp.concatenate(parts, axis=-1)


def join_kernel(groups, *refs):
    out = refs[-1]
    width = refs[0].shape[1] // groups
    at = 0
    for g in range(groups):
        for ref in refs[:-1]:
            out[:, at : at + width] = ref[:, g * width : (g + 1) * width]
            at += width


def join_columns(items, groups):
    rows, width = items[0].shape
    block = rows // 2
    return pl.pallas_call(
        functools.partial(join_kernel, groups),
        out_shape=jax.ShapeDtypeStruct((rows, width * len(items)), items[0].dtype),
        grid=(2,),
        in_specs=[pl.BlockSpec((block, width), lambda i: (i, 0))] * len(items),
        out_specs=pl.BlockSpec((block, width * len(items)), lambda i: (i, 0)),
        name="join",
    )(*items)


def compose(earlier, later, rows):
    decay, state = later[:rows], later[rows:]
    return jnp.concatenate([earlier[:rows] * decay, decay * earlier[rows:] + state], axis=0)


def other_blocks(summary, rows, backward):
    width = summary.shape[-1]
    empty = jnp.concatenate([jnp.ones((rows, width), F32), jnp.zeros((rows, width), F32)], axis=0)
    outer = empty
    for axis in ("co", "sc", "sx"):
        count, mine = lax.axis_size(axis), lax.axis_index(axis)
        items = around(summary, axis)
        if axis == "co":
            items = [chunk_roll(item, r) for r, item in enumerate(items)]
        if count == 2:
            mate = items[1]
            ahead = (mine == 0) if backward else (mine == 1)
            joined = compose(mate, summary, rows)
            outer = jnp.where(ahead, compose(mate, outer, rows), outer)
            summary = jnp.where(ahead, joined, compose(summary, mate, rows))
        else:
            table = jnp.stack(items)
            total, inner = empty, empty
            for place in reversed(range(count)) if backward else range(count):
                item = table[lax.rem(mine - place + count, count)]
                total = compose(total, item, rows)
                ahead = (place > mine) if backward else (place < mine)
                inner = jnp.where(ahead, compose(inner, item, rows), inner)
            outer = compose(inner, outer, rows)
            summary = total
    return outer


def matmul(left, right):
    return jnp.dot(left, right, preferred_element_type=F32)


def over_tokens(left, right):
    return lax.dot_general(left, right, (((0,), (0,)), ((), ())), preferred_element_type=F32)


def times_transpose(left, right):
    return lax.dot_general(left, right, (((1,), (1,)), ((), ())), preferred_element_type=F32)


def weight_grad(left, right, halved):
    if halved == 0:
        halves = [over_tokens(half, right).astype(BF) for half in cut(left, 2, 1)]
    else:
        halves = [over_tokens(left, half).astype(BF) for half in cut(right, 2, 1)]
    return [lax.optimization_barrier(half) for half in halves]


def gelu_parts(value):
    square = value * value
    wave = jnp.tanh(GELU_C * (value + GELU_K * value * square))
    half = 0.5 * (1.0 + wave)
    slope = half + 0.5 * value * (1.0 - wave * wave) * (GELU_C * (1.0 + 3.0 * GELU_K * square))
    return value * half, slope


def minus_expm1(value):
    series = 1.0 + value * (1.0 / 7.0)
    for order in (6.0, 5.0, 4.0, 3.0, 2.0):
        series = 1.0 + value * (1.0 / order) * series
    return -jnp.where(value > -0.3, value * series, jnp.exp(value) - 1.0)


def decay_terms(rate, soft):
    log_decay = -8.0 * rate * soft
    return jnp.exp(log_decay), jnp.sqrt(minus_expm1(2.0 * log_decay))


def rows_times(values, pieces, columns=slice(None)):
    total = None
    size = pieces[0].shape[0]
    for i, piece in enumerate(pieces):
        term = matmul(values[:, i * size : (i + 1) * size], piece[:, columns])
        total = term if total is None else total + term
    return total


def columns_times(values, pieces):
    total = None
    size = pieces[0].shape[1]
    for i, piece in enumerate(pieces):
        term = times_transpose(values[:, i * size : (i + 1) * size], piece[...])
        total = term if total is None else total + term
    return total


def gates_kernel(
    count, here, x_ref, border_ref, gain_ref, tail_ref, gate_ref, vec_ref, *refs
):
    pieces, refs = refs[:count], refs[count:]
    n_ref, u_ref, v_ref, ra_ref, ri_ref, a_ref, e_ref, before_ref, end_ref, pad, held = refs
    step = pl.program_id(0)
    rows = held.shape[0] // 2
    size, width = u_ref.shape
    lag = tail_ref.shape[0]

    def normal(value):
        value = value.astype(F32)
        root = lax.rsqrt(jnp.mean(value * value, axis=-1, keepdims=True) + 1e-06)
        return (value * root * gain_ref[...]).astype(BF)

    @pl.when(step == 0)
    def _():
        edge = rows_times(normal(border_ref[...]), pieces).astype(BF).astype(F32)
        pad[0:lag, :] = jnp.where(here[1] == 1, tail_ref[...].astype(BF).astype(F32), edge)
        held[0:rows, :] = jnp.ones((rows, width), F32)
        held[rows:, :] = jnp.zeros((rows, width), F32)

    @pl.when(step > 0)
    def _():
        pad[0:lag, :] = pad[size : size + lag, :]

    low = normal(x_ref[...])
    n_ref[...] = low
    conv_in = rows_times(low, pieces).astype(BF)
    u_ref[...] = conv_in
    pad[lag:, :] = conv_in.astype(F32)
    before_ref[...] = pad[0:lag, :]
    taps = lag // rows + 1
    conv = vec_ref[taps : taps + 1, :] + vec_ref[0:1, :] * pad[lag : lag + size, :]
    for k in range(1, taps):
        conv = conv + vec_ref[k : k + 1, :] * pad[lag - rows * k : lag - rows * k + size, :]
    low = conv.astype(BF)
    v_ref[...] = low
    pre = jnp.dot(low, gate_ref[...], preferred_element_type=F32)
    ra = jax.nn.sigmoid(pre[:, :width] + vec_ref[taps + 1 : taps + 2, :])
    ri = jax.nn.sigmoid(pre[:, width:] + vec_ref[taps + 2 : taps + 3, :])
    decay, root = decay_terms(ra, vec_ref[taps + 3 : taps + 4, :])
    ra_ref[...] = ra
    ri_ref[...] = ri
    a_ref[...] = decay
    e_ref[...] = low.astype(F32) * ri * root
    prod = held[0:rows, :]
    state = held[rows:, :]
    for t in range(size // rows):
        now = a_ref[t * rows : (t + 1) * rows, :]
        state = now * state + e_ref[t * rows : (t + 1) * rows, :]
        prod = prod * now
    held[0:rows, :] = prod
    held[rows:, :] = state
    end_ref[0:rows, :] = prod
    end_ref[rows:, :] = state


def branch_kernel(count, n_ref, *refs):
    refs[count][...] = rows_times(n_ref[...], refs[:count])


def states_kernel(place, a_ref, e_ref, yp_ref, enter_ref, h_ref, z_ref, before_ref, end_ref, held):
    step = pl.program_id(0)
    rows = held.shape[0]

    @pl.when(step == 0)
    def _():
        held[...] = enter_ref[...]

    state = held[...]
    before_ref[...] = state
    for t in range(a_ref.shape[0] // rows):
        at = slice(t * rows, (t + 1) * rows)
        state = a_ref[at, :] * state + e_ref[at, :]
        h_ref[at, :] = state
    held[...] = state
    end_ref[...] = state
    act, _ = gelu_parts(yp_ref[...])
    z_ref[...] = (h_ref[...] * act).astype(BF)


def back_kernel(count, place, g_ref, yp_ref, h_ref, a_ref, *refs):
    pieces = refs[:count]
    dh_ref, dyp_ref, end_ref, held = refs[count:]
    step = pl.program_id(0)
    rows = held.shape[0]

    @pl.when(step == 0)
    def _():
        held[...] = jnp.zeros(held.shape, F32)

    act, slope = gelu_parts(yp_ref[...])
    dz = columns_times(g_ref[...], pieces)
    dh_ref[...] = dz * act
    dyp_ref[...] = (dz * h_ref[...] * slope).astype(BF)
    carry = held[...]
    for t in reversed(range(a_ref.shape[0] // rows)):
        at = slice(t * rows, (t + 1) * rows)
        carry = a_ref[at, :] * (dh_ref[at, :] + carry)
    held[...] = carry
    end_ref[...] = carry


def mlp_kernel(count, n_ref, dy_ref, *refs):
    gates, ups, downs = refs[:count], refs[count : 2 * count], refs[2 * count : 3 * count]
    m_ref, dg_ref, du_ref = refs[3 * count :]
    gate = rows_times(n_ref[...], gates)
    up = rows_times(n_ref[...], ups)
    grad = columns_times(dy_ref[...], downs)
    act, slope = gelu_parts(gate)
    m_ref[...] = (act * up).astype(BF)
    dg_ref[...] = (grad * up * slope).astype(BF)
    du_ref[...] = (grad * act).astype(BF)


def product_kernel(count, per, x_ref, *refs):
    out_ref = refs[count]
    step = pl.program_id(0)
    for i in range(count):

        @pl.when(step // per == i)
        def _():
            out_ref[...] = matmul(x_ref[...], refs[i][...]).astype(BF)


def transposed_kernel(count, per, x_ref, y_ref, *refs):
    out_ref = refs[2 * count]
    step = pl.program_id(0)
    for i in range(count):

        @pl.when(step // per == i)
        def _():
            out_ref[...] = (
                times_transpose(x_ref[...], refs[i][...])
                + times_transpose(y_ref[...], refs[count + i][...])
            ).astype(BF)


def grads_kernel(
    place, dh_ref, a_ref, ra_ref, ri_ref, v_ref, h_ref, hb_ref, u_ref, ub_ref, gate_ref, vec_ref,
    late_ref, gates_ref, du_ref, edge_ref, last_ref, sums_ref, end_ref, held, pad, spad, hpad, upad,
):
    step = pl.program_id(0)
    rows = held.shape[0]
    size = dh_ref.shape[0]
    width = dh_ref.shape[1]
    lag = ub_ref.shape[0]
    taps = lag // rows + 1

    @pl.when(step == 0)
    def _():
        held[...] = late_ref[...]
        pad[size:, :] = jnp.zeros((lag, width), F32)
        sums_ref[...] = jnp.zeros(sums_ref.shape, F32)

    @pl.when(step > 0)
    def _():
        pad[size:, :] = pad[0:lag, :]

    carry = held[...]
    for t in reversed(range(size // rows)):
        at = slice(t * rows, (t + 1) * rows)
        now = dh_ref[at, :] + carry
        spad[at, :] = now
        carry = a_ref[at, :] * now
    held[...] = carry
    end_ref[...] = carry
    hpad[0:rows, :] = hb_ref[...]
    hpad[rows:, :] = h_ref[...]
    upad[0:lag, :] = ub_ref[...]
    upad[lag:, :] = u_ref[...].astype(F32)
    s = spad[...]
    ra = ra_ref[...]
    ri = ri_ref[...]
    soft = vec_ref[taps + 3 : taps + 4, :]
    decay, root = decay_terms(ra, soft)
    v = v_ref[...].astype(F32)
    sv = s * v
    grad_log = decay * (s * hpad[0:size, :] - sv * ri * decay / root)
    rated = grad_log * ra
    dap = (-8.0 * soft * rated * (1.0 - ra)).astype(BF)
    dip = (sv * root * ri * (1.0 - ri)).astype(BF)
    gates_ref[:, :width] = dap
    gates_ref[:, width:] = dip
    dv = s * ri * root + lax.dot_general(
        gates_ref[...], gate_ref[...], (((1,), (1,)), ((), ())), preferred_element_type=F32
    )
    pad[0:size, :] = dv

    def fold(value):
        return jnp.sum(value.reshape(size // rows, rows, width), axis=0)

    terms = [dap.astype(F32), dip.astype(F32), rated, dv]
    terms = terms + [dv * upad[lag - rows * k : lag - rows * k + size, :] for k in range(taps)]
    for i, term in enumerate(terms):
        sums_ref[i * rows : (i + 1) * rows, :] += fold(term)
    du = vec_ref[0:1, :] * dv
    for k in range(1, taps):
        du = du + vec_ref[k : k + 1, :] * pad[rows * k : rows * k + size, :]
    du_ref[...] = du.astype(BF)

    @pl.when(step == 0)
    def _():
        last_ref[...] = du[size - lag :, :]

    for t in range(taps - 1):
        row = jnp.zeros((rows, width), F32)
        for k in range(taps - 1 - t, taps):
            at = (t + k - (taps - 1)) * rows
            row = row + vec_ref[k : k + 1, :] * pad[at : at + rows, :]
        edge_ref[t * rows : (t + 1) * rows, :] = row


def gate_matrix_kernel(blocks_ref, out_ref):
    kinds, heads, span, _ = blocks_ref.shape
    out_ref[...] = jnp.zeros(out_ref.shape, BF)
    for g in range(kinds):
        for h in range(heads):
            at = (g * heads + h) * span
            out_ref[h * span : (h + 1) * span, at : at + span] = blocks_ref[g, h]


def gate_matrix(blocks):
    kinds, heads, span, _ = blocks.shape
    return pl.pallas_call(
        gate_matrix_kernel,
        out_shape=jax.ShapeDtypeStruct((heads * span, kinds * heads * span), BF),
        name="gate_matrix",
    )(blocks)


def whole(shape):
    return pl.BlockSpec(shape, lambda *_: (0,) * len(shape))


def gates_call(place, x, border, gain, tail, gate, vec, pieces, rows):
    steps, size, model = x.shape
    lag, width = tail.shape
    wide = pieces[0].shape[0]
    here = pl.BlockSpec((None, size, width), lambda j, c: (j, 0, 0))
    full = jax.ShapeDtypeStruct((steps, size, width), F32)
    low = jax.ShapeDtypeStruct((steps, size, width), BF)
    rowed = pl.BlockSpec((None, size, model), lambda j, c: (j ^ c[0], 0, 0))
    return pl.pallas_call(
        functools.partial(gates_kernel, len(pieces)),
        out_shape=(
            jax.ShapeDtypeStruct(x.shape, BF),
            low,
            low,
            full,
            full,
            full,
            full,
            jax.ShapeDtypeStruct((steps, lag, width), F32),
            jax.ShapeDtypeStruct((2 * rows, width), F32),
        ),
        grid_spec=pltpu.PrefetchScalarGridSpec(
            num_scalar_prefetch=1,
            grid=(steps,),
            in_specs=[
                rowed,
                whole(border.shape),
                whole(gain.shape),
                whole(tail.shape),
                whole(gate.shape),
                whole(vec.shape),
            ]
            + [pl.BlockSpec((wide, width), lambda j, c: (0, 0))] * len(pieces),
            out_specs=[
                rowed,
                here,
                here,
                here,
                here,
                here,
                here,
                pl.BlockSpec((None, lag, width), lambda j, c: (j, 0, 0)),
                whole((2 * rows, width)),
            ],
            scratch_shapes=[
                pltpu.VMEM((size + lag, width), F32),
                pltpu.VMEM((2 * rows, width), F32),
            ],
        ),
        name="gates",
    )(place, x, border, gain, tail, gate, vec, *pieces)


def branch_call(n, pieces):
    steps, size, model = n.shape
    wide, width = pieces[0].shape
    return pl.pallas_call(
        functools.partial(branch_kernel, len(pieces)),
        out_shape=jax.ShapeDtypeStruct((steps, size, width), F32),
        grid=(steps,),
        in_specs=[pl.BlockSpec((None, size, model), lambda j: (j, 0, 0))]
        + [whole((wide, width))] * len(pieces),
        out_specs=pl.BlockSpec((None, size, width), lambda j: (j, 0, 0)),
        name="branch",
    )(n, *pieces)


def states_call(place, a, e, yp, enter):
    steps, size, width = a.shape
    rows = enter.shape[0]
    here = pl.BlockSpec((None, size, width), lambda j, c: (j, 0, 0))
    there = pl.BlockSpec((None, size, width), lambda j, c: (j ^ c[0], 0, 0))
    return pl.pallas_call(
        states_kernel,
        out_shape=(
            jax.ShapeDtypeStruct((steps, size, width), F32),
            jax.ShapeDtypeStruct((steps, size, width), BF),
            jax.ShapeDtypeStruct((steps, rows, width), F32),
            jax.ShapeDtypeStruct((rows, width), F32),
        ),
        grid_spec=pltpu.PrefetchScalarGridSpec(
            num_scalar_prefetch=1,
            grid=(steps,),
            in_specs=[here, here, there, whole((rows, width))],
            out_specs=[
                here,
                there,
                pl.BlockSpec((None, rows, width), lambda j, c: (j, 0, 0)),
                whole((rows, width)),
            ],
            scratch_shapes=[pltpu.VMEM((rows, width), F32)],
        ),
        name="states",
    )(place, a, e, yp, enter)


def back_call(place, g, yp, h, a, pieces, rows):
    steps, size, width = a.shape
    last = steps - 1
    here = pl.BlockSpec((None, size, width), lambda j, c: (last - j, 0, 0))
    there = pl.BlockSpec((None, size, width), lambda j, c: ((last - j) ^ c[0], 0, 0))
    return pl.pallas_call(
        functools.partial(back_kernel, len(pieces)),
        out_shape=(
            jax.ShapeDtypeStruct((steps, size, width), F32),
            jax.ShapeDtypeStruct((steps, size, width), BF),
            jax.ShapeDtypeStruct((rows, width), F32),
        ),
        grid_spec=pltpu.PrefetchScalarGridSpec(
            num_scalar_prefetch=1,
            grid=(steps,),
            in_specs=[
                pl.BlockSpec((None, size, g.shape[2]), lambda j, c: ((last - j) ^ c[0], 0, 0)),
                there,
                here,
                here,
            ]
            + [whole(pieces[0].shape)] * len(pieces),
            out_specs=[here, there, whole((rows, width))],
            scratch_shapes=[pltpu.VMEM((rows, width), F32)],
        ),
        name="back",
    )(place, g, yp, h, a, *pieces)


def grads_call(place, dh, a, ra, ri, v, h, h_before, u, u_before, gate, vec, late):
    steps, size, width = a.shape
    rows = late.shape[0]
    lag = u_before.shape[1]
    last = steps - 1
    count = lag // rows + 5
    here = pl.BlockSpec((None, size, width), lambda j, c: (last - j, 0, 0))
    there = pl.BlockSpec((None, size, width), lambda j, c: ((last - j) ^ c[0], 0, 0))
    small = lambda size: pl.BlockSpec((None, size, width), lambda j, c: (last - j, 0, 0))
    return pl.pallas_call(
        grads_kernel,
        out_shape=(
            jax.ShapeDtypeStruct((steps, size, 2 * width), BF),
            jax.ShapeDtypeStruct((steps, size, width), BF),
            jax.ShapeDtypeStruct((lag, width), F32),
            jax.ShapeDtypeStruct((lag, width), F32),
            jax.ShapeDtypeStruct((count * rows, width), F32),
            jax.ShapeDtypeStruct((rows, width), F32),
        ),
        grid_spec=pltpu.PrefetchScalarGridSpec(
            num_scalar_prefetch=1,
            grid=(steps,),
            in_specs=[
            here,
            here,
            here,
            here,
            here,
            here,
            small(rows),
            here,
            small(lag),
            whole(gate.shape),
            whole(vec.shape),
            whole(late.shape),
        ],
        out_specs=[
            pl.BlockSpec((None, size, 2 * width), lambda j, c: (last - j, 0, 0)),
            there,
            whole((lag, width)),
            whole((lag, width)),
            whole((count * rows, width)),
            whole((rows, width)),
        ],
        scratch_shapes=[
            pltpu.VMEM((rows, width), F32),
            pltpu.VMEM((size + lag, width), F32),
            pltpu.VMEM((size, width), F32),
            pltpu.VMEM((size + rows, width), F32),
            pltpu.VMEM((size + lag, width), F32),
        ],
        ),
        name="grads",
    )(place, dh, a, ra, ri, v, h, h_before, u, u_before, gate, vec, late)


def tile_of(size, most):
    return max(t for t in range(128, most + 1, 128) if size % t == 0)


def mlp_call(n, dy, gates, ups, downs):
    tokens, model = n.shape
    wide, units = gates[0].shape
    tile = tile_of(units, 256)
    count = len(gates)
    out = pl.BlockSpec((tokens, tile), lambda j: (0, j))
    return pl.pallas_call(
        functools.partial(mlp_kernel, count),
        out_shape=[jax.ShapeDtypeStruct((tokens, units), BF)] * 3,
        grid=(units // tile,),
        in_specs=[whole((tokens, model))] * 2
        + [pl.BlockSpec((wide, tile), lambda j: (0, j))] * (2 * count)
        + [pl.BlockSpec((tile, wide), lambda j: (j, 0))] * count,
        out_specs=[out] * 3,
        name="mlp",
    )(n, dy, *gates, *ups, *downs)


def clipped(step, per, i):
    return jnp.clip(step - i * per, 0, per - 1)


def product_call(x, pieces):
    tokens, depth = x.shape
    wide = pieces[0].shape[1]
    tile = tile_of(wide, 512)
    per, count = wide // tile, len(pieces)
    return pl.pallas_call(
        functools.partial(product_kernel, count, per),
        out_shape=jax.ShapeDtypeStruct((tokens, wide * count), BF),
        grid=(per * count,),
        in_specs=[whole(x.shape)]
        + [
            pl.BlockSpec((depth, tile), lambda s, i=i: (0, clipped(s, per, i)))
            for i in range(count)
        ],
        out_specs=pl.BlockSpec((tokens, tile), lambda s: (0, s)),
        name="product",
    )(x, *pieces)


def transposed_call(x, y, first, second):
    tokens, depth = x.shape
    wide = first[0].shape[0]
    tile = tile_of(wide, 256)
    per, count = wide // tile, len(first)
    return pl.pallas_call(
        functools.partial(transposed_kernel, count, per),
        out_shape=jax.ShapeDtypeStruct((tokens, wide * count), BF),
        grid=(per * count,),
        in_specs=[whole(x.shape), whole(y.shape)]
        + [
            pl.BlockSpec((tile, depth), lambda s, i=i: (clipped(s, per, i), 0))
            for i in range(count)
        ]
        * 2,
        out_specs=pl.BlockSpec((tokens, tile), lambda s: (0, s)),
        name="transposed",
    )(x, y, *first, *second)


def norm_back(grad_norm, normed, inv_root, gain):
    scaled = grad_norm * gain
    mean_term = jnp.mean(scaled * normed, axis=-1, keepdims=True)
    return inv_root * (scaled - normed * mean_term)


def inverse_rms(value):
    return lax.rsqrt(jnp.mean(value * value, axis=-1, keepdims=True) + 1e-06)


def shards(
    tokens,
    norm_gain,
    mlp_gain,
    recur_proj,
    branch_proj,
    out_proj,
    gate_proj,
    up_proj,
    down_proj,
    recur_gate,
    input_gate,
    recur_bias,
    input_bias,
    decay_param,
    conv_bias,
    conv_weight,
    init_state,
    init_tail,
    reset_flags,
    cotangent,
):
    nsx, nsc, nco = (lax.axis_size(name) for name in BLOCKS)
    nseq = nsx * nsc
    co = lax.axis_index("co")
    first = lax.axis_index(BLOCKS) == 0
    ci = lax.axis_index(PEERS)
    place = jnp.stack([ci, first]).astype(jnp.int32)
    rows, share, model = tokens.shape
    own = rows * share
    group = PEER * own
    taps = conv_weight.shape[0]
    lag = taps - 1
    part = conv_bias.shape[0]
    chunk = part * nseq
    width = chunk * nco
    keep = (1 - reset_flags).astype(F32)[:, None]
    heads, span = recur_gate.shape[0], recur_gate.shape[2]
    unit = norm_gain.shape[0]
    sx, sc = lax.axis_index("sx"), lax.axis_index("sc")

    def owned(value):
        return feature_order(jnp.swapaxes(value, 0, 1).reshape(own, model))

    mine = owned(tokens)
    border = jnp.swapaxes(tokens[:, share - lag :], 0, 1).reshape(lag * rows, model)
    border = feature_order(before_last(border))

    vectors = jnp.concatenate(
        [
            conv_weight,
            conv_bias[None],
            recur_bias[None],
            input_bias[None],
            decay_param[None],
            init_state,
            jnp.swapaxes(init_tail, 0, 1).reshape(lag * rows, part),
        ],
        axis=0,
    )
    both = jnp.stack([recur_gate, input_gate]).reshape(-1, span)
    lines, lists = both.shape[0], vectors.shape[0]
    gains = jnp.stack([norm_gain, mlp_gain])
    packed = jnp.concatenate(
        [
            both,
            jnp.pad(vectors, ((0, 0), (0, span - part))),
            jnp.pad(
                jnp.concatenate([gains] + [peer(gains, k) for k in range(1, PEER)], axis=0),
                ((0, 0), (0, span - unit)),
            ),
        ],
        axis=0,
    )
    table = around(after(packed, border)[None], "co")
    ready = table[1:]
    table = jnp.concatenate(table, axis=0)
    for axis in ("sx", "sc"):
        table = jnp.concatenate(around(table, axis), axis=0)

    links = {"co": ready, "sx": ready}

    def travel(value, axis):
        items = around(after(value, *links[axis]), axis)
        links[axis] = items[1:]
        return items

    def gather(shard):
        return over_die(travel(join_columns(travel(shard, "co"), 1), "sx"))

    recur_chunks = travel(recur_proj, "co")
    x_group = peer_rows(mine, (border,))
    x_all = jnp.stack(x_group)
    recur_pieces = over_die(travel(join_columns(recur_chunks, 1), "sx"))
    branch_chunks = travel(after(branch_proj, x_group[2]), "co")
    out_chunks = travel(out_proj, "co")
    grad_mine = owned(cotangent)
    grad_near = peer(after(grad_mine, x_group[1]), 1)
    grad_far = peer(after(grad_mine, *out_chunks[1:]), 2)
    grad_group = [grad_mine, grad_near, grad_far, peer(grad_far, 1)]
    grad_full = jnp.concatenate(grad_group, axis=0)

    gains = table[:, lines + lists :, :unit].reshape(-1, PEER, 2 * unit)
    gains = jnp.swapaxes(gains, 0, 1).reshape(-1, 2 * unit)
    lot = jnp.arange(model // unit)
    rel = lot // (model // unit // nseq)
    here_seq = ((sx - rel % nsx) % nsx) * nsc + (sc - rel // nsx) % nsc
    whole_unit = here_seq * (model // unit // nseq) + lot % (model // unit // nseq)
    from_chan, from_seq = whole_unit // nseq, whole_unit % nseq
    source = ((from_chan % PEER) ^ lax.axis_index(PEERS)) * nsc + (sc - from_seq % nsc) % nsc
    source = source * nsx + (sx - from_seq // nsc) % nsx
    source = source * nco + (co - from_chan // PEER) % nco
    pick = (source[:, None] == jnp.arange(model // unit)[None, :]).astype(F32)
    gains = jnp.dot(pick, gains.astype(F32), precision=lax.Precision.HIGHEST)
    gain_one = gains[:, :unit].reshape(1, model)
    gain_two = gains[:, unit:].reshape(1, model)

    table = table[:, : lines + lists].reshape(nseq, nco, lines + lists, span)
    table = jnp.concatenate(
        [
            lax.dynamic_slice_in_dim(
                table, ((sc - s % nsc) % nsc) * nsx + (sx - s // nsc) % nsx, 1, 0
            )
            for s in range(nseq)
        ],
        axis=0,
    )
    vectors = table[:, :, lines:, :part]
    vectors = jnp.transpose(vectors, (2, 1, 0, 3)).reshape(-1, width).astype(F32)
    decay32 = vectors[taps + 3 : taps + 4]
    vec = jnp.concatenate([vectors[: taps + 3], jax.nn.softplus(-decay32)], axis=0)
    vec = jnp.pad(vec, ((0, -vec.shape[0] % 8), (0, 0)))
    state_start = vectors[taps + 4 : taps + 4 + rows] * keep
    tail_start = vectors[taps + 4 + rows :] * jnp.tile(keep, (lag, 1))
    both = table[:, :, :lines].reshape(nseq, nco, 2, heads, -1, span)
    both = jnp.transpose(both, (2, 1, 3, 0, 4, 5)).reshape(2, nco * heads, span, span)
    gate = gate_matrix(both)

    normal_in, u, v, ra, ri, decay, drive, u_before, summary = gates_call(
        place, x_all, border, gain_one, tail_start, gate, vec, recur_pieces, rows
    )
    branch_chunks = [branch_chunks[0]] + [after(item, recur_pieces[-1]) for item in branch_chunks[1:]]
    branch_pieces = over_die(travel(join_columns(branch_chunks, 1), "sx"))
    yp = branch_call(normal_in, branch_pieces)
    ends = u[PEER - 1, own - lag * rows :]
    outer = other_blocks(summary, rows, False)
    enter = outer[:rows] * state_start + outer[rows:]
    enter = after(enter, grad_near, grad_far)

    out_chunks = [out_chunks[0]] + [after(item, enter) for item in out_chunks[1:]]
    out_pieces = over_die(travel(jnp.concatenate(out_chunks, axis=0), "sx"))
    gate_chunks, up_chunks, down_chunks = (
        around(after(shard, enter), "co") for shard in (gate_proj, up_proj, down_proj)
    )

    h, z, h_before, h_end = states_call(place, decay, drive, yp, enter)
    z_rows = z.reshape(group, width)
    branch = product_call(z_rows, out_pieces)
    terms = cut(branch, PEER, 0)
    cross = peer(terms[3], 1)
    near = peer(after(terms[1], cross), 1)
    far = peer((terms[2].astype(F32) + cross.astype(F32)).astype(BF), 2)
    gate_chunks[1:] = [after(item, branch) for item in gate_chunks[1:]]
    gate_pieces = over_die(travel(join_columns(gate_chunks, 1), "sx"))
    resid = mine.astype(F32) + terms[0].astype(F32) + near.astype(F32) + far.astype(F32)
    resid = after(resid, grad_full)
    up_chunks[1:] = [after(item, resid) for item in up_chunks[1:]]
    up_pieces = over_die(travel(join_columns(up_chunks, 1), "sx"))

    inv_two = inverse_rms(resid)
    normed_two = resid * inv_two
    normal_group = peer_rows((normed_two * gain_two).astype(BF))
    normal_mid = jnp.concatenate(normal_group, axis=0)
    down_chunks[1:] = [after(item, normal_group[2]) for item in down_chunks[1:]]
    down_pieces = over_die(travel(jnp.concatenate(down_chunks, axis=0), "sx"))
    hidden, grad_gate, grad_up = mlp_call(
        normal_mid, grad_full, gate_pieces, up_pieces, down_pieces
    )
    def over_cores(halves):
        return sum_around(halves, "sc").astype(BF)

    def over_chips(grad, axis):
        return sum_around(cut(grad, nsx, axis), "sx").astype(BF)

    def over_chunks(grad, axis, *hold):
        return sum_around(cut(grad, nco, axis), "co", hold)

    down_grad = weight_grad(hidden, grad_full, 1)
    grad_gate, grad_up, down_sent = lax.optimization_barrier((grad_gate, grad_up, down_grad[1]))
    down_grad = over_cores([down_grad[0], down_sent])
    mid = transposed_call(grad_gate, grad_up, gate_pieces, up_pieces)
    mid_sum = peer_sum(cut(mid, PEER, 0))

    up_grad = over_cores(weight_grad(normal_mid, grad_up, 0))
    gate_grad = over_cores(weight_grad(normal_mid, grad_gate, 0))
    mlp = product_call(after(hidden, mid_sum), down_pieces)
    down_grad = over_chips(down_grad, 1)
    mid_sum = after(mid_sum, up_grad)
    gain_two_part = jnp.sum(mid_sum * normed_two, axis=0, keepdims=True)
    resid_grad = grad_mine.astype(F32) + norm_back(mid_sum, normed_two, inv_two, gain_two)
    resid_group = peer_rows(resid_grad.astype(BF))
    resid_all = jnp.stack(resid_group)
    up_grad = over_chips(after(up_grad, down_grad), 0)
    down_out = over_chunks(after(down_grad, resid_group[2]), 0)
    resid_all = after(resid_all, up_grad, down_out, gate_grad)

    dh, grad_branch, local_end = back_call(place, resid_all, yp, h, decay, out_pieces, rows)
    mlp_terms = cut(after(mlp, resid_all), PEER, 0)
    mlp_cross = peer(mlp_terms[3], 1)
    mlp_near = peer(after(mlp_terms[1], mlp_cross), 1)
    local_end = after(local_end, mlp_cross)
    late = other_blocks(jnp.concatenate([summary[:rows], local_end], axis=0), rows, True)[rows:]
    gate_grad = over_chips(after(gate_grad, late), 0)
    relay = (mlp_terms[2].astype(F32) + mlp_cross.astype(F32)).astype(BF)
    mlp_far = peer(after(relay, late), 2)
    mlp_sum = mlp_terms[0].astype(F32) + mlp_near.astype(F32) + mlp_far.astype(F32)
    mixed = (resid + mlp_sum).astype(BF)
    gates_low, grad_u, edge_out, last, sums, start_grad = grads_call(
        place, dh, decay, ra, ri, v, h, h_before, u, u_before, gate, vec, late
    )
    edge_in = chunk_roll(block_shift(edge_out, -1), -1)
    grad_branch, resid_late = lax.optimization_barrier(
        (grad_branch, resid_all, edge_out, mlp_cross)
    )[:2]
    grad_branch = grad_branch.reshape(group, width)
    normal_rows = normal_in.reshape(group, model)
    out_grad = over_cores(weight_grad(z_rows, resid_late.reshape(group, model), 1))
    branch_grad = over_cores(weight_grad(normal_rows, grad_branch, 0))
    fixed = (last + edge_in).astype(BF)[None]
    grad_u = lax.dynamic_update_slice(
        grad_u, fixed, (lax.bitwise_xor(ci, PEER - 1), own - lag * rows, 0)
    )
    grad_u = grad_u.reshape(group, width)
    back = transposed_call(grad_u, grad_branch, recur_pieces, branch_pieces)
    up_last = around_back(cut(after(up_grad, late), nco, 1), "co")
    gate_last = around_back(cut(after(gate_grad, late), nco, 1), "co")
    terms = cut(after(back, mlp_near, mlp_far, *up_last[1:]), PEER, 0)
    cross = peer(terms[3], 1)
    near = peer(after(terms[1], cross), 1)
    relay = (terms[2].astype(F32) + cross.astype(F32)).astype(BF)
    far = peer(after(relay, *gate_last[1:]), 2)
    back_sum = terms[0].astype(F32) + near.astype(F32) + far.astype(F32)
    both_grad = over_tokens(v.reshape(group, width), gates_low.reshape(group, 2 * width))
    recur_grad = over_cores(weight_grad(normal_rows, grad_u, 0))
    value = mine.astype(F32)
    inv_one = inverse_rms(value)
    normed_one = value * inv_one
    x_value = after(x_all, late).astype(F32)
    gain_one_part = jnp.sum(
        back.reshape(PEER, own, model).astype(F32) * (x_value * inverse_rms(x_value)), axis=(0, 1)
    )[None]
    tokens_grad = resid_grad + norm_back(back_sum, normed_one, inv_one, gain_one)

    up_out = sum(item.astype(F32) for item in up_last)
    gate_out = sum(item.astype(F32) for item in gate_last)
    out_grad = over_chips(out_grad, 1)
    branch_grad = over_chips(after(branch_grad, out_grad), 0)
    out_out = over_chunks(out_grad, 0, back_sum)
    recur_grad = over_chips(after(recur_grad, branch_grad), 0)
    branch_out = over_chunks(branch_grad, 1, back_sum)
    recur_out = over_chunks(recur_grad, 1)

    pieces = jnp.stack(
        [
            both_grad[span * h : span * (h + 1), g * width + span * h : g * width + span * (h + 1)]
            for g in range(2)
            for h in range(nco * heads)
        ]
    )
    pieces = pieces.reshape(2, nco, heads, nseq, -1, span)
    pieces = jnp.transpose(pieces, (3, 1, 0, 2, 4, 5)).reshape(nseq, nco, -1, span)
    sums = jnp.sum(sums.reshape(-1, rows, width), axis=1)
    small = jnp.concatenate(
        [
            sums[0:2],
            sums[2:3] * 8.0 * jax.nn.sigmoid(-decay32),
            sums[3:],
            jnp.where(first, keep * start_grad, 0.0),
            jnp.where(first, jnp.tile(keep, (lag, 1)) * edge_out, 0.0),
        ],
        axis=0,
    )
    small = jnp.transpose(small.reshape(-1, nco, nseq, part), (2, 1, 0, 3))
    small = jnp.pad(small, ((0, 0), (0, 0), (0, 0), (0, span - part)))
    packed = jnp.concatenate([pieces, small], axis=2)
    packed = jnp.concatenate(
        [
            lax.dynamic_slice_in_dim(packed, ((sx - rx) % nsx) * nsc + (sc - rc) % nsc, 1, 0)
            for rc in range(nsc)
            for rx in range(nsx)
        ],
        axis=0,
    ).astype(BF)
    packed = over_chips(over_cores(cut(packed, nsc, 0)), 0)[0]
    packed = over_chunks(after(packed, back_sum), 0)[0]
    both_out = packed[:lines].reshape(2, heads, -1, span)
    small = packed[lines:, :part]

    total = feature_restore(jnp.concatenate([gain_one_part, gain_two_part], axis=0))
    for axis in ("sc", "sx", "cb", "ca", "co"):
        if axis == "cb":
            total = after(total, back_sum)
        total = sum(around(total, axis)[1:], total)
    start = (lax.axis_index(("co", "ca", "cb")) * nseq + sx * nsc + sc) * unit
    gain_out = lax.dynamic_slice_in_dim(total, start, unit, 1)

    finish = after(jnp.concatenate([h_end, ends.astype(F32)], axis=0), hidden)
    reach = jnp.where(co == nco - 1, finish[:, :chunk], 0.0)
    for k in range(1, nco):
        piece = finish[:, (nco - k) * chunk : (nco - k + 1) * chunk]
        reach = reach + lax.ppermute(piece, "co", [(nco - 1, k - 1)])
    group_states = reach[:rows][None]
    group_tails = jnp.swapaxes(reach[rows:].reshape(lag, rows, chunk), 0, 1).astype(BF)[None]

    def returned(value):
        return jnp.swapaxes(feature_restore(value).reshape(share, rows, model), 0, 1)

    return (
        returned(mixed),
        returned(tokens_grad),
        gain_out[0],
        gain_out[1],
        recur_out,
        branch_out,
        out_out,
        gate_out,
        up_out,
        down_out,
        both_out[0],
        both_out[1],
        small[0],
        small[1],
        small[2],
        small[3],
        small[4 : 4 + taps],
        small[4 + taps : 4 + taps + rows],
        jnp.swapaxes(small[4 + taps + rows :].reshape(lag, rows, part), 0, 1),
        group_states,
        group_tails,
    )


def solution(mesh):
    nseq, nchan = mesh.devices.shape
    fine = Mesh(
        mesh.devices.reshape(nseq // 2, 2, nchan // PEER, 2, 2), ("sx", "sc", "co", "ca", "cb")
    )
    seq = ("sx", "sc")
    chan = ("co", "ca", "cb")
    place = P(None, seq + chan, None)
    vector = P(chan + seq)
    in_specs = (
        place,
        vector,
        vector,
        P(seq, chan),
        P(seq, chan),
        P(chan, seq),
        P(seq, chan),
        P(seq, chan),
        P(chan, seq),
        P(chan, seq, None),
        P(chan, seq, None),
        vector,
        vector,
        vector,
        vector,
        P(None, chan + seq),
        P(None, chan + seq),
        P(None, None, chan + seq),
        P(),
        place,
    )
    out_specs = (
        place,
        place,
        vector,
        vector,
        P(seq, chan),
        P(seq, chan),
        P(chan, seq),
        P(seq, chan),
        P(seq, chan),
        P(chan, seq),
        P(chan, seq, None),
        P(chan, seq, None),
        vector,
        vector,
        vector,
        vector,
        P(None, chan + seq),
        P(None, chan + seq),
        P(None, None, chan + seq),
        P(seq, None, chan),
        P(seq, None, None, chan),
    )
    return jax.shard_map(shards, mesh=fine, in_specs=in_specs, out_specs=out_specs, check_vma=False)
```

```python
import functools

import jax
import jax.numpy as jnp
from jax import lax
from jax.experimental import pallas as pl
from jax.experimental.pallas import tpu as pltpu
from jax.sharding import Mesh
from jax.sharding import PartitionSpec as P

BF = jnp.bfloat16
F32 = jnp.float32
BLOCKS = ("sx", "sc", "co")
PEERS = ("ca", "cb")
PEER = 4
GELU_C = 0.7978845608028654
GELU_K = 0.044715


def shift(value, axis, step):
    count = lax.axis_size(axis)
    return lax.ppermute(value, axis, [(i, (i + step) % count) for i in range(count)])


def block_shift(value, step):
    count = lax.axis_size(BLOCKS)
    route = [(i, i + step) for i in range(count) if 0 <= i + step < count]
    return lax.ppermute(value, BLOCKS, route)


def peer(value, step):
    return lax.ppermute(value, PEERS, [(i, i ^ step) for i in range(PEER)])


def before_last(value):
    count = lax.axis_size(BLOCKS)
    return sum(
        lax.ppermute(
            value,
            BLOCKS + PEERS,
            [((b - 1) * PEER + PEER - 1, b * PEER + k) for b in range(1, count)],
        )
        for k in range(PEER)
    )


def peer_rows(value, hold=()):
    near = peer(value, 1)
    far = peer(after(value, *hold), 2)
    return [value, near, far, peer(after(far, near), 1)]


def peer_sum(terms, hold=()):
    mine, near, far, across = terms
    across = peer(across, 1)
    near = peer(after(near, across), 1)
    relay = (far.astype(F32) + across.astype(F32)).astype(BF)
    far = peer(after(relay, *hold), 2)
    return mine.astype(F32) + near.astype(F32) + far.astype(F32)


def after(value, *done):
    return lax.optimization_barrier((value, *done))[0]


def around(value, axis):
    return [value] + [shift(value, axis, r) for r in range(1, lax.axis_size(axis))]


def over_die(items):
    return items + [shift(item, "sc", r) for r in range(1, lax.axis_size("sc")) for item in items]


def cut(value, count, axis):
    size = value.shape[axis] // count
    return [lax.slice_in_dim(value, r * size, (r + 1) * size, axis=axis) for r in range(count)]


def around_back(parts, axis):
    return parts[:1] + [shift(part, axis, -1 - r) for r, part in enumerate(parts[1:])]


def sum_around(parts, axis, hold=()):
    total = parts[0].astype(F32)
    for r in range(1, len(parts)):
        term = shift(parts[r].astype(BF), axis, -r)
        total = total + after(term, *hold).astype(F32)
    return total


def chunk_roll(value, step):
    count = lax.axis_size("co")
    step = step % count
    if step == 0:
        return value
    width = value.shape[-1] // count
    cut = width * (count - step)
    return jnp.concatenate([value[..., cut:], value[..., :cut]], axis=-1)


def feature_order(value):
    nsx, nsc = lax.axis_size("sx"), lax.axis_size("sc")
    sx, sc = lax.axis_index("sx"), lax.axis_index("sc")
    width = value.shape[-1] // (nsx * nsc)
    parts = []
    for rc in range(nsc):
        for rx in range(nsx):
            owner = lax.rem(sx - rx + nsx, nsx) * nsc + lax.rem(sc - rc + nsc, nsc)
            parts.append(lax.dynamic_slice_in_dim(value, owner * width, width, value.ndim - 1))
    return jnp.concatenate(parts, axis=-1)


def feature_restore(value):
    nsx, nsc = lax.axis_size("sx"), lax.axis_size("sc")
    sx, sc = lax.axis_index("sx"), lax.axis_index("sc")
    width = value.shape[-1] // (nsx * nsc)
    parts = []
    for owner in range(nsx * nsc):
        rx = lax.rem(sx - owner // nsc + nsx, nsx)
        rc = lax.rem(sc - owner % nsc + nsc, nsc)
        parts.append(
            lax.dynamic_slice_in_dim(value, (rc * nsx + rx) * width, width, value.ndim - 1)
        )
    return jnp.concatenate(parts, axis=-1)


def join_kernel(groups, *refs):
    out = refs[-1]
    width = refs[0].shape[1] // groups
    at = 0
    for g in range(groups):
        for ref in refs[:-1]:
            out[:, at : at + width] = ref[:, g * width : (g + 1) * width]
            at += width


def join_columns(items, groups):
    rows, width = items[0].shape
    block = rows // 2
    return pl.pallas_call(
        functools.partial(join_kernel, groups),
        out_shape=jax.ShapeDtypeStruct((rows, width * len(items)), items[0].dtype),
        grid=(2,),
        in_specs=[pl.BlockSpec((block, width), lambda i: (i, 0))] * len(items),
        out_specs=pl.BlockSpec((block, width * len(items)), lambda i: (i, 0)),
        name="join",
    )(*items)


def compose(earlier, later, rows):
    decay, state = later[:rows], later[rows:]
    return jnp.concatenate([earlier[:rows] * decay, decay * earlier[rows:] + state], axis=0)


def other_blocks(summary, rows, backward):
    width = summary.shape[-1]
    empty = jnp.concatenate([jnp.ones((rows, width), F32), jnp.zeros((rows, width), F32)], axis=0)
    outer = empty
    for axis in ("co", "sc", "sx"):
        count, mine = lax.axis_size(axis), lax.axis_index(axis)
        items = around(summary, axis)
        if axis == "co":
            mark = items[1]
            items = [chunk_roll(item, r) for r, item in enumerate(items)]
        if count == 2:
            mate = items[1]
            ahead = (mine == 0) if backward else (mine == 1)
            joined = compose(mate, summary, rows)
            outer = jnp.where(ahead, compose(mate, outer, rows), outer)
            summary = jnp.where(ahead, joined, compose(summary, mate, rows))
        else:
            table = jnp.stack(items)
            total, inner = empty, empty
            for place in reversed(range(count)) if backward else range(count):
                item = table[lax.rem(mine - place + count, count)]
                total = compose(total, item, rows)
                ahead = (place > mine) if backward else (place < mine)
                inner = jnp.where(ahead, compose(inner, item, rows), inner)
            outer = compose(inner, outer, rows)
            summary = total
    return outer, mark


def matmul(left, right):
    return jnp.dot(left, right, preferred_element_type=F32)


def over_tokens(left, right):
    return lax.dot_general(left, right, (((0,), (0,)), ((), ())), preferred_element_type=F32)


def times_transpose(left, right):
    return lax.dot_general(left, right, (((1,), (1,)), ((), ())), preferred_element_type=F32)


def weight_grad(left, right, halved):
    if halved == 0:
        halves = [over_tokens(half, right).astype(BF) for half in cut(left, 2, 1)]
    else:
        halves = [over_tokens(left, half).astype(BF) for half in cut(right, 2, 1)]
    return [lax.optimization_barrier(half) for half in halves]


def gelu_parts(value):
    square = value * value
    wave = jnp.tanh(GELU_C * (value + GELU_K * value * square))
    half = 0.5 * (1.0 + wave)
    slope = half + 0.5 * value * (1.0 - wave * wave) * (GELU_C * (1.0 + 3.0 * GELU_K * square))
    return value * half, slope


def minus_expm1(value):
    series = 1.0 + value * (1.0 / 7.0)
    for order in (6.0, 5.0, 4.0, 3.0, 2.0):
        series = 1.0 + value * (1.0 / order) * series
    return -jnp.where(value > -0.3, value * series, jnp.exp(value) - 1.0)


def decay_terms(rate, soft):
    log_decay = -8.0 * rate * soft
    return jnp.exp(log_decay), jnp.sqrt(minus_expm1(2.0 * log_decay))


def rows_times(values, pieces, columns=slice(None)):
    total = None
    size = pieces[0].shape[0]
    for i, piece in enumerate(pieces):
        term = matmul(values[:, i * size : (i + 1) * size], piece[:, columns])
        total = term if total is None else total + term
    return total


def columns_times(values, pieces):
    total = None
    size = pieces[0].shape[1]
    for i, piece in enumerate(pieces):
        term = times_transpose(values[:, i * size : (i + 1) * size], piece[...])
        total = term if total is None else total + term
    return total


def gates_kernel(
    count, here, x_ref, border_ref, gain_ref, tail_ref, gate_ref, vec_ref, *refs
):
    pieces, refs = refs[:count], refs[count:]
    n_ref, u_ref, v_ref, ra_ref, ri_ref, a_ref, e_ref, before_ref, end_ref, pad, held = refs
    step = pl.program_id(0)
    rows = held.shape[0] // 2
    size, width = u_ref.shape
    lag = tail_ref.shape[0]

    def normal(value):
        value = value.astype(F32)
        root = lax.rsqrt(jnp.mean(value * value, axis=-1, keepdims=True) + 1e-06)
        return (value * root * gain_ref[...]).astype(BF)

    @pl.when(step == 0)
    def _():
        edge = rows_times(normal(border_ref[...]), pieces).astype(BF).astype(F32)
        pad[0:lag, :] = jnp.where(here[1] == 1, tail_ref[...].astype(BF).astype(F32), edge)
        held[0:rows, :] = jnp.ones((rows, width), F32)
        held[rows:, :] = jnp.zeros((rows, width), F32)

    @pl.when(step > 0)
    def _():
        pad[0:lag, :] = pad[size : size + lag, :]

    low = normal(x_ref[...])
    n_ref[...] = low
    conv_in = rows_times(low, pieces).astype(BF)
    u_ref[...] = conv_in
    pad[lag:, :] = conv_in.astype(F32)
    before_ref[...] = pad[0:lag, :]
    taps = lag // rows + 1
    conv = vec_ref[taps : taps + 1, :] + vec_ref[0:1, :] * pad[lag : lag + size, :]
    for k in range(1, taps):
        conv = conv + vec_ref[k : k + 1, :] * pad[lag - rows * k : lag - rows * k + size, :]
    low = conv.astype(BF)
    v_ref[...] = low
    pre = jnp.dot(low, gate_ref[...], preferred_element_type=F32)
    ra = jax.nn.sigmoid(pre[:, :width] + vec_ref[taps + 1 : taps + 2, :])
    ri = jax.nn.sigmoid(pre[:, width:] + vec_ref[taps + 2 : taps + 3, :])
    decay, root = decay_terms(ra, vec_ref[taps + 3 : taps + 4, :])
    ra_ref[...] = ra
    ri_ref[...] = ri
    a_ref[...] = decay
    e_ref[...] = low.astype(F32) * ri * root
    prod = held[0:rows, :]
    state = held[rows:, :]
    for t in range(size // rows):
        now = a_ref[t * rows : (t + 1) * rows, :]
        state = now * state + e_ref[t * rows : (t + 1) * rows, :]
        prod = prod * now
    held[0:rows, :] = prod
    held[rows:, :] = state
    end_ref[0:rows, :] = prod
    end_ref[rows:, :] = state


def branch_kernel(count, n_ref, *refs):
    refs[count][...] = rows_times(n_ref[...], refs[:count])


def states_kernel(place, a_ref, e_ref, yp_ref, enter_ref, h_ref, z_ref, before_ref, end_ref, held):
    step = pl.program_id(0)
    rows = held.shape[0]

    @pl.when(step == 0)
    def _():
        held[...] = enter_ref[...]

    state = held[...]
    before_ref[...] = state
    for t in range(a_ref.shape[0] // rows):
        at = slice(t * rows, (t + 1) * rows)
        state = a_ref[at, :] * state + e_ref[at, :]
        h_ref[at, :] = state
    held[...] = state
    end_ref[...] = state
    act, _ = gelu_parts(yp_ref[...])
    z_ref[...] = (h_ref[...] * act).astype(BF)


def back_kernel(count, place, g_ref, yp_ref, h_ref, a_ref, *refs):
    pieces = refs[:count]
    dh_ref, dyp_ref, end_ref, held = refs[count:]
    step = pl.program_id(0)
    rows = held.shape[0]

    @pl.when(step == 0)
    def _():
        held[...] = jnp.zeros(held.shape, F32)

    act, slope = gelu_parts(yp_ref[...])
    dz = columns_times(g_ref[...], pieces)
    dh_ref[...] = dz * act
    dyp_ref[...] = (dz * h_ref[...] * slope).astype(BF)
    carry = held[...]
    for t in reversed(range(a_ref.shape[0] // rows)):
        at = slice(t * rows, (t + 1) * rows)
        carry = a_ref[at, :] * (dh_ref[at, :] + carry)
    held[...] = carry
    end_ref[...] = carry


def mlp_kernel(count, n_ref, dy_ref, *refs):
    gates, ups, downs = refs[:count], refs[count : 2 * count], refs[2 * count : 3 * count]
    m_ref, dg_ref, du_ref = refs[3 * count :]
    gate = rows_times(n_ref[...], gates)
    up = rows_times(n_ref[...], ups)
    grad = columns_times(dy_ref[...], downs)
    act, slope = gelu_parts(gate)
    m_ref[...] = (act * up).astype(BF)
    dg_ref[...] = (grad * up * slope).astype(BF)
    du_ref[...] = (grad * act).astype(BF)


def product_kernel(count, per, x_ref, *refs):
    out_ref = refs[count]
    step = pl.program_id(0)
    for i in range(count):

        @pl.when(step // per == i)
        def _():
            out_ref[...] = matmul(x_ref[...], refs[i][...]).astype(BF)


def transposed_kernel(count, per, x_ref, y_ref, *refs):
    out_ref = refs[2 * count]
    step = pl.program_id(0)
    for i in range(count):

        @pl.when(step // per == i)
        def _():
            out_ref[...] = (
                times_transpose(x_ref[...], refs[i][...])
                + times_transpose(y_ref[...], refs[count + i][...])
            ).astype(BF)


def grads_kernel(
    place, dh_ref, a_ref, ra_ref, ri_ref, v_ref, h_ref, hb_ref, u_ref, ub_ref, gate_ref, vec_ref,
    late_ref, gates_ref, du_ref, edge_ref, last_ref, sums_ref, end_ref, held, pad, spad, hpad, upad,
):
    step = pl.program_id(0)
    rows = held.shape[0]
    size = dh_ref.shape[0]
    width = dh_ref.shape[1]
    lag = ub_ref.shape[0]
    taps = lag // rows + 1

    @pl.when(step == 0)
    def _():
        held[...] = late_ref[...]
        pad[size:, :] = jnp.zeros((lag, width), F32)
        sums_ref[...] = jnp.zeros(sums_ref.shape, F32)

    @pl.when(step > 0)
    def _():
        pad[size:, :] = pad[0:lag, :]

    carry = held[...]
    for t in reversed(range(size // rows)):
        at = slice(t * rows, (t + 1) * rows)
        now = dh_ref[at, :] + carry
        spad[at, :] = now
        carry = a_ref[at, :] * now
    held[...] = carry
    end_ref[...] = carry
    hpad[0:rows, :] = hb_ref[...]
    hpad[rows:, :] = h_ref[...]
    upad[0:lag, :] = ub_ref[...]
    upad[lag:, :] = u_ref[...].astype(F32)
    s = spad[...]
    ra = ra_ref[...]
    ri = ri_ref[...]
    soft = vec_ref[taps + 3 : taps + 4, :]
    decay, root = decay_terms(ra, soft)
    v = v_ref[...].astype(F32)
    sv = s * v
    grad_log = decay * (s * hpad[0:size, :] - sv * ri * decay / root)
    rated = grad_log * ra
    dap = (-8.0 * soft * rated * (1.0 - ra)).astype(BF)
    dip = (sv * root * ri * (1.0 - ri)).astype(BF)
    gates_ref[:, :width] = dap
    gates_ref[:, width:] = dip
    dv = s * ri * root + lax.dot_general(
        gates_ref[...], gate_ref[...], (((1,), (1,)), ((), ())), preferred_element_type=F32
    )
    pad[0:size, :] = dv

    def fold(value):
        return jnp.sum(value.reshape(size // rows, rows, width), axis=0)

    terms = [dap.astype(F32), dip.astype(F32), rated, dv]
    terms = terms + [dv * upad[lag - rows * k : lag - rows * k + size, :] for k in range(taps)]
    for i, term in enumerate(terms):
        sums_ref[i * rows : (i + 1) * rows, :] += fold(term)
    du = vec_ref[0:1, :] * dv
    for k in range(1, taps):
        du = du + vec_ref[k : k + 1, :] * pad[rows * k : rows * k + size, :]
    du_ref[...] = du.astype(BF)

    @pl.when(step == 0)
    def _():
        last_ref[...] = du[size - lag :, :]

    for t in range(taps - 1):
        row = jnp.zeros((rows, width), F32)
        for k in range(taps - 1 - t, taps):
            at = (t + k - (taps - 1)) * rows
            row = row + vec_ref[k : k + 1, :] * pad[at : at + rows, :]
        edge_ref[t * rows : (t + 1) * rows, :] = row


def gate_matrix_kernel(blocks_ref, out_ref):
    kinds, heads, span, _ = blocks_ref.shape
    out_ref[...] = jnp.zeros(out_ref.shape, BF)
    for g in range(kinds):
        for h in range(heads):
            at = (g * heads + h) * span
            out_ref[h * span : (h + 1) * span, at : at + span] = blocks_ref[g, h]


def gate_matrix(blocks):
    kinds, heads, span, _ = blocks.shape
    return pl.pallas_call(
        gate_matrix_kernel,
        out_shape=jax.ShapeDtypeStruct((heads * span, kinds * heads * span), BF),
        name="gate_matrix",
    )(blocks)


def whole(shape):
    return pl.BlockSpec(shape, lambda *_: (0,) * len(shape))


def gates_call(place, x, border, gain, tail, gate, vec, pieces, rows):
    steps, size, model = x.shape
    lag, width = tail.shape
    wide = pieces[0].shape[0]
    here = pl.BlockSpec((None, size, width), lambda j, c: (j, 0, 0))
    full = jax.ShapeDtypeStruct((steps, size, width), F32)
    low = jax.ShapeDtypeStruct((steps, size, width), BF)
    rowed = pl.BlockSpec((None, size, model), lambda j, c: (j ^ c[0], 0, 0))
    return pl.pallas_call(
        functools.partial(gates_kernel, len(pieces)),
        out_shape=(
            jax.ShapeDtypeStruct(x.shape, BF),
            low,
            low,
            full,
            full,
            full,
            full,
            jax.ShapeDtypeStruct((steps, lag, width), F32),
            jax.ShapeDtypeStruct((2 * rows, width), F32),
        ),
        grid_spec=pltpu.PrefetchScalarGridSpec(
            num_scalar_prefetch=1,
            grid=(steps,),
            in_specs=[
                rowed,
                whole(border.shape),
                whole(gain.shape),
                whole(tail.shape),
                whole(gate.shape),
                whole(vec.shape),
            ]
            + [pl.BlockSpec((wide, width), lambda j, c: (0, 0))] * len(pieces),
            out_specs=[
                rowed,
                here,
                here,
                here,
                here,
                here,
                here,
                pl.BlockSpec((None, lag, width), lambda j, c: (j, 0, 0)),
                whole((2 * rows, width)),
            ],
            scratch_shapes=[
                pltpu.VMEM((size + lag, width), F32),
                pltpu.VMEM((2 * rows, width), F32),
            ],
        ),
        name="gates",
    )(place, x, border, gain, tail, gate, vec, *pieces)


def branch_call(n, pieces):
    steps, size, model = n.shape
    wide, width = pieces[0].shape
    return pl.pallas_call(
        functools.partial(branch_kernel, len(pieces)),
        out_shape=jax.ShapeDtypeStruct((steps, size, width), F32),
        grid=(steps,),
        in_specs=[pl.BlockSpec((None, size, model), lambda j: (j, 0, 0))]
        + [whole((wide, width))] * len(pieces),
        out_specs=pl.BlockSpec((None, size, width), lambda j: (j, 0, 0)),
        name="branch",
    )(n, *pieces)


def states_call(place, a, e, yp, enter):
    steps, size, width = a.shape
    rows = enter.shape[0]
    here = pl.BlockSpec((None, size, width), lambda j, c: (j, 0, 0))
    there = pl.BlockSpec((None, size, width), lambda j, c: (j ^ c[0], 0, 0))
    return pl.pallas_call(
        states_kernel,
        out_shape=(
            jax.ShapeDtypeStruct((steps, size, width), F32),
            jax.ShapeDtypeStruct((steps, size, width), BF),
            jax.ShapeDtypeStruct((steps, rows, width), F32),
            jax.ShapeDtypeStruct((rows, width), F32),
        ),
        grid_spec=pltpu.PrefetchScalarGridSpec(
            num_scalar_prefetch=1,
            grid=(steps,),
            in_specs=[here, here, there, whole((rows, width))],
            out_specs=[
                here,
                there,
                pl.BlockSpec((None, rows, width), lambda j, c: (j, 0, 0)),
                whole((rows, width)),
            ],
            scratch_shapes=[pltpu.VMEM((rows, width), F32)],
        ),
        name="states",
    )(place, a, e, yp, enter)


def back_call(place, g, yp, h, a, pieces, rows):
    steps, size, width = a.shape
    last = steps - 1
    here = pl.BlockSpec((None, size, width), lambda j, c: (last - j, 0, 0))
    there = pl.BlockSpec((None, size, width), lambda j, c: ((last - j) ^ c[0], 0, 0))
    return pl.pallas_call(
        functools.partial(back_kernel, len(pieces)),
        out_shape=(
            jax.ShapeDtypeStruct((steps, size, width), F32),
            jax.ShapeDtypeStruct((steps, size, width), BF),
            jax.ShapeDtypeStruct((rows, width), F32),
        ),
        grid_spec=pltpu.PrefetchScalarGridSpec(
            num_scalar_prefetch=1,
            grid=(steps,),
            in_specs=[
                pl.BlockSpec((None, size, g.shape[2]), lambda j, c: ((last - j) ^ c[0], 0, 0)),
                there,
                here,
                here,
            ]
            + [whole(pieces[0].shape)] * len(pieces),
            out_specs=[here, there, whole((rows, width))],
            scratch_shapes=[pltpu.VMEM((rows, width), F32)],
        ),
        name="back",
    )(place, g, yp, h, a, *pieces)


def grads_call(place, dh, a, ra, ri, v, h, h_before, u, u_before, gate, vec, late):
    steps, size, width = a.shape
    rows = late.shape[0]
    lag = u_before.shape[1]
    last = steps - 1
    count = lag // rows + 5
    here = pl.BlockSpec((None, size, width), lambda j, c: (last - j, 0, 0))
    there = pl.BlockSpec((None, size, width), lambda j, c: ((last - j) ^ c[0], 0, 0))
    small = lambda size: pl.BlockSpec((None, size, width), lambda j, c: (last - j, 0, 0))
    return pl.pallas_call(
        grads_kernel,
        out_shape=(
            jax.ShapeDtypeStruct((steps, size, 2 * width), BF),
            jax.ShapeDtypeStruct((steps, size, width), BF),
            jax.ShapeDtypeStruct((lag, width), F32),
            jax.ShapeDtypeStruct((lag, width), F32),
            jax.ShapeDtypeStruct((count * rows, width), F32),
            jax.ShapeDtypeStruct((rows, width), F32),
        ),
        grid_spec=pltpu.PrefetchScalarGridSpec(
            num_scalar_prefetch=1,
            grid=(steps,),
            in_specs=[
            here,
            here,
            here,
            here,
            here,
            here,
            small(rows),
            here,
            small(lag),
            whole(gate.shape),
            whole(vec.shape),
            whole(late.shape),
        ],
        out_specs=[
            pl.BlockSpec((None, size, 2 * width), lambda j, c: (last - j, 0, 0)),
            there,
            whole((lag, width)),
            whole((lag, width)),
            whole((count * rows, width)),
            whole((rows, width)),
        ],
        scratch_shapes=[
            pltpu.VMEM((rows, width), F32),
            pltpu.VMEM((size + lag, width), F32),
            pltpu.VMEM((size, width), F32),
            pltpu.VMEM((size + rows, width), F32),
            pltpu.VMEM((size + lag, width), F32),
        ],
        ),
        name="grads",
    )(place, dh, a, ra, ri, v, h, h_before, u, u_before, gate, vec, late)


def tile_of(size, most):
    return max(t for t in range(128, most + 1, 128) if size % t == 0)


def mlp_call(n, dy, gates, ups, downs):
    tokens, model = n.shape
    wide, units = gates[0].shape
    tile = tile_of(units, 256)
    count = len(gates)
    out = pl.BlockSpec((tokens, tile), lambda j: (0, j))
    return pl.pallas_call(
        functools.partial(mlp_kernel, count),
        out_shape=[jax.ShapeDtypeStruct((tokens, units), BF)] * 3,
        grid=(units // tile,),
        in_specs=[whole((tokens, model))] * 2
        + [pl.BlockSpec((wide, tile), lambda j: (0, j))] * (2 * count)
        + [pl.BlockSpec((tile, wide), lambda j: (j, 0))] * count,
        out_specs=[out] * 3,
        name="mlp",
    )(n, dy, *gates, *ups, *downs)


def clipped(step, per, i):
    return jnp.clip(step - i * per, 0, per - 1)


def product_call(x, pieces, size=None, at=0):
    depth = x.shape[1]
    tokens = size or x.shape[0]
    wide = pieces[0].shape[1]
    tile = tile_of(wide, 512)
    per, count = wide // tile, len(pieces)
    return pl.pallas_call(
        functools.partial(product_kernel, count, per),
        out_shape=jax.ShapeDtypeStruct((tokens, wide * count), BF),
        grid=(per * count,),
        in_specs=[pl.BlockSpec((tokens, depth), lambda s: (at, 0))]
        + [
            pl.BlockSpec((depth, tile), lambda s, i=i: (0, clipped(s, per, i)))
            for i in range(count)
        ],
        out_specs=pl.BlockSpec((tokens, tile), lambda s: (0, s)),
        name="product",
    )(x, *pieces)


def transposed_call(x, y, first, second, size=None, at=0):
    depth = x.shape[1]
    tokens = size or x.shape[0]
    wide = first[0].shape[0]
    tile = tile_of(wide, 256)
    per, count = wide // tile, len(first)
    return pl.pallas_call(
        functools.partial(transposed_kernel, count, per),
        out_shape=jax.ShapeDtypeStruct((tokens, wide * count), BF),
        grid=(per * count,),
        in_specs=[pl.BlockSpec((tokens, depth), lambda s: (at, 0))] * 2
        + [
            pl.BlockSpec((tile, depth), lambda s, i=i: (clipped(s, per, i), 0))
            for i in range(count)
        ]
        * 2,
        out_specs=pl.BlockSpec((tokens, tile), lambda s: (0, s)),
        name="transposed",
    )(x, y, *first, *second)


def norm_back(grad_norm, normed, inv_root, gain):
    scaled = grad_norm * gain
    mean_term = jnp.mean(scaled * normed, axis=-1, keepdims=True)
    return inv_root * (scaled - normed * mean_term)


def inverse_rms(value):
    return lax.rsqrt(jnp.mean(value * value, axis=-1, keepdims=True) + 1e-06)


def shards(
    tokens,
    norm_gain,
    mlp_gain,
    recur_proj,
    branch_proj,
    out_proj,
    gate_proj,
    up_proj,
    down_proj,
    recur_gate,
    input_gate,
    recur_bias,
    input_bias,
    decay_param,
    conv_bias,
    conv_weight,
    init_state,
    init_tail,
    reset_flags,
    cotangent,
):
    nsx, nsc, nco = (lax.axis_size(name) for name in BLOCKS)
    nseq = nsx * nsc
    co = lax.axis_index("co")
    first = lax.axis_index(BLOCKS) == 0
    ci = lax.axis_index(PEERS)
    place = jnp.stack([ci, first]).astype(jnp.int32)
    rows, share, model = tokens.shape
    own = rows * share
    group = PEER * own
    taps = conv_weight.shape[0]
    lag = taps - 1
    part = conv_bias.shape[0]
    chunk = part * nseq
    width = chunk * nco
    keep = (1 - reset_flags).astype(F32)[:, None]
    heads, span = recur_gate.shape[0], recur_gate.shape[2]
    unit = norm_gain.shape[0]
    sx, sc = lax.axis_index("sx"), lax.axis_index("sc")

    def owned(value):
        return feature_order(jnp.swapaxes(value, 0, 1).reshape(own, model))

    mine = owned(tokens)
    border = jnp.swapaxes(tokens[:, share - lag :], 0, 1).reshape(lag * rows, model)
    border = feature_order(before_last(border))

    vectors = jnp.concatenate(
        [
            conv_weight,
            conv_bias[None],
            recur_bias[None],
            input_bias[None],
            decay_param[None],
            init_state,
            jnp.swapaxes(init_tail, 0, 1).reshape(lag * rows, part),
        ],
        axis=0,
    )
    both = jnp.stack([recur_gate, input_gate]).reshape(-1, span)
    lines, lists = both.shape[0], vectors.shape[0]
    gains = jnp.stack([norm_gain, mlp_gain])
    gains_got = [peer(gains, k) for k in range(1, PEER)]
    packed = jnp.concatenate(
        [
            both,
            jnp.pad(vectors, ((0, 0), (0, span - part))),
            jnp.pad(
                jnp.concatenate([gains] + gains_got, axis=0),
                ((0, 0), (0, span - unit)),
            ),
        ],
        axis=0,
    )
    x_near = peer(after(mine, *gains_got), 1)
    table = around(packed[None], "co")
    x_far = peer(after(mine, *gains_got), 2)
    x_across = peer(after(x_far, x_near), 1)
    table = around(jnp.concatenate(table, axis=0), "sx")
    ready = table[1:]
    table = jnp.concatenate(table, axis=0)
    table = jnp.concatenate(around(table, "sc"), axis=0)

    links = {"co": ready, "sx": ready}

    def travel(value, axis):
        items = around(after(value, *links[axis]), axis)
        links[axis] = items[1:]
        return items

    def gather(shard):
        return over_die(travel(join_columns(travel(shard, "co"), 1), "sx"))

    recur_chunks = travel(recur_proj, "co")
    x_all = [mine, x_near, x_far, x_across]
    recur_rows = travel(join_columns(recur_chunks, 1), "sx")
    recur_pieces = over_die(recur_rows)
    branch_chunks = travel(branch_proj, "co")
    out_chunks = travel(out_proj, "co")
    grad_mine = owned(cotangent)
    grad_near = peer(after(grad_mine, x_across), 1)
    x_all = after(jnp.stack(x_all), *branch_chunks[1:])
    branch_chunks[1:] = [after(item, *recur_rows[1:]) for item in branch_chunks[1:]]
    branch_rows = travel(join_columns(branch_chunks, 1), "sx")
    branch_pieces = over_die(branch_rows)

    gains = table[:, lines + lists :, :unit].reshape(-1, PEER, 2 * unit)
    gains = jnp.swapaxes(gains, 0, 1).reshape(-1, 2 * unit)
    lot = jnp.arange(model // unit)
    rel = lot // (model // unit // nseq)
    here_seq = ((sx - rel % nsx) % nsx) * nsc + (sc - rel // nsx) % nsc
    whole_unit = here_seq * (model // unit // nseq) + lot % (model // unit // nseq)
    from_chan, from_seq = whole_unit // nseq, whole_unit % nseq
    source = ((from_chan % PEER) ^ lax.axis_index(PEERS)) * nsc + (sc - from_seq % nsc) % nsc
    source = source * nsx + (sx - from_seq // nsc) % nsx
    source = source * nco + (co - from_chan // PEER) % nco
    pick = (source[:, None] == jnp.arange(model // unit)[None, :]).astype(F32)
    gains = jnp.dot(pick, gains.astype(F32), precision=lax.Precision.HIGHEST)
    gain_one = gains[:, :unit].reshape(1, model)
    gain_two = gains[:, unit:].reshape(1, model)

    table = table[:, : lines + lists].reshape(nseq, nco, lines + lists, span)
    table = jnp.concatenate(
        [
            lax.dynamic_slice_in_dim(
                table, ((sc - s % nsc) % nsc) * nsx + (sx - s // nsc) % nsx, 1, 0
            )
            for s in range(nseq)
        ],
        axis=0,
    )
    vectors = table[:, :, lines:, :part]
    vectors = jnp.transpose(vectors, (2, 1, 0, 3)).reshape(-1, width).astype(F32)
    decay32 = vectors[taps + 3 : taps + 4]
    vec = jnp.concatenate([vectors[: taps + 3], jax.nn.softplus(-decay32)], axis=0)
    vec = jnp.pad(vec, ((0, -vec.shape[0] % 8), (0, 0)))
    state_start = vectors[taps + 4 : taps + 4 + rows] * keep
    tail_start = vectors[taps + 4 + rows :] * jnp.tile(keep, (lag, 1))
    both = table[:, :, :lines].reshape(nseq, nco, 2, heads, -1, span)
    both = jnp.transpose(both, (2, 1, 3, 0, 4, 5)).reshape(2, nco * heads, span, span)
    gate = gate_matrix(both)

    normal_in, u, v, ra, ri, decay, drive, u_before, summary = gates_call(
        place, x_all, border, gain_one, tail_start, gate, vec, recur_pieces, rows
    )
    ends = u[PEER - 1, own - lag * rows :]
    outer, mark = other_blocks(after(summary, *branch_rows[1:]), rows, False)
    enter = outer[:rows] * state_start + outer[rows:]
    out_rows = travel(jnp.concatenate(out_chunks, axis=0), "sx")
    out_pieces = over_die(out_rows)
    yp = branch_call(normal_in, branch_pieces)
    grad_far = peer(after(grad_mine, mark), 2)
    grad_full = jnp.concatenate([grad_mine, grad_near, grad_far, peer(grad_far, 1)], axis=0)

    gate_chunks, up_chunks, down_chunks = (
        around(after(shard, mark), "co") for shard in (gate_proj, up_proj, down_proj)
    )

    h, z, h_before, h_end = states_call(place, decay, drive, yp, after(enter, grad_near, *out_rows[1:]))
    z_rows = after(z, *gate_chunks[1:]).reshape(group, width)
    last_term = product_call(z_rows, out_pieces, own, PEER - 1)
    z_rows, last_term = lax.optimization_barrier((z_rows, last_term))
    branch = product_call(z_rows, out_pieces, own * (PEER - 1))
    terms = cut(branch, PEER - 1, 0) + [last_term]
    cross = peer(terms[3], 1)
    near = peer(after(terms[1], cross), 1)
    relay = (terms[2].astype(F32) + cross.astype(F32)).astype(BF)
    far = peer(after(relay, *up_chunks[1:]), 2)
    gate_pieces = over_die(travel(join_columns(gate_chunks, 1), "sx"))
    resid = mine.astype(F32) + terms[0].astype(F32) + near.astype(F32) + far.astype(F32)
    up_pieces = over_die(travel(join_columns(up_chunks, 1), "sx"))

    inv_two = inverse_rms(resid)
    normed_two = resid * inv_two
    normal_mine = after((normed_two * gain_two).astype(BF), *down_chunks[1:])
    normal_near, normal_far = peer(normal_mine, 1), peer(normal_mine, 2)
    normal_across = peer(after(normal_far, normal_near, grad_full), 1)
    normal_group = [normal_mine, normal_near, normal_far, normal_across]
    normal_mid = jnp.concatenate(normal_group, axis=0)
    down_pieces = over_die(travel(jnp.concatenate(down_chunks, axis=0), "sx"))
    hidden, grad_gate, grad_up = mlp_call(
        normal_mid, grad_full, gate_pieces, up_pieces, down_pieces
    )
    def over_cores(halves):
        return sum_around(halves, "sc").astype(BF)

    def over_chips(grad, axis):
        return sum_around(cut(grad, nsx, axis), "sx").astype(BF)

    def over_chunks(grad, axis, *hold):
        return sum_around(cut(grad, nco, axis), "co", hold)

    down_grad = over_cores(weight_grad(hidden, grad_full, 1))
    grad_gate, grad_up, down_grad = lax.optimization_barrier((grad_gate, grad_up, down_grad))
    last_term = transposed_call(
        grad_gate, grad_up, gate_pieces, up_pieces, own, PEER - 1
    )
    grad_gate, last_term = lax.optimization_barrier((grad_gate, last_term))
    mid = transposed_call(grad_gate, grad_up, gate_pieces, up_pieces, own * (PEER - 1))
    terms = cut(mid, PEER - 1, 0) + [last_term]
    cross = peer(terms[3], 1)
    relay = (terms[2].astype(F32) + cross.astype(F32)).astype(BF)
    down_grad = over_chips(down_grad, 1)
    near = peer(after(terms[1], cross), 1)
    far = peer(relay, 2)
    normal_late = after(normal_mid, cross)
    up_grad = over_cores(weight_grad(normal_late, grad_up, 0))
    gate_grad = over_cores(weight_grad(normal_late, grad_gate, 0))
    up_grad = over_chips(after(up_grad, down_grad), 0)
    down_last = around_back(cut(down_grad, nco, 0), "co")
    mid_sum = terms[0].astype(F32) + near.astype(F32) + far.astype(F32)
    mid_sum = after(mid_sum, gate_grad, down_grad)
    mlp = product_call(after(hidden, mid_sum), down_pieces)
    gate_grad = over_chips(after(gate_grad, up_grad), 0)
    gain_two_part = jnp.sum(mid_sum * normed_two, axis=0, keepdims=True)
    resid_grad = grad_mine.astype(F32) + norm_back(mid_sum, normed_two, inv_two, gain_two)
    resid_mine = resid_grad.astype(BF)
    resid_near, resid_far = peer(resid_mine, 1), peer(resid_mine, 2)
    resid_across = peer(after(resid_far, resid_near), 1)
    resid_all = jnp.stack([resid_mine, resid_near, resid_far, resid_across])

    dh, grad_branch, local_end = back_call(place, resid_all, yp, h, decay, out_pieces, rows)
    mlp_terms = cut(after(mlp, resid_all), PEER, 0)
    mlp_cross = peer(mlp_terms[3], 1)
    mlp_near = peer(after(mlp_terms[1], mlp_cross), 1)
    local_end = after(local_end, mlp_cross, gate_grad)
    late, mark = other_blocks(jnp.concatenate([summary[:rows], local_end], axis=0), rows, True)
    late = late[rows:]
    relay = (mlp_terms[2].astype(F32) + mlp_cross.astype(F32)).astype(BF)
    mlp_far = peer(after(relay, mark), 2)
    up_last = around_back(cut(after(up_grad, mark), nco, 1), "co")
    gate_last = around_back(cut(after(gate_grad, mlp_far), nco, 1), "co")
    mlp_sum = mlp_terms[0].astype(F32) + mlp_near.astype(F32) + mlp_far.astype(F32)
    mixed = (resid + mlp_sum).astype(BF)
    gates_low, grad_u, edge_out, last, sums, start_grad = grads_call(
        place, dh, decay, ra, ri, v, h, h_before, u, u_before, gate, vec, late
    )
    edge_in = chunk_roll(block_shift(edge_out, -1), -1)
    grad_branch, resid_late = lax.optimization_barrier(
        (grad_branch, resid_all, edge_out, mlp_far)
    )[:2]
    grad_branch = grad_branch.reshape(group, width)
    normal_rows = normal_in.reshape(group, model)
    out_grad = over_cores(weight_grad(z_rows, resid_late.reshape(group, model), 1))
    branch_grad = over_cores(weight_grad(normal_rows, grad_branch, 0))
    fixed = (last + edge_in).astype(BF)[None]
    grad_u = lax.dynamic_update_slice(
        grad_u, fixed, (lax.bitwise_xor(ci, PEER - 1), own - lag * rows, 0)
    )
    grad_u = after(grad_u, mlp_near, *up_last[1:]).reshape(group, width)
    last_term = transposed_call(grad_u, grad_branch, recur_pieces, branch_pieces, own, PEER - 1)
    grad_u, last_term = lax.optimization_barrier((grad_u, last_term))
    back = transposed_call(
        grad_u, grad_branch, recur_pieces, branch_pieces, own * (PEER - 1)
    )
    terms = cut(back, PEER - 1, 0) + [last_term]
    cross = peer(terms[3], 1)
    near = peer(after(terms[1], cross, out_grad, branch_grad), 1)
    relay = (terms[2].astype(F32) + cross.astype(F32)).astype(BF)
    out_grad = over_chips(out_grad, 1)
    far = peer(relay, 2)
    out_last = around_back(cut(out_grad, nco, 0), "co")
    back_sum = terms[0].astype(F32) + near.astype(F32) + far.astype(F32)
    back_sum = after(back_sum, *out_last[1:])
    both_grad = over_tokens(v.reshape(group, width), gates_low.reshape(group, 2 * width))
    recur_grad = over_cores(weight_grad(normal_rows, after(grad_u, cross), 0))
    value = mine.astype(F32)
    inv_one = inverse_rms(value)
    normed_one = value * inv_one
    x_value = after(x_all, cross).astype(F32)
    x_value = x_value * inverse_rms(x_value)
    gain_one_part = sum(
        jnp.sum(terms[k].astype(F32) * x_value[k], axis=0, keepdims=True) for k in range(PEER)
    )
    tokens_grad = resid_grad + norm_back(back_sum, normed_one, inv_one, gain_one)

    down_out = sum(after(item, late).astype(F32) for item in down_last)
    up_out = sum(item.astype(F32) for item in up_last)
    gate_out = sum(after(item, far).astype(F32) for item in gate_last)
    branch_grad = over_chips(branch_grad, 0)
    out_out = sum(item.astype(F32) for item in out_last)
    held = recur_grad
    recur_grad = over_chips(recur_grad, 0)
    branch_out = over_chunks(branch_grad, 1, back_sum)
    recur_out = over_chunks(recur_grad, 1)

    pieces = jnp.stack(
        [
            both_grad[span * h : span * (h + 1), g * width + span * h : g * width + span * (h + 1)]
            for g in range(2)
            for h in range(nco * heads)
        ]
    )
    pieces = pieces.reshape(2, nco, heads, nseq, -1, span)
    pieces = jnp.transpose(pieces, (3, 1, 0, 2, 4, 5)).reshape(nseq, nco, -1, span)
    sums = jnp.sum(sums.reshape(-1, rows, width), axis=1)
    small = jnp.concatenate(
        [
            sums[0:2],
            sums[2:3] * 8.0 * jax.nn.sigmoid(-decay32),
            sums[3:],
            jnp.where(first, keep * start_grad, 0.0),
            jnp.where(first, jnp.tile(keep, (lag, 1)) * edge_out, 0.0),
        ],
        axis=0,
    )
    small = jnp.transpose(small.reshape(-1, nco, nseq, part), (2, 1, 0, 3))
    small = jnp.pad(small, ((0, 0), (0, 0), (0, 0), (0, span - part)))
    packed = jnp.concatenate([pieces, small], axis=2)
    packed = jnp.concatenate(
        [
            lax.dynamic_slice_in_dim(packed, ((sx - rx) % nsx) * nsc + (sc - rc) % nsc, 1, 0)
            for rc in range(nsc)
            for rx in range(nsx)
        ],
        axis=0,
    ).astype(BF)
    packed = over_chips(over_cores(cut(packed, nsc, 0)), 0)[0]
    packed = over_chunks(after(packed, back_sum), 0)[0]
    both_out = packed[:lines].reshape(2, heads, -1, span)
    small = packed[lines:, :part]

    total = feature_restore(jnp.concatenate([gain_one_part, gain_two_part], axis=0))
    for axis in ("sc", "sx", "cb", "ca"):
        if axis == "cb":
            total = after(total, back_sum)
        total = sum(around(total, axis)[1:], total)
    finish = jnp.concatenate([h_end, ends.astype(F32)], axis=0)
    reach = finish[:, :chunk]
    fill = -reach.size % model
    gathered = total
    for r in range(1, nco):
        piece = finish[:, (nco - r) * chunk : (nco - r + 1) * chunk].reshape(1, -1)
        piece = jnp.pad(piece, ((0, 0), (0, fill))).reshape(-1, model)
        got = shift(jnp.concatenate([total, piece], axis=0), "co", r)
        gathered = gathered + got[:2]
        piece = got[2:].reshape(-1)[: reach.size].reshape(reach.shape)
        reach = jnp.where(co == r - 1, piece, reach)
    total = gathered
    start = (lax.axis_index(("co", "ca", "cb")) * nseq + sx * nsc + sc) * unit
    gain_out = lax.dynamic_slice_in_dim(total, start, unit, 1)

    group_states = reach[:rows][None]
    group_tails = jnp.swapaxes(reach[rows:].reshape(lag, rows, chunk), 0, 1).astype(BF)[None]

    def returned(value):
        return jnp.swapaxes(feature_restore(value).reshape(share, rows, model), 0, 1)

    return (
        returned(mixed),
        returned(tokens_grad),
        gain_out[0],
        gain_out[1],
        recur_out,
        branch_out,
        out_out,
        gate_out,
        up_out,
        down_out,
        both_out[0],
        both_out[1],
        small[0],
        small[1],
        small[2],
        small[3],
        small[4 : 4 + taps],
        small[4 + taps : 4 + taps + rows],
        jnp.swapaxes(small[4 + taps + rows :].reshape(lag, rows, part), 0, 1),
        group_states,
        group_tails,
    )


def solution(mesh):
    nseq, nchan = mesh.devices.shape
    fine = Mesh(
        mesh.devices.reshape(nseq // 2, 2, nchan // PEER, 2, 2), ("sx", "sc", "co", "ca", "cb")
    )
    seq = ("sx", "sc")
    chan = ("co", "ca", "cb")
    place = P(None, seq + chan, None)
    vector = P(chan + seq)
    in_specs = (
        place,
        vector,
        vector,
        P(seq, chan),
        P(seq, chan),
        P(chan, seq),
        P(seq, chan),
        P(seq, chan),
        P(chan, seq),
        P(chan, seq, None),
        P(chan, seq, None),
        vector,
        vector,
        vector,
        vector,
        P(None, chan + seq),
        P(None, chan + seq),
        P(None, None, chan + seq),
        P(),
        place,
    )
    out_specs = (
        place,
        place,
        vector,
        vector,
        P(seq, chan),
        P(seq, chan),
        P(chan, seq),
        P(seq, chan),
        P(seq, chan),
        P(chan, seq),
        P(chan, seq, None),
        P(chan, seq, None),
        vector,
        vector,
        vector,
        vector,
        P(None, chan + seq),
        P(None, chan + seq),
        P(None, None, chan + seq),
        P(seq, None, chan),
        P(seq, None, None, chan),
    )
    return jax.shard_map(shards, mesh=fine, in_specs=in_specs, out_specs=out_specs, check_vma=False)
```

```python
import functools

import jax
import jax.numpy as jnp
from jax import lax
from jax.experimental import pallas as pl
from jax.experimental.pallas import tpu as pltpu
from jax.sharding import Mesh
from jax.sharding import PartitionSpec as P

BF = jnp.bfloat16
F32 = jnp.float32
BLOCKS = ("sx", "sc", "co")
PEERS = ("ca", "cb")
PEER = 4
GELU_C = 0.7978845608028654
GELU_K = 0.044715


def shift(value, axis, step):
    count = lax.axis_size(axis)
    return lax.ppermute(value, axis, [(i, (i + step) % count) for i in range(count)])


def block_shift(value, step):
    count = lax.axis_size(BLOCKS)
    route = [(i, i + step) for i in range(count) if 0 <= i + step < count]
    return lax.ppermute(value, BLOCKS, route)


def peer(value, step):
    return lax.ppermute(value, PEERS, [(i, i ^ step) for i in range(PEER)])


def before_last(value):
    count = lax.axis_size(BLOCKS)
    return sum(
        lax.ppermute(
            value,
            BLOCKS + PEERS,
            [((b - 1) * PEER + PEER - 1, b * PEER + k) for b in range(1, count)],
        )
        for k in range(PEER)
    )


def peer_rows(value, hold=()):
    near = peer(value, 1)
    far = peer(after(value, *hold), 2)
    return [value, near, far, peer(after(far, near), 1)]


def peer_sum(terms, hold=()):
    mine, near, far, across = terms
    across = peer(across, 1)
    near = peer(after(near, across), 1)
    relay = (far.astype(F32) + across.astype(F32)).astype(BF)
    far = peer(after(relay, *hold), 2)
    return mine.astype(F32) + near.astype(F32) + far.astype(F32)


def after(value, *done):
    return lax.optimization_barrier((value, *done))[0]


def around(value, axis):
    return [value] + [shift(value, axis, r) for r in range(1, lax.axis_size(axis))]


def over_die(items):
    return items + [shift(item, "sc", r) for r in range(1, lax.axis_size("sc")) for item in items]


def cut(value, count, axis):
    size = value.shape[axis] // count
    return [lax.slice_in_dim(value, r * size, (r + 1) * size, axis=axis) for r in range(count)]


def around_back(parts, axis):
    return parts[:1] + [shift(part, axis, -1 - r) for r, part in enumerate(parts[1:])]


def sum_around(parts, axis, hold=()):
    total = parts[0].astype(F32)
    for r in range(1, len(parts)):
        term = shift(parts[r].astype(BF), axis, -r)
        total = total + after(term, *hold).astype(F32)
    return total


def chunk_roll(value, step):
    count = lax.axis_size("co")
    step = step % count
    if step == 0:
        return value
    width = value.shape[-1] // count
    cut = width * (count - step)
    return jnp.concatenate([value[..., cut:], value[..., :cut]], axis=-1)


def feature_order(value):
    nsx, nsc = lax.axis_size("sx"), lax.axis_size("sc")
    sx, sc = lax.axis_index("sx"), lax.axis_index("sc")
    width = value.shape[-1] // (nsx * nsc)
    parts = []
    for rc in range(nsc):
        for rx in range(nsx):
            owner = lax.rem(sx - rx + nsx, nsx) * nsc + lax.rem(sc - rc + nsc, nsc)
            parts.append(lax.dynamic_slice_in_dim(value, owner * width, width, value.ndim - 1))
    return jnp.concatenate(parts, axis=-1)


def feature_restore(value):
    nsx, nsc = lax.axis_size("sx"), lax.axis_size("sc")
    sx, sc = lax.axis_index("sx"), lax.axis_index("sc")
    width = value.shape[-1] // (nsx * nsc)
    parts = []
    for owner in range(nsx * nsc):
        rx = lax.rem(sx - owner // nsc + nsx, nsx)
        rc = lax.rem(sc - owner % nsc + nsc, nsc)
        parts.append(
            lax.dynamic_slice_in_dim(value, (rc * nsx + rx) * width, width, value.ndim - 1)
        )
    return jnp.concatenate(parts, axis=-1)


def join_kernel(groups, *refs):
    out = refs[-1]
    width = refs[0].shape[1] // groups
    at = 0
    for g in range(groups):
        for ref in refs[:-1]:
            out[:, at : at + width] = ref[:, g * width : (g + 1) * width]
            at += width


def join_columns(items, groups):
    rows, width = items[0].shape
    block = rows // 2
    return pl.pallas_call(
        functools.partial(join_kernel, groups),
        out_shape=jax.ShapeDtypeStruct((rows, width * len(items)), items[0].dtype),
        grid=(2,),
        in_specs=[pl.BlockSpec((block, width), lambda i: (i, 0))] * len(items),
        out_specs=pl.BlockSpec((block, width * len(items)), lambda i: (i, 0)),
        name="join",
    )(*items)


def compose(earlier, later, rows):
    decay, state = later[:rows], later[rows:]
    return jnp.concatenate([earlier[:rows] * decay, decay * earlier[rows:] + state], axis=0)


def other_blocks(summary, rows, backward):
    width = summary.shape[-1]
    empty = jnp.concatenate([jnp.ones((rows, width), F32), jnp.zeros((rows, width), F32)], axis=0)
    outer = empty
    for axis in ("co", "sc", "sx"):
        count, mine = lax.axis_size(axis), lax.axis_index(axis)
        items = around(summary, axis)
        if axis == "co":
            mark = items[1]
            items = [chunk_roll(item, r) for r, item in enumerate(items)]
        if count == 2:
            mate = items[1]
            ahead = (mine == 0) if backward else (mine == 1)
            joined = compose(mate, summary, rows)
            outer = jnp.where(ahead, compose(mate, outer, rows), outer)
            summary = jnp.where(ahead, joined, compose(summary, mate, rows))
        else:
            table = jnp.stack(items)
            total, inner = empty, empty
            for place in reversed(range(count)) if backward else range(count):
                item = table[lax.rem(mine - place + count, count)]
                total = compose(total, item, rows)
                ahead = (place > mine) if backward else (place < mine)
                inner = jnp.where(ahead, compose(inner, item, rows), inner)
            outer = compose(inner, outer, rows)
            summary = total
    return outer, mark


def matmul(left, right):
    return jnp.dot(left, right, preferred_element_type=F32)


def over_tokens(left, right):
    return lax.dot_general(left, right, (((0,), (0,)), ((), ())), preferred_element_type=F32)


def times_transpose(left, right):
    return lax.dot_general(left, right, (((1,), (1,)), ((), ())), preferred_element_type=F32)


def weight_grad(left, right, halved):
    if halved == 0:
        halves = [over_tokens(half, right).astype(BF) for half in cut(left, 2, 1)]
    else:
        halves = [over_tokens(left, half).astype(BF) for half in cut(right, 2, 1)]
    return [lax.optimization_barrier(half) for half in halves]


def gelu_parts(value):
    square = value * value
    wave = jnp.tanh(GELU_C * (value + GELU_K * value * square))
    half = 0.5 * (1.0 + wave)
    slope = half + 0.5 * value * (1.0 - wave * wave) * (GELU_C * (1.0 + 3.0 * GELU_K * square))
    return value * half, slope


def minus_expm1(value):
    series = 1.0 + value * (1.0 / 7.0)
    for order in (6.0, 5.0, 4.0, 3.0, 2.0):
        series = 1.0 + value * (1.0 / order) * series
    return -jnp.where(value > -0.3, value * series, jnp.exp(value) - 1.0)


def decay_terms(rate, soft):
    log_decay = -8.0 * rate * soft
    return jnp.exp(log_decay), jnp.sqrt(minus_expm1(2.0 * log_decay))


def rows_times(values, pieces, columns=slice(None)):
    total = None
    size = pieces[0].shape[0]
    for i, piece in enumerate(pieces):
        term = matmul(values[:, i * size : (i + 1) * size], piece[:, columns])
        total = term if total is None else total + term
    return total


def columns_times(values, pieces):
    total = None
    size = pieces[0].shape[1]
    for i, piece in enumerate(pieces):
        term = times_transpose(values[:, i * size : (i + 1) * size], piece[...])
        total = term if total is None else total + term
    return total


def gates_kernel(
    count, here, x_ref, border_ref, gain_ref, tail_ref, gate_ref, vec_ref, *refs
):
    pieces, refs = refs[:count], refs[count:]
    n_ref, u_ref, v_ref, ra_ref, ri_ref, a_ref, e_ref, before_ref, end_ref, pad, held = refs
    step = pl.program_id(0)
    rows = held.shape[0] // 2
    size, width = u_ref.shape
    lag = tail_ref.shape[0]

    def normal(value):
        value = value.astype(F32)
        root = lax.rsqrt(jnp.mean(value * value, axis=-1, keepdims=True) + 1e-06)
        return (value * root * gain_ref[...]).astype(BF)

    @pl.when(step == 0)
    def _():
        edge = rows_times(normal(border_ref[...]), pieces).astype(BF).astype(F32)
        pad[0:lag, :] = jnp.where(here[1] == 1, tail_ref[...].astype(BF).astype(F32), edge)
        held[0:rows, :] = jnp.ones((rows, width), F32)
        held[rows:, :] = jnp.zeros((rows, width), F32)

    @pl.when(step > 0)
    def _():
        pad[0:lag, :] = pad[size : size + lag, :]

    low = normal(x_ref[...])
    n_ref[...] = low
    conv_in = rows_times(low, pieces).astype(BF)
    u_ref[...] = conv_in
    pad[lag:, :] = conv_in.astype(F32)
    before_ref[...] = pad[0:lag, :]
    taps = lag // rows + 1
    conv = vec_ref[taps : taps + 1, :] + vec_ref[0:1, :] * pad[lag : lag + size, :]
    for k in range(1, taps):
        conv = conv + vec_ref[k : k + 1, :] * pad[lag - rows * k : lag - rows * k + size, :]
    low = conv.astype(BF)
    v_ref[...] = low
    pre = jnp.dot(low, gate_ref[...], preferred_element_type=F32)
    ra = jax.nn.sigmoid(pre[:, :width] + vec_ref[taps + 1 : taps + 2, :])
    ri = jax.nn.sigmoid(pre[:, width:] + vec_ref[taps + 2 : taps + 3, :])
    decay, root = decay_terms(ra, vec_ref[taps + 3 : taps + 4, :])
    ra_ref[...] = ra
    ri_ref[...] = ri
    a_ref[...] = decay
    e_ref[...] = low.astype(F32) * ri * root
    prod = held[0:rows, :]
    state = held[rows:, :]
    for t in range(size // rows):
        now = a_ref[t * rows : (t + 1) * rows, :]
        state = now * state + e_ref[t * rows : (t + 1) * rows, :]
        prod = prod * now
    held[0:rows, :] = prod
    held[rows:, :] = state
    end_ref[0:rows, :] = prod
    end_ref[rows:, :] = state


def branch_kernel(count, n_ref, *refs):
    refs[count][...] = rows_times(n_ref[...], refs[:count])


def states_kernel(place, a_ref, e_ref, yp_ref, enter_ref, h_ref, z_ref, before_ref, end_ref, held):
    step = pl.program_id(0)
    rows = held.shape[0]

    @pl.when(step == 0)
    def _():
        held[...] = enter_ref[...]

    state = held[...]
    before_ref[...] = state
    for t in range(a_ref.shape[0] // rows):
        at = slice(t * rows, (t + 1) * rows)
        state = a_ref[at, :] * state + e_ref[at, :]
        h_ref[at, :] = state
    held[...] = state
    end_ref[...] = state
    act, _ = gelu_parts(yp_ref[...])
    z_ref[...] = (h_ref[...] * act).astype(BF)


def back_kernel(count, place, g_ref, yp_ref, h_ref, a_ref, *refs):
    pieces = refs[:count]
    dh_ref, dyp_ref, end_ref, held = refs[count:]
    step = pl.program_id(0)
    rows = held.shape[0]

    @pl.when(step == 0)
    def _():
        held[...] = jnp.zeros(held.shape, F32)

    act, slope = gelu_parts(yp_ref[...])
    dz = columns_times(g_ref[...], pieces)
    dh_ref[...] = dz * act
    dyp_ref[...] = (dz * h_ref[...] * slope).astype(BF)
    carry = held[...]
    for t in reversed(range(a_ref.shape[0] // rows)):
        at = slice(t * rows, (t + 1) * rows)
        carry = a_ref[at, :] * (dh_ref[at, :] + carry)
    held[...] = carry
    end_ref[...] = carry


def mlp_kernel(count, n_ref, dy_ref, *refs):
    gates, ups, downs = refs[:count], refs[count : 2 * count], refs[2 * count : 3 * count]
    m_ref, dg_ref, du_ref = refs[3 * count :]
    gate = rows_times(n_ref[...], gates)
    up = rows_times(n_ref[...], ups)
    grad = columns_times(dy_ref[...], downs)
    act, slope = gelu_parts(gate)
    m_ref[...] = (act * up).astype(BF)
    dg_ref[...] = (grad * up * slope).astype(BF)
    du_ref[...] = (grad * act).astype(BF)


def product_kernel(count, per, x_ref, *refs):
    out_ref = refs[count]
    step = pl.program_id(0)
    for i in range(count):

        @pl.when(step // per == i)
        def _():
            out_ref[...] = matmul(x_ref[...], refs[i][...]).astype(BF)


def transposed_kernel(count, per, x_ref, y_ref, *refs):
    out_ref = refs[2 * count]
    step = pl.program_id(0)
    for i in range(count):

        @pl.when(step // per == i)
        def _():
            out_ref[...] = (
                times_transpose(x_ref[...], refs[i][...])
                + times_transpose(y_ref[...], refs[count + i][...])
            ).astype(BF)


def grads_kernel(
    place, dh_ref, a_ref, ra_ref, ri_ref, v_ref, h_ref, hb_ref, u_ref, ub_ref, gate_ref, vec_ref,
    late_ref, gates_ref, du_ref, edge_ref, last_ref, sums_ref, end_ref, held, pad, spad, hpad, upad,
):
    step = pl.program_id(0)
    rows = held.shape[0]
    size = dh_ref.shape[0]
    width = dh_ref.shape[1]
    lag = ub_ref.shape[0]
    taps = lag // rows + 1

    @pl.when(step == 0)
    def _():
        held[...] = late_ref[...]
        pad[size:, :] = jnp.zeros((lag, width), F32)
        sums_ref[...] = jnp.zeros(sums_ref.shape, F32)

    @pl.when(step > 0)
    def _():
        pad[size:, :] = pad[0:lag, :]

    carry = held[...]
    for t in reversed(range(size // rows)):
        at = slice(t * rows, (t + 1) * rows)
        now = dh_ref[at, :] + carry
        spad[at, :] = now
        carry = a_ref[at, :] * now
    held[...] = carry
    end_ref[...] = carry
    hpad[0:rows, :] = hb_ref[...]
    hpad[rows:, :] = h_ref[...]
    upad[0:lag, :] = ub_ref[...]
    upad[lag:, :] = u_ref[...].astype(F32)
    s = spad[...]
    ra = ra_ref[...]
    ri = ri_ref[...]
    soft = vec_ref[taps + 3 : taps + 4, :]
    decay, root = decay_terms(ra, soft)
    v = v_ref[...].astype(F32)
    sv = s * v
    grad_log = decay * (s * hpad[0:size, :] - sv * ri * decay / root)
    rated = grad_log * ra
    dap = (-8.0 * soft * rated * (1.0 - ra)).astype(BF)
    dip = (sv * root * ri * (1.0 - ri)).astype(BF)
    gates_ref[:, :width] = dap
    gates_ref[:, width:] = dip
    dv = s * ri * root + lax.dot_general(
        gates_ref[...], gate_ref[...], (((1,), (1,)), ((), ())), preferred_element_type=F32
    )
    pad[0:size, :] = dv

    def fold(value):
        return jnp.sum(value.reshape(size // rows, rows, width), axis=0)

    terms = [dap.astype(F32), dip.astype(F32), rated, dv]
    terms = terms + [dv * upad[lag - rows * k : lag - rows * k + size, :] for k in range(taps)]
    for i, term in enumerate(terms):
        sums_ref[i * rows : (i + 1) * rows, :] += fold(term)
    du = vec_ref[0:1, :] * dv
    for k in range(1, taps):
        du = du + vec_ref[k : k + 1, :] * pad[rows * k : rows * k + size, :]
    du_ref[...] = du.astype(BF)

    @pl.when(step == 0)
    def _():
        last_ref[...] = du[size - lag :, :]

    for t in range(taps - 1):
        row = jnp.zeros((rows, width), F32)
        for k in range(taps - 1 - t, taps):
            at = (t + k - (taps - 1)) * rows
            row = row + vec_ref[k : k + 1, :] * pad[at : at + rows, :]
        edge_ref[t * rows : (t + 1) * rows, :] = row


def gate_matrix_kernel(blocks_ref, out_ref):
    kinds, heads, span, _ = blocks_ref.shape
    out_ref[...] = jnp.zeros(out_ref.shape, BF)
    for g in range(kinds):
        for h in range(heads):
            at = (g * heads + h) * span
            out_ref[h * span : (h + 1) * span, at : at + span] = blocks_ref[g, h]


def gate_matrix(blocks):
    kinds, heads, span, _ = blocks.shape
    return pl.pallas_call(
        gate_matrix_kernel,
        out_shape=jax.ShapeDtypeStruct((heads * span, kinds * heads * span), BF),
        name="gate_matrix",
    )(blocks)


def whole(shape):
    return pl.BlockSpec(shape, lambda *_: (0,) * len(shape))


def gates_call(place, x, border, gain, tail, gate, vec, pieces, rows):
    steps, size, model = x.shape
    lag, width = tail.shape
    wide = pieces[0].shape[0]
    here = pl.BlockSpec((None, size, width), lambda j, c: (j, 0, 0))
    full = jax.ShapeDtypeStruct((steps, size, width), F32)
    low = jax.ShapeDtypeStruct((steps, size, width), BF)
    rowed = pl.BlockSpec((None, size, model), lambda j, c: (j ^ c[0], 0, 0))
    return pl.pallas_call(
        functools.partial(gates_kernel, len(pieces)),
        out_shape=(
            jax.ShapeDtypeStruct(x.shape, BF),
            low,
            low,
            full,
            full,
            full,
            full,
            jax.ShapeDtypeStruct((steps, lag, width), F32),
            jax.ShapeDtypeStruct((2 * rows, width), F32),
        ),
        grid_spec=pltpu.PrefetchScalarGridSpec(
            num_scalar_prefetch=1,
            grid=(steps,),
            in_specs=[
                rowed,
                whole(border.shape),
                whole(gain.shape),
                whole(tail.shape),
                whole(gate.shape),
                whole(vec.shape),
            ]
            + [pl.BlockSpec((wide, width), lambda j, c: (0, 0))] * len(pieces),
            out_specs=[
                rowed,
                here,
                here,
                here,
                here,
                here,
                here,
                pl.BlockSpec((None, lag, width), lambda j, c: (j, 0, 0)),
                whole((2 * rows, width)),
            ],
            scratch_shapes=[
                pltpu.VMEM((size + lag, width), F32),
                pltpu.VMEM((2 * rows, width), F32),
            ],
        ),
        name="gates",
    )(place, x, border, gain, tail, gate, vec, *pieces)


def branch_call(n, pieces):
    steps, size, model = n.shape
    wide, width = pieces[0].shape
    return pl.pallas_call(
        functools.partial(branch_kernel, len(pieces)),
        out_shape=jax.ShapeDtypeStruct((steps, size, width), F32),
        grid=(steps,),
        in_specs=[pl.BlockSpec((None, size, model), lambda j: (j, 0, 0))]
        + [whole((wide, width))] * len(pieces),
        out_specs=pl.BlockSpec((None, size, width), lambda j: (j, 0, 0)),
        name="branch",
    )(n, *pieces)


def states_call(place, a, e, yp, enter):
    steps, size, width = a.shape
    rows = enter.shape[0]
    here = pl.BlockSpec((None, size, width), lambda j, c: (j, 0, 0))
    there = pl.BlockSpec((None, size, width), lambda j, c: (j ^ c[0], 0, 0))
    return pl.pallas_call(
        states_kernel,
        out_shape=(
            jax.ShapeDtypeStruct((steps, size, width), F32),
            jax.ShapeDtypeStruct((steps, size, width), BF),
            jax.ShapeDtypeStruct((steps, rows, width), F32),
            jax.ShapeDtypeStruct((rows, width), F32),
        ),
        grid_spec=pltpu.PrefetchScalarGridSpec(
            num_scalar_prefetch=1,
            grid=(steps,),
            in_specs=[here, here, there, whole((rows, width))],
            out_specs=[
                here,
                there,
                pl.BlockSpec((None, rows, width), lambda j, c: (j, 0, 0)),
                whole((rows, width)),
            ],
            scratch_shapes=[pltpu.VMEM((rows, width), F32)],
        ),
        name="states",
    )(place, a, e, yp, enter)


def back_call(place, g, yp, h, a, pieces, rows):
    steps, size, width = a.shape
    last = steps - 1
    here = pl.BlockSpec((None, size, width), lambda j, c: (last - j, 0, 0))
    there = pl.BlockSpec((None, size, width), lambda j, c: ((last - j) ^ c[0], 0, 0))
    return pl.pallas_call(
        functools.partial(back_kernel, len(pieces)),
        out_shape=(
            jax.ShapeDtypeStruct((steps, size, width), F32),
            jax.ShapeDtypeStruct((steps, size, width), BF),
            jax.ShapeDtypeStruct((rows, width), F32),
        ),
        grid_spec=pltpu.PrefetchScalarGridSpec(
            num_scalar_prefetch=1,
            grid=(steps,),
            in_specs=[
                pl.BlockSpec((None, size, g.shape[2]), lambda j, c: ((last - j) ^ c[0], 0, 0)),
                there,
                here,
                here,
            ]
            + [whole(pieces[0].shape)] * len(pieces),
            out_specs=[here, there, whole((rows, width))],
            scratch_shapes=[pltpu.VMEM((rows, width), F32)],
        ),
        name="back",
    )(place, g, yp, h, a, *pieces)


def grads_call(place, dh, a, ra, ri, v, h, h_before, u, u_before, gate, vec, late):
    steps, size, width = a.shape
    rows = late.shape[0]
    lag = u_before.shape[1]
    last = steps - 1
    count = lag // rows + 5
    here = pl.BlockSpec((None, size, width), lambda j, c: (last - j, 0, 0))
    there = pl.BlockSpec((None, size, width), lambda j, c: ((last - j) ^ c[0], 0, 0))
    small = lambda size: pl.BlockSpec((None, size, width), lambda j, c: (last - j, 0, 0))
    return pl.pallas_call(
        grads_kernel,
        out_shape=(
            jax.ShapeDtypeStruct((steps, size, 2 * width), BF),
            jax.ShapeDtypeStruct((steps, size, width), BF),
            jax.ShapeDtypeStruct((lag, width), F32),
            jax.ShapeDtypeStruct((lag, width), F32),
            jax.ShapeDtypeStruct((count * rows, width), F32),
            jax.ShapeDtypeStruct((rows, width), F32),
        ),
        grid_spec=pltpu.PrefetchScalarGridSpec(
            num_scalar_prefetch=1,
            grid=(steps,),
            in_specs=[
            here,
            here,
            here,
            here,
            here,
            here,
            small(rows),
            here,
            small(lag),
            whole(gate.shape),
            whole(vec.shape),
            whole(late.shape),
        ],
        out_specs=[
            pl.BlockSpec((None, size, 2 * width), lambda j, c: (last - j, 0, 0)),
            there,
            whole((lag, width)),
            whole((lag, width)),
            whole((count * rows, width)),
            whole((rows, width)),
        ],
        scratch_shapes=[
            pltpu.VMEM((rows, width), F32),
            pltpu.VMEM((size + lag, width), F32),
            pltpu.VMEM((size, width), F32),
            pltpu.VMEM((size + rows, width), F32),
            pltpu.VMEM((size + lag, width), F32),
        ],
        ),
        name="grads",
    )(place, dh, a, ra, ri, v, h, h_before, u, u_before, gate, vec, late)


def tile_of(size, most):
    return max(t for t in range(128, most + 1, 128) if size % t == 0)


def mlp_call(n, dy, gates, ups, downs):
    tokens, model = n.shape
    wide, units = gates[0].shape
    tile = tile_of(units, 256)
    count = len(gates)
    out = pl.BlockSpec((tokens, tile), lambda j: (0, j))
    return pl.pallas_call(
        functools.partial(mlp_kernel, count),
        out_shape=[jax.ShapeDtypeStruct((tokens, units), BF)] * 3,
        grid=(units // tile,),
        in_specs=[whole((tokens, model))] * 2
        + [pl.BlockSpec((wide, tile), lambda j: (0, j))] * (2 * count)
        + [pl.BlockSpec((tile, wide), lambda j: (j, 0))] * count,
        out_specs=[out] * 3,
        name="mlp",
    )(n, dy, *gates, *ups, *downs)


def clipped(step, per, i):
    return jnp.clip(step - i * per, 0, per - 1)


def product_call(x, pieces, size=None, at=0):
    depth = x.shape[1]
    tokens = size or x.shape[0]
    wide = pieces[0].shape[1]
    tile = tile_of(wide, 512)
    per, count = wide // tile, len(pieces)
    return pl.pallas_call(
        functools.partial(product_kernel, count, per),
        out_shape=jax.ShapeDtypeStruct((tokens, wide * count), BF),
        grid=(per * count,),
        in_specs=[pl.BlockSpec((tokens, depth), lambda s: (at, 0))]
        + [
            pl.BlockSpec((depth, tile), lambda s, i=i: (0, clipped(s, per, i)))
            for i in range(count)
        ],
        out_specs=pl.BlockSpec((tokens, tile), lambda s: (0, s)),
        name="product",
    )(x, *pieces)


def transposed_call(x, y, first, second, size=None, at=0):
    depth = x.shape[1]
    tokens = size or x.shape[0]
    wide = first[0].shape[0]
    tile = tile_of(wide, 256)
    per, count = wide // tile, len(first)
    return pl.pallas_call(
        functools.partial(transposed_kernel, count, per),
        out_shape=jax.ShapeDtypeStruct((tokens, wide * count), BF),
        grid=(per * count,),
        in_specs=[pl.BlockSpec((tokens, depth), lambda s: (at, 0))] * 2
        + [
            pl.BlockSpec((tile, depth), lambda s, i=i: (clipped(s, per, i), 0))
            for i in range(count)
        ]
        * 2,
        out_specs=pl.BlockSpec((tokens, tile), lambda s: (0, s)),
        name="transposed",
    )(x, y, *first, *second)


def norm_back(grad_norm, normed, inv_root, gain):
    scaled = grad_norm * gain
    mean_term = jnp.mean(scaled * normed, axis=-1, keepdims=True)
    return inv_root * (scaled - normed * mean_term)


def inverse_rms(value):
    return lax.rsqrt(jnp.mean(value * value, axis=-1, keepdims=True) + 1e-06)


def shards(
    tokens,
    norm_gain,
    mlp_gain,
    recur_proj,
    branch_proj,
    out_proj,
    gate_proj,
    up_proj,
    down_proj,
    recur_gate,
    input_gate,
    recur_bias,
    input_bias,
    decay_param,
    conv_bias,
    conv_weight,
    init_state,
    init_tail,
    reset_flags,
    cotangent,
):
    nsx, nsc, nco = (lax.axis_size(name) for name in BLOCKS)
    nseq = nsx * nsc
    co = lax.axis_index("co")
    first = lax.axis_index(BLOCKS) == 0
    ci = lax.axis_index(PEERS)
    place = jnp.stack([ci, first]).astype(jnp.int32)
    rows, share, model = tokens.shape
    own = rows * share
    group = PEER * own
    taps = conv_weight.shape[0]
    lag = taps - 1
    part = conv_bias.shape[0]
    chunk = part * nseq
    width = chunk * nco
    keep = (1 - reset_flags).astype(F32)[:, None]
    heads, span = recur_gate.shape[0], recur_gate.shape[2]
    unit = norm_gain.shape[0]
    sx, sc = lax.axis_index("sx"), lax.axis_index("sc")

    def owned(value):
        return feature_order(jnp.swapaxes(value, 0, 1).reshape(own, model))

    mine = owned(tokens)
    border = jnp.swapaxes(tokens[:, share - lag :], 0, 1).reshape(lag * rows, model)
    border = feature_order(before_last(border))

    vectors = jnp.concatenate(
        [
            conv_weight,
            conv_bias[None],
            recur_bias[None],
            input_bias[None],
            decay_param[None],
            init_state,
            jnp.swapaxes(init_tail, 0, 1).reshape(lag * rows, part),
        ],
        axis=0,
    )
    both = jnp.stack([recur_gate, input_gate]).reshape(-1, span)
    lines, lists = both.shape[0], vectors.shape[0]
    gains = jnp.stack([norm_gain, mlp_gain])
    gains_got = [peer(gains, k) for k in range(1, PEER)]
    packed = jnp.concatenate(
        [
            both,
            jnp.pad(vectors, ((0, 0), (0, span - part))),
            jnp.pad(
                jnp.concatenate([gains] + gains_got, axis=0),
                ((0, 0), (0, span - unit)),
            ),
        ],
        axis=0,
    )
    x_near = peer(after(mine, *gains_got), 1)
    table = around(packed[None], "co")
    x_far = peer(after(mine, *gains_got), 2)
    x_across = peer(after(x_far, x_near), 1)
    table = around(jnp.concatenate(table, axis=0), "sx")
    ready = table[1:]
    table = jnp.concatenate(table, axis=0)
    table = jnp.concatenate(around(table, "sc"), axis=0)

    links = {"co": ready, "sx": ready}

    def travel(value, axis):
        items = around(after(value, *links[axis]), axis)
        links[axis] = items[1:]
        return items

    def gather(shard):
        return over_die(travel(join_columns(travel(shard, "co"), 1), "sx"))

    recur_chunks = travel(recur_proj, "co")
    x_all = [mine, x_near, x_far, x_across]
    recur_rows = travel(join_columns(recur_chunks, 1), "sx")
    recur_pieces = over_die(recur_rows)
    branch_chunks = travel(branch_proj, "co")
    out_chunks = travel(out_proj, "co")
    grad_mine = owned(cotangent)
    grad_near = peer(after(grad_mine, x_across), 1)
    x_all = after(jnp.stack(x_all), *branch_chunks[1:])
    branch_chunks[1:] = [after(item, *recur_rows[1:]) for item in branch_chunks[1:]]
    branch_rows = travel(join_columns(branch_chunks, 1), "sx")
    branch_pieces = over_die(branch_rows)

    gains = table[:, lines + lists :, :unit].reshape(-1, PEER, 2 * unit)
    gains = jnp.swapaxes(gains, 0, 1).reshape(-1, 2 * unit)
    lot = jnp.arange(model // unit)
    rel = lot // (model // unit // nseq)
    here_seq = ((sx - rel % nsx) % nsx) * nsc + (sc - rel // nsx) % nsc
    whole_unit = here_seq * (model // unit // nseq) + lot % (model // unit // nseq)
    from_chan, from_seq = whole_unit // nseq, whole_unit % nseq
    source = ((from_chan % PEER) ^ lax.axis_index(PEERS)) * nsc + (sc - from_seq % nsc) % nsc
    source = source * nsx + (sx - from_seq // nsc) % nsx
    source = source * nco + (co - from_chan // PEER) % nco
    pick = (source[:, None] == jnp.arange(model // unit)[None, :]).astype(F32)
    gains = jnp.dot(pick, gains.astype(F32), precision=lax.Precision.HIGHEST)
    gain_one = gains[:, :unit].reshape(1, model)
    gain_two = gains[:, unit:].reshape(1, model)

    table = table[:, : lines + lists].reshape(nseq, nco, lines + lists, span)
    table = jnp.concatenate(
        [
            lax.dynamic_slice_in_dim(
                table, ((sc - s % nsc) % nsc) * nsx + (sx - s // nsc) % nsx, 1, 0
            )
            for s in range(nseq)
        ],
        axis=0,
    )
    vectors = table[:, :, lines:, :part]
    vectors = jnp.transpose(vectors, (2, 1, 0, 3)).reshape(-1, width).astype(F32)
    decay32 = vectors[taps + 3 : taps + 4]
    vec = jnp.concatenate([vectors[: taps + 3], jax.nn.softplus(-decay32)], axis=0)
    vec = jnp.pad(vec, ((0, -vec.shape[0] % 8), (0, 0)))
    state_start = vectors[taps + 4 : taps + 4 + rows] * keep
    tail_start = vectors[taps + 4 + rows :] * jnp.tile(keep, (lag, 1))
    both = table[:, :, :lines].reshape(nseq, nco, 2, heads, -1, span)
    both = jnp.transpose(both, (2, 1, 3, 0, 4, 5)).reshape(2, nco * heads, span, span)
    gate = gate_matrix(both)

    normal_in, u, v, ra, ri, decay, drive, u_before, summary = gates_call(
        place, x_all, border, gain_one, tail_start, gate, vec, recur_pieces, rows
    )
    ends = u[PEER - 1, own - lag * rows :]
    outer, mark = other_blocks(after(summary, *branch_rows[1:]), rows, False)
    enter = outer[:rows] * state_start + outer[rows:]
    out_rows = travel(jnp.concatenate(out_chunks, axis=0), "sx")
    out_pieces = over_die(out_rows)
    yp = branch_call(normal_in, branch_pieces)
    grad_far = peer(after(grad_mine, mark), 2)
    grad_full = jnp.concatenate([grad_mine, grad_near, grad_far, peer(grad_far, 1)], axis=0)

    gate_chunks, up_chunks, down_chunks = (
        around(after(shard, mark), "co") for shard in (gate_proj, up_proj, down_proj)
    )

    h, z, h_before, h_end = states_call(place, decay, drive, yp, after(enter, grad_near, *out_rows[1:]))
    z_rows = after(z, *gate_chunks[1:]).reshape(group, width)
    last_term = product_call(z_rows, out_pieces, own, PEER - 1)
    z_rows, last_term = lax.optimization_barrier((z_rows, last_term))
    branch = product_call(z_rows, out_pieces, own * (PEER - 1))
    terms = cut(branch, PEER - 1, 0) + [last_term]
    cross = peer(terms[3], 1)
    near = peer(after(terms[1], cross), 1)
    relay = (terms[2].astype(F32) + cross.astype(F32)).astype(BF)
    far = peer(after(relay, *up_chunks[1:]), 2)
    gate_pieces = over_die(travel(join_columns(gate_chunks, 1), "sx"))
    resid = mine.astype(F32) + terms[0].astype(F32) + near.astype(F32) + far.astype(F32)
    up_pieces = over_die(travel(join_columns(up_chunks, 1), "sx"))

    inv_two = inverse_rms(resid)
    normed_two = resid * inv_two
    normal_mine = after((normed_two * gain_two).astype(BF), *down_chunks[1:])
    normal_near, normal_far = peer(normal_mine, 1), peer(normal_mine, 2)
    normal_across = peer(after(normal_far, normal_near, grad_full), 1)
    normal_group = [normal_mine, normal_near, normal_far, normal_across]
    normal_mid = jnp.concatenate(normal_group, axis=0)
    down_pieces = over_die(travel(jnp.concatenate(down_chunks, axis=0), "sx"))
    hidden, grad_gate, grad_up = mlp_call(
        normal_mid, grad_full, gate_pieces, up_pieces, down_pieces
    )
    def over_cores(halves):
        return sum_around(halves, "sc").astype(BF)

    def over_chips(grad, axis):
        return sum_around(cut(grad, nsx, axis), "sx").astype(BF)

    def over_chunks(grad, axis, *hold):
        return sum_around(cut(grad, nco, axis), "co", hold)

    down_grad = over_cores(weight_grad(hidden, grad_full, 1))
    grad_gate, grad_up, down_grad = lax.optimization_barrier((grad_gate, grad_up, down_grad))
    last_term = transposed_call(
        grad_gate, grad_up, gate_pieces, up_pieces, own, PEER - 1
    )
    grad_gate, last_term = lax.optimization_barrier((grad_gate, last_term))
    mid = transposed_call(grad_gate, grad_up, gate_pieces, up_pieces, own * (PEER - 1))
    terms = cut(mid, PEER - 1, 0) + [last_term]
    cross = peer(terms[3], 1)
    relay = (terms[2].astype(F32) + cross.astype(F32)).astype(BF)
    down_grad = over_chips(down_grad, 1)
    near = peer(after(terms[1], cross), 1)
    far = peer(relay, 2)
    normal_late = after(normal_mid, cross)
    up_grad = over_cores(weight_grad(normal_late, grad_up, 0))
    gate_grad = over_cores(weight_grad(normal_late, grad_gate, 0))
    up_grad = over_chips(after(up_grad, down_grad), 0)
    down_last = around_back(cut(down_grad, nco, 0), "co")
    mid_sum = terms[0].astype(F32) + near.astype(F32) + far.astype(F32)
    mid_sum = after(mid_sum, gate_grad, down_grad)
    mlp = product_call(after(hidden, mid_sum), down_pieces)
    gate_grad = over_chips(after(gate_grad, up_grad), 0)
    gain_two_part = jnp.sum(mid_sum * normed_two, axis=0, keepdims=True)
    resid_grad = grad_mine.astype(F32) + norm_back(mid_sum, normed_two, inv_two, gain_two)
    resid_mine = resid_grad.astype(BF)
    resid_near, resid_far = peer(resid_mine, 1), peer(resid_mine, 2)
    resid_across = peer(after(resid_far, resid_near), 1)
    resid_all = jnp.stack([resid_mine, resid_near, resid_far, resid_across])

    dh, grad_branch, local_end = back_call(place, resid_all, yp, h, decay, out_pieces, rows)
    mlp_terms = cut(after(mlp, resid_all), PEER, 0)
    mlp_cross = peer(mlp_terms[3], 1)
    mlp_near = peer(after(mlp_terms[1], mlp_cross), 1)
    local_end = after(local_end, mlp_cross, gate_grad)
    late, mark = other_blocks(jnp.concatenate([summary[:rows], local_end], axis=0), rows, True)
    late = late[rows:]
    relay = (mlp_terms[2].astype(F32) + mlp_cross.astype(F32)).astype(BF)
    mlp_far = peer(after(relay, mark), 2)
    up_last = around_back(cut(after(up_grad, mark), nco, 1), "co")
    gate_last = around_back(cut(after(gate_grad, mlp_far), nco, 1), "co")
    mlp_sum = mlp_terms[0].astype(F32) + mlp_near.astype(F32) + mlp_far.astype(F32)
    mixed = (resid + mlp_sum).astype(BF)
    gates_low, grad_u, edge_out, last, sums, start_grad = grads_call(
        place, dh, decay, ra, ri, v, h, h_before, u, u_before, gate, vec, late
    )
    edge_in = chunk_roll(block_shift(edge_out, -1), -1)
    grad_branch, resid_late = lax.optimization_barrier(
        (grad_branch, resid_all, edge_out, mlp_far)
    )[:2]
    grad_branch = grad_branch.reshape(group, width)
    normal_rows = normal_in.reshape(group, model)
    out_grad = over_cores(weight_grad(z_rows, resid_late.reshape(group, model), 1))
    branch_grad = over_cores(weight_grad(normal_rows, grad_branch, 0))
    fixed = (last + edge_in).astype(BF)[None]
    grad_u = lax.dynamic_update_slice(
        grad_u, fixed, (lax.bitwise_xor(ci, PEER - 1), own - lag * rows, 0)
    )
    grad_u = after(grad_u, mlp_near, *up_last[1:]).reshape(group, width)
    last_term = transposed_call(grad_u, grad_branch, recur_pieces, branch_pieces, own, PEER - 1)
    grad_u, last_term = lax.optimization_barrier((grad_u, last_term))
    back = transposed_call(
        grad_u, grad_branch, recur_pieces, branch_pieces, own * (PEER - 1)
    )
    terms = cut(back, PEER - 1, 0) + [last_term]
    cross = peer(terms[3], 1)
    near = peer(after(terms[1], cross, out_grad, branch_grad), 1)
    relay = (terms[2].astype(F32) + cross.astype(F32)).astype(BF)
    out_grad = over_chips(out_grad, 1)
    far = peer(relay, 2)
    out_last = around_back(cut(out_grad, nco, 0), "co")
    back_sum = terms[0].astype(F32) + near.astype(F32) + far.astype(F32)
    both_grad = over_tokens(v.reshape(group, width), gates_low.reshape(group, 2 * width))
    recur_grad = over_cores(weight_grad(normal_rows, after(grad_u, cross), 0))
    branch_grad = over_chips(branch_grad, 0)
    back_sum = after(back_sum, branch_grad, recur_grad)
    value = mine.astype(F32)
    inv_one = inverse_rms(value)
    normed_one = value * inv_one
    x_value = after(x_all, cross).astype(F32)
    x_value = x_value * inverse_rms(x_value)
    gain_one_part = sum(
        jnp.sum(terms[k].astype(F32) * x_value[k], axis=0, keepdims=True) for k in range(PEER)
    )
    tokens_grad = resid_grad + norm_back(back_sum, normed_one, inv_one, gain_one)

    down_out = sum(after(item, late).astype(F32) for item in down_last)
    up_out = sum(item.astype(F32) for item in up_last)
    gate_out = sum(after(item, far).astype(F32) for item in gate_last)
    out_out = sum(item.astype(F32) for item in out_last)
    held = recur_grad
    recur_grad = over_chips(recur_grad, 0)
    branch_out = over_chunks(branch_grad, 1, back_sum)
    recur_out = over_chunks(recur_grad, 1)

    pieces = jnp.stack(
        [
            both_grad[span * h : span * (h + 1), g * width + span * h : g * width + span * (h + 1)]
            for g in range(2)
            for h in range(nco * heads)
        ]
    )
    pieces = pieces.reshape(2, nco, heads, nseq, -1, span)
    pieces = jnp.transpose(pieces, (3, 1, 0, 2, 4, 5)).reshape(nseq, nco, -1, span)
    sums = jnp.sum(sums.reshape(-1, rows, width), axis=1)
    small = jnp.concatenate(
        [
            sums[0:2],
            sums[2:3] * 8.0 * jax.nn.sigmoid(-decay32),
            sums[3:],
            jnp.where(first, keep * start_grad, 0.0),
            jnp.where(first, jnp.tile(keep, (lag, 1)) * edge_out, 0.0),
        ],
        axis=0,
    )
    small = jnp.transpose(small.reshape(-1, nco, nseq, part), (2, 1, 0, 3))
    small = jnp.pad(small, ((0, 0), (0, 0), (0, 0), (0, span - part)))
    packed = jnp.concatenate([pieces, small], axis=2)
    packed = jnp.concatenate(
        [
            lax.dynamic_slice_in_dim(packed, ((sx - rx) % nsx) * nsc + (sc - rc) % nsc, 1, 0)
            for rc in range(nsc)
            for rx in range(nsx)
        ],
        axis=0,
    ).astype(BF)
    packed = over_chips(over_cores(cut(packed, nsc, 0)), 0)[0]
    packed = over_chunks(after(packed, back_sum), 0)[0]
    both_out = packed[:lines].reshape(2, heads, -1, span)
    small = packed[lines:, :part]

    total = feature_restore(jnp.concatenate([gain_one_part, gain_two_part], axis=0))
    for axis in ("sc", "sx", "cb", "ca"):
        if axis == "cb":
            total = after(total, back_sum, *out_last[1:])
        total = sum(around(total, axis)[1:], total)
    finish = jnp.concatenate([h_end, ends.astype(F32)], axis=0)
    reach = finish[:, :chunk]
    fill = -reach.size % model
    gathered = total
    for r in range(1, nco):
        piece = finish[:, (nco - r) * chunk : (nco - r + 1) * chunk].reshape(1, -1)
        piece = jnp.pad(piece, ((0, 0), (0, fill))).reshape(-1, model)
        got = shift(jnp.concatenate([total, piece], axis=0), "co", r)
        gathered = gathered + got[:2]
        piece = got[2:].reshape(-1)[: reach.size].reshape(reach.shape)
        reach = jnp.where(co == r - 1, piece, reach)
    total = gathered
    start = (lax.axis_index(("co", "ca", "cb")) * nseq + sx * nsc + sc) * unit
    gain_out = lax.dynamic_slice_in_dim(total, start, unit, 1)

    group_states = reach[:rows][None]
    group_tails = jnp.swapaxes(reach[rows:].reshape(lag, rows, chunk), 0, 1).astype(BF)[None]

    def returned(value):
        return jnp.swapaxes(feature_restore(value).reshape(share, rows, model), 0, 1)

    return (
        returned(mixed),
        returned(tokens_grad),
        gain_out[0],
        gain_out[1],
        recur_out,
        branch_out,
        out_out,
        gate_out,
        up_out,
        down_out,
        both_out[0],
        both_out[1],
        small[0],
        small[1],
        small[2],
        small[3],
        small[4 : 4 + taps],
        small[4 + taps : 4 + taps + rows],
        jnp.swapaxes(small[4 + taps + rows :].reshape(lag, rows, part), 0, 1),
        group_states,
        group_tails,
    )


def solution(mesh):
    nseq, nchan = mesh.devices.shape
    fine = Mesh(
        mesh.devices.reshape(nseq // 2, 2, nchan // PEER, 2, 2), ("sx", "sc", "co", "ca", "cb")
    )
    seq = ("sx", "sc")
    chan = ("co", "ca", "cb")
    place = P(None, seq + chan, None)
    vector = P(chan + seq)
    in_specs = (
        place,
        vector,
        vector,
        P(seq, chan),
        P(seq, chan),
        P(chan, seq),
        P(seq, chan),
        P(seq, chan),
        P(chan, seq),
        P(chan, seq, None),
        P(chan, seq, None),
        vector,
        vector,
        vector,
        vector,
        P(None, chan + seq),
        P(None, chan + seq),
        P(None, None, chan + seq),
        P(),
        place,
    )
    out_specs = (
        place,
        place,
        vector,
        vector,
        P(seq, chan),
        P(seq, chan),
        P(chan, seq),
        P(seq, chan),
        P(seq, chan),
        P(chan, seq),
        P(chan, seq, None),
        P(chan, seq, None),
        vector,
        vector,
        vector,
        vector,
        P(None, chan + seq),
        P(None, chan + seq),
        P(None, None, chan + seq),
        P(seq, None, chan),
        P(seq, None, None, chan),
    )
    return jax.shard_map(shards, mesh=fine, in_specs=in_specs, out_specs=out_specs, check_vma=False)
```
